128 devices in a mesh: wide: 32 (over z, y, x_hi), narrow: 4 (over x_lo, core).
Axes of the slice: x: 4 (x_hi: 2, x_lo: 2; x = x_hi * 2 + x_lo), y: 4, z: 4, core: 2. Of those that a mesh axis runs over, the one named last changes fastest.
Arguments:
- noise: bfloat16 [128, 32, 256], P('wide'), may hold values from -6 to 6
- diagonal_tile_blocks: bfloat16 [128, 256, 256], P(('wide', 'narrow')), may hold values from -0.375 to 0.375
- left_factors: bfloat16 [128, 128, 128, 256], P('wide', 'narrow'), may hold values from -0.046875 to 0.046875
- right_factors: bfloat16 [128, 128, 128, 256], P('wide', 'narrow'), may hold values from -0.375 to 0.375
- ranks: int32 [128, 128], P('wide', 'narrow'), may hold values from 0 to 128, as said below
- owner: int32 [128], replicated, may hold values from 0 to 127, as said below
- courant_x: float32 [128, 256], P('wide', 'narrow'), may hold values from 0.05 to 0.4
- courant_number_second: float32 [128, 256], P('wide', 'narrow'), may hold values from 0.05 to 0.4
- upwind_x: int32 [128, 256], P('wide', 'narrow'), may hold values from 0 to 1
- upwind_y: int32 [128, 256], P('wide', 'narrow'), may hold values from 0 to 1
Outputs:
- tracer: float32 [32, 128, 256], P(None, 'wide', 'narrow')
The draws below stay inside these ranges and needn't reach their ends.
Inputs may be any that keep to these rules, and one draw needn't show every extreme that they name: owner is a permutation of the tile rows 0 to 127. ranks[p, c] is 0 where c >= owner[p] and at least 1 where c < owner[p].
All inputs are finite; a program needn't handle non-finite values.
Results may differ from the reference program's by a relative error of at most 0.0016.
Values may be sent and summed in bfloat16 or wider, within the bound.
No kernel may reach another device: no remote copies, remote signals or barrier semaphores. Data moves between devices by JAX's collectives and lax.ppermute only.
A program may use at most 64 MiB of HBM per device.

```python
import jax
import jax.numpy as jnp
import numpy as np
from jax import lax

TSIDE = 16
R = 128
S = 32
TX = 8
TY = 16
ITERS = 4
TS = 256
NT = 128
GX = 128
GY = 256


def owner_of(key):
    return jax.random.permutation(jax.random.fold_in(key, 11), NT).astype(jnp.int32)


def draw_owner(key, part):
    return owner_of(key)


def draw_ranks(key, part):
    holder = owner_of(key)
    tile_rows = holder[:, None]
    tile_cols = jnp.arange(NT, dtype=jnp.int32)[None, :]
    raw_ranks = jax.random.randint(jax.random.fold_in(key, 12), (NT, NT), 1, R + 1).astype(jnp.int32)
    forced = (tile_rows == NT - 1) & (tile_cols == 0)
    raw_ranks = jnp.where(forced, R, raw_ranks)
    return jnp.where(tile_cols < tile_rows, raw_ranks, 0).astype(jnp.int32)


def place_ends(drawn, own_key, low, top_value):
    dims = drawn.shape
    index_at = [jax.random.randint(jax.random.fold_in(own_key, axis), (), 0, dims[axis]) for axis in range(len(dims))]
    drawn = drawn.at[tuple(index_at)].set(low)
    longest = dims.index(max(dims))
    index_at[longest] = (index_at[longest] + 1) % dims[longest]
    return drawn.at[tuple(index_at)].set(top_value)


def block_scale(key, dims, split, least, top_value):
    loudness = 1.0
    for dim, parts in split:
        heights = jax.random.uniform(jax.random.fold_in(jax.random.fold_in(key, 6), dim), (parts,), jnp.float32, least / len(split), top_value / len(split))
        loudness = loudness * jnp.repeat(jnp.exp(heights), dims[dim] // parts).reshape((-1,) + (1,) * (len(dims) - 1 - dim))
    return loudness


def gaussian(stream_key, extent, spread, limit, split=(), kind=jnp.bfloat16):
    loudness = block_scale(stream_key, extent, split, -0.22, 0.18) if split else 1.0
    result = jax.random.normal(stream_key, extent, jnp.float32) * spread * loudness
    return jnp.minimum(jnp.maximum(result, -limit), limit).astype(kind)


def setup_inputs(seed: int = 0) -> dict:
    splits = jax.random.split(jax.random.key(seed), 11)
    return {
        "noise": gaussian(splits[0], (NT, S, TS), 1.0, 6.0, ((0, 32),)),
        "diagonal_tile_blocks": gaussian(splits[1], (NT, TS, TS), TS ** -0.5, 0.375, ((0, 128),)),
        "left_factors": gaussian(splits[2], (NT, NT, R, TS), (R * NT) ** -0.5, 0.046875, ((0, 32), (1, 4))),
        "right_factors": gaussian(splits[3], (NT, NT, R, TS), TS ** -0.5, 0.375, ((0, 32), (1, 4))),
        "ranks": draw_ranks(jax.random.fold_in(splits[10], 71), 0),
        "owner": draw_owner(jax.random.fold_in(splits[10], 71), 0),
        "courant_x": jnp.clip(0.05 + 0.35 * jax.random.uniform(splits[6], (GX, GY), jnp.float32) ** block_scale(splits[6], (GX, GY), ((0, 32), (1, 4)), -0.2, 0.2), 0.05, 0.4),
        "courant_number_second": jnp.clip(0.05 + 0.35 * jax.random.uniform(splits[7], (GX, GY), jnp.float32) ** block_scale(splits[7], (GX, GY), ((0, 32), (1, 4)), -0.2, 0.2), 0.05, 0.4),
        "upwind_x": place_ends(jax.random.randint(splits[8], (GX, GY), 0, 2), jax.random.fold_in(splits[8], 1), 0, 1).astype(jnp.int32),
        "upwind_y": place_ends(jax.random.randint(splits[9], (GX, GY), 0, 2), jax.random.fold_in(splits[9], 1), 0, 1).astype(jnp.int32),
    }


mixing = 0.05


def morton_table(tiles_x, tiles_y):
    bits_x = tiles_x.bit_length() - 1
    bits_y = tiles_y.bit_length() - 1
    table = np.zeros((tiles_x, tiles_y), np.int32)
    for first in range(tiles_x):
        for second in range(tiles_y):
            morton_code = 0
            position = 0
            for level in range(max(bits_x, bits_y)):
                if level < bits_y:
                    morton_code = morton_code | (((second >> level) & 1) << position)
                    position = position + 1
                if level < bits_x:
                    morton_code = morton_code | (((first >> level) & 1) << position)
                    position = position + 1
            table[first, second] = morton_code
    return table


def advance(center, low_x, high_x, low_y, high_y, courant_x, courant_number_second, upwind_x, upwind_y):
    from_x = jnp.where(upwind_x == 1, low_x, high_x)
    from_y = jnp.where(upwind_y == 1, low_y, high_y)
    return (center - courant_x * (center - from_x) - courant_number_second * (center - from_y)
            + mixing * (low_x + high_x + low_y + high_y - 4.0 * center))


def reference(noise, diagonal_tile_blocks, left_factors, right_factors, ranks, owner, courant_x, courant_number_second, upwind_x, upwind_y):
    noise_wide = noise.astype(jnp.float32)
    levels = jnp.arange(R, dtype=jnp.int32)

    def one_row(operands):
        left_row, right_row, rank_row, tile_row, diag_row = operands
        coeff = jnp.einsum('csk,crk->csr', noise_wide, right_row.astype(jnp.float32))
        keep = levels[None, None, :] < rank_row[:, None, None]
        coeff = jnp.where(keep, coeff, 0.0).astype(jnp.bfloat16)
        offdiag = jnp.einsum('csr,crk->sk', coeff.astype(jnp.float32), left_row.astype(jnp.float32))
        local_noise_tiles = lax.dynamic_index_in_dim(noise, tile_row, 0, keepdims=False)
        diagonal = jnp.dot(local_noise_tiles, jnp.tril(diag_row).T, preferred_element_type=jnp.float32)
        return offdiag + diagonal

    rowsample = lax.map(one_row, (left_factors, right_factors, ranks, owner, diagonal_tile_blocks))
    inverse_permutation = jnp.argsort(owner).astype(jnp.int32)
    sample_member = rowsample[inverse_permutation]
    table = jnp.asarray(morton_table(TX, TY)).reshape(-1)
    grid = sample_member[table].reshape(TX, TY, S, TSIDE, TSIDE)
    tracer = grid.transpose(2, 0, 3, 1, 4).reshape(S, GX, GY)
    for step_index in range(ITERS):
        tracer = advance(tracer, jnp.roll(tracer, 1, 1), jnp.roll(tracer, -1, 1),
                         jnp.roll(tracer, 1, 2), jnp.roll(tracer, -1, 2),
                         courant_x, courant_number_second, upwind_x, upwind_y)
    return tracer
```

```python
import functools

import jax
import jax.numpy as jnp
import numpy as np
from jax import lax
from jax.experimental import pallas as pl
from jax.experimental.pallas import tpu as pltpu
from jax.sharding import PartitionSpec as P

ITERS = 4
MIXING = 0.05
BOTH = ("wide", "narrow")
VMEM = pltpu.VMEM
SMEM = pltpu.SMEM


def specs(*spaces):
    return [pl.BlockSpec(memory_space=space) for space in spaces]


def factor_kernel(info, ranks, noise, right, left, diag, out, coeff, turned):
    rows, cols, rank_max, cells = right.shape
    members = noise.shape[1]
    levels = lax.broadcasted_iota(jnp.int32, (members, rank_max), 1)
    for c in range(cols):
        block = right[:, c].reshape(rows * rank_max, cells)
        product = lax.dot_general(
            noise[c], block, (((1,), (1,)), ((), ())), preferred_element_type=jnp.float32
        )
        for p in range(rows):
            piece = product[:, p * rank_max : (p + 1) * rank_max]
            piece = jnp.where(levels < ranks[p, c], piece, 0.0).astype(jnp.bfloat16)
            coeff[p, :, c * rank_max : (c + 1) * rank_max] = piece
    for p in range(rows):
        total = jnp.dot(
            coeff[p],
            left[p].reshape(cols * rank_max, cells),
            preferred_element_type=jnp.float32,
        )
        local = info[p] - info[rows]
        held = jnp.logical_and(local >= 0, local < cols)
        tile = noise[jnp.clip(local, 0, cols - 1)]
        own = lax.dot_general(
            tile, diag[p], (((1,), (1,)), ((), ())), preferred_element_type=jnp.float32
        )
        total = total + jnp.where(held, own, 0.0)
        for g in range(members // 8):
            for h in range(2):
                turned[pl.ds(64 * g + 2 * p + h, 8, stride=8), :] = total[
                    8 * g : 8 * g + 8, 128 * h : 128 * h + 128
                ]
    for d in range(out.shape[0]):
        member = d % members
        out[d] = turned[8 * member : 8 * member + 8, :]


def spread_kernel(got, cx, cy):
    for tx in range(8):
        quarters = [got[tx * 64 + k * 16 : tx * 64 + k * 16 + 16, :] for k in range(4)]
        for pair in range(2):
            a, b = quarters[2 * pair], quarters[2 * pair + 1]
            lane = lax.broadcasted_iota(jnp.int32, (16, 128), 1)
            first = jnp.where(lane < 64, a, pltpu.roll(b, 64, 1))
            second = jnp.where(lane < 64, pltpu.roll(a, 64, 1), b)
            cx[tx * 16 : tx * 16 + 16, pair * 128 : pair * 128 + 128] = first
            cy[tx * 16 : tx * 16 + 16, pair * 128 : pair * 128 + 128] = second


def stencil_kernel(plane, place, got, cx_ref, cy_ref, out, summed, field_ref):
    total = got[:, 0] + got[:, 1] + got[:, 2] + got[:, 3]
    summed[...] = total.reshape(256, 128)
    target = lax.broadcasted_iota(jnp.int32, (128, 128), 0)
    one_hot = jnp.where(target == place[...], 1.0, 0.0)
    halves = [
        jnp.dot(
            one_hot,
            summed[pl.ds(h, 128, stride=2), :],
            precision=lax.Precision.HIGHEST,
            preferred_element_type=jnp.float32,
        )
        for h in range(2)
    ]
    field = jnp.concatenate(halves, axis=1)
    shape = field.shape
    lane = lax.broadcasted_iota(jnp.int32, shape, 1)
    column = lane % 16
    tile_y = lax.broadcasted_iota(jnp.int32, shape, 0) % 16
    top, bottom = lane < 16, lane >= 240
    left, right = column == 0, column == 15
    first, last = tile_y == 0, tile_y == 15
    cx, cy = cx_ref[...], cy_ref[...]
    low_x_up, low_y_up = cx > 0, cy > 0
    cx, cy = jnp.abs(cx), jnp.abs(cy)
    for _ in range(ITERS):
        down = pltpu.roll(field, 16, 1)
        low_x = jnp.where(top, pltpu.roll(down, 16, 0), down)
        up = pltpu.roll(field, 240, 1)
        high_x = jnp.where(bottom, pltpu.roll(up, 112, 0), up)
        edge = pltpu.roll(field, 241, 1)
        edge = jnp.where(first, pltpu.roll(edge, 113, 0), pltpu.roll(edge, 1, 0))
        low_y = jnp.where(left, edge, pltpu.roll(field, 1, 1))
        edge = pltpu.roll(field, 15, 1)
        edge = jnp.where(last, pltpu.roll(edge, 15, 0), pltpu.roll(edge, 127, 0))
        high_y = jnp.where(right, edge, pltpu.roll(field, 255, 1))
        from_x = jnp.where(low_x_up, low_x, high_x)
        from_y = jnp.where(low_y_up, low_y, high_y)
        field = (
            field
            - cx * (field - from_x)
            - cy * (field - from_y)
            + MIXING * (low_x + high_x + low_y + high_y - 4.0 * field)
        )
    field_ref[...] = field
    mine = field_ref[pl.ds(pl.multiple_of(plane[0] * 32, 32), 32), :]
    for txl in range(2):
        for k in range(4):
            for nd in range(4):
                row = txl * 16 + nd * 4
                half = (k // 2) * 128
                out[txl * 16 + k * 4 + nd] = mine[row : row + 4, half : half + 128]


def block_kernel(parity, got, out):
    lane = lax.broadcasted_iota(jnp.int32, (got.shape[0], 128), 1)
    odd = parity[0] == 1
    pieces = []
    for a in range(4):
        x = got[:, a, :]
        pieces.append(jnp.where(odd, pltpu.roll(x, 64, 1), x))
    for i in range(4):
        line = jnp.zeros(lane.shape, jnp.float32)
        for a in range(4):
            shift = (16 * (a - i)) % 128
            moved = pltpu.roll(pieces[a], shift, 1) if shift else pieces[a]
            line = jnp.where(lane // 16 == a, moved, line)
        out[:, i, :] = line[:, :64]


def shared(value, count):
    return jnp.broadcast_to(value[None], (count, *value.shape))


def per_device(
    noise,
    diagonal_tile_blocks,
    left_factors,
    right_factors,
    ranks,
    owner,
    courant_x,
    courant_number_second,
    upwind_x,
    upwind_y,
):
    wide, narrow = lax.axis_size("wide"), lax.axis_size("narrow")
    group = wide // narrow
    devices = wide * narrow
    w, n = lax.axis_index("wide"), lax.axis_index("narrow")
    plane = w // group
    rows, cols = ranks.shape
    members = noise.shape[1]
    cells = noise.shape[2]

    swap = [
        ((z * group + r) * narrow + b, (b * group + r) * narrow + z)
        for z in range(narrow)
        for r in range(group)
        for b in range(narrow)
    ]
    planes = [[z * group + r for r in range(group)] for z in range(narrow)]
    slabs = [[z * group * narrow + i for i in range(group * narrow)] for z in range(narrow)]

    with jax.named_scope("diagonal_gather"):
        diag = lax.all_to_all(
            shared(jnp.tril(diagonal_tile_blocks[0]), narrow), "narrow", 0, 0, tiled=True
        )
    with jax.named_scope("noise_gather"):
        swapped = lax.ppermute(noise, BOTH, swap)
        columns = lax.all_to_all(
            shared(swapped, group), "wide", 0, 0, axis_index_groups=planes, tiled=True
        ).reshape(group * rows, members, cells)

    with jax.named_scope("coefficient_gather"):
        signed = [
            jnp.where(flag == 1, value, -value)
            .reshape(rows, 4, 16)
            .transpose(1, 0, 2)
            .reshape(4, 64)
            for value, flag in ((courant_x, upwind_x), (courant_number_second, upwind_y))
        ]
        own = jnp.concatenate(signed, axis=1)
        everyone = lax.all_to_all(shared(own, devices), BOTH, 0, 0, tiled=True)
        cx, cy = pl.pallas_call(
            spread_kernel,
            out_shape=[jax.ShapeDtypeStruct((128, 256), jnp.float32)] * 2,
            in_specs=specs(VMEM),
            out_specs=specs(VMEM, VMEM),
        )(everyone.reshape(devices * 4, 128))

    with jax.named_scope("factors"):
        info = jnp.concatenate(
            [lax.dynamic_slice_in_dim(owner, w * rows, rows), (n * cols)[None].astype(jnp.int32)]
        )
        partial_sums = pl.pallas_call(
            factor_kernel,
            out_shape=jax.ShapeDtypeStruct((devices, 8, 128), jnp.float32),
            in_specs=specs(SMEM, SMEM, VMEM, VMEM, VMEM, VMEM),
            out_specs=pl.BlockSpec(memory_space=VMEM),
            scratch_shapes=[
                pltpu.VMEM((rows, members, cols * ranks_max(left_factors)), jnp.bfloat16),
                pltpu.VMEM((members * 8, 128), jnp.float32),
            ],
            compiler_params=pltpu.CompilerParams(vmem_limit_bytes=40 << 20),
        )(info, ranks, columns, right_factors, left_factors, diag)

    with jax.named_scope("member_exchange"):
        got = lax.all_to_all(partial_sums, BOTH, 0, 0, tiled=True)

    with jax.named_scope("stencil"):
        bits = [(owner >> b) & 1 for b in range(7)]
        tile_y = bits[0] | bits[2] << 1 | bits[4] << 2 | bits[6] << 3
        tile_x = bits[1] | bits[3] << 1 | bits[5] << 2
        place = (tile_x * 16 + tile_y)[None]
        blocks = pl.pallas_call(
            stencil_kernel,
            out_shape=jax.ShapeDtypeStruct((members, 4, 128), jnp.float32),
            in_specs=specs(SMEM, VMEM, VMEM, VMEM, VMEM),
            out_specs=pl.BlockSpec(memory_space=VMEM),
            scratch_shapes=[
                pltpu.VMEM((256, 128), jnp.float32),
                pltpu.VMEM((128, 256), jnp.float32),
            ],
        )(plane[None].astype(jnp.int32), place, got.reshape(wide, narrow, 8, 128), cx, cy)

    with jax.named_scope("block_exchange"):
        mine = lax.all_to_all(blocks, BOTH, 0, 0, axis_index_groups=slabs, tiled=True)

    with jax.named_scope("block"):
        return pl.pallas_call(
            block_kernel,
            out_shape=jax.ShapeDtypeStruct((members, 4, 64), jnp.float32),
            in_specs=specs(SMEM, VMEM),
            out_specs=pl.BlockSpec(memory_space=VMEM),
        )((w % 2)[None].astype(jnp.int32), mine)


def ranks_max(factors):
    return factors.shape[2]


def solution(mesh):
    placed = (
        P("wide", None, None),
        P(("wide", "narrow"), None, None),
        P("wide", "narrow", None, None),
        P("wide", "narrow", None, None),
        P("wide", "narrow"),
        P(),
        P("wide", "narrow"),
        P("wide", "narrow"),
        P("wide", "narrow"),
        P("wide", "narrow"),
    )
    return jax.shard_map(
        per_device, mesh=mesh, in_specs=placed, out_specs=P(None, "wide", "narrow"), check_vma=False
    )
```

```python
import functools

import jax
import jax.numpy as jnp
import numpy as np
from jax import lax
from jax.experimental import pallas as pl
from jax.experimental.pallas import tpu as pltpu
from jax.sharding import PartitionSpec as P

ITERS = 4
MIXING = 0.05
BOTH = ("wide", "narrow")
VMEM = pltpu.VMEM
SMEM = pltpu.SMEM
MIB = 1 << 20


def specs(*spaces):
    return [pl.BlockSpec(memory_space=space) for space in spaces]


def near(value):
    return pltpu.with_memory_space_constraint(value, VMEM)


def far(value):
    return pltpu.with_memory_space_constraint(value, pltpu.HBM)


def limit(mib):
    return pltpu.CompilerParams(vmem_limit_bytes=mib * MIB)


def factor_kernel(info, keep, noise, right, left, d0, d1, d2, d3, out, coeff, turned, own):
    rows, cols, rank_max, cells = right.shape
    members = noise.shape[1]
    for j, diag in enumerate((d0, d1, d2, d3)):
        row = info[rows] ^ j
        local = info[row]
        held = jnp.logical_and(local >= 0, local < cols)
        tile = noise[jnp.clip(local, 0, cols - 1)]
        term = lax.dot_general(
            tile, diag[...], (((1,), (1,)), ((), ())), preferred_element_type=jnp.float32
        )
        own[row] = jnp.where(held, term, 0.0)
    for c in range(cols):
        span = slice(c * rank_max, (c + 1) * rank_max)
        block = right[:, c].reshape(rows * rank_max, cells)
        product = lax.dot_general(
            noise[c], block, (((1,), (1,)), ((), ())), preferred_element_type=jnp.float32
        )
        for p in range(rows):
            piece = product[:, p * rank_max : (p + 1) * rank_max]
            piece = jnp.where(keep[p : p + 1, span] > 0, piece, 0.0)
            coeff[p, :, span] = piece.astype(jnp.bfloat16)
    for p in range(rows):
        total = own[p] + jnp.dot(
            coeff[p],
            left[p].reshape(cols * rank_max, cells),
            preferred_element_type=jnp.float32,
        )
        for g in range(members // 8):
            for h in range(2):
                turned[pl.ds(64 * g + 2 * p + h, 8, stride=8), :] = total[
                    8 * g : 8 * g + 8, 128 * h : 128 * h + 128
                ]
    for d in range(out.shape[0]):
        member = d % members
        out[d] = turned[8 * member : 8 * member + 8, :]


def fetch_kernel(right, left, right_out, left_out, done):
    parts = 4
    copies = []
    for i, (source, target) in enumerate(((right, right_out), (left, left_out))):
        for j in range(parts):
            copies.append(pltpu.make_async_copy(source.at[j], target.at[j], done.at[parts * i + j]))
    for copy in copies:
        copy.start()
    for copy in copies:
        copy.wait()


def weight_kernel(parity, low, own, high, out):
    lane = lax.broadcasted_iota(jnp.int32, (8, 128), 1)
    odd = parity[0] == 1
    pieces = [
        jnp.concatenate(
            [low[4 * q + 2 : 4 * q + 4, :], own[4 * q : 4 * q + 4, :], high[4 * q : 4 * q + 2, :]],
            axis=0,
        )
        for q in range(3)
    ]
    turned = [pltpu.roll(piece, 64, 1) for piece in pieces]
    zero = jnp.zeros((8, 128), jnp.float32)
    for h in range(2):
        signed = []
        for first, second in ((pieces, turned), (turned, pieces)):
            if h == 0:
                even_form = jnp.where(lane < 64, zero, second[0])
                odd_form = jnp.where(lane < 64, first[0], second[1])
            else:
                even_form = jnp.where(lane < 64, first[1], second[2])
                odd_form = jnp.where(lane < 64, first[2], zero)
            signed.append(jnp.where(odd, odd_form, even_form))
        cx, cy = signed
        span = slice(128 * h, 128 * h + 128)
        out[0, :, span] = 1.0 - jnp.abs(cx) - jnp.abs(cy) - 4.0 * MIXING
        out[1, :, span] = MIXING + jnp.maximum(cx, 0.0)
        out[2, :, span] = MIXING + jnp.maximum(-cx, 0.0)
        out[3, :, span] = MIXING + jnp.maximum(cy, 0.0)
        out[4, :, span] = MIXING + jnp.maximum(-cy, 0.0)


def place_kernel(place, got, out, summed, window):
    total = got[:, 0] + got[:, 1] + got[:, 2] + got[:, 3]
    summed[...] = total.reshape(256, 128)
    target = lax.broadcasted_iota(jnp.int32, (64, 128), 0)
    one_hot = jnp.where(target == place[...], 1.0, 0.0).astype(jnp.bfloat16)
    one_hot = jnp.concatenate([one_hot] * 3, axis=1)
    for h in range(2):
        rest = summed[pl.ds(h, 128, stride=2), :]
        parts = []
        for _ in range(3):
            part = rest.astype(jnp.bfloat16)
            parts.append(part)
            rest = rest - part.astype(jnp.float32)
        field = jnp.dot(
            one_hot, jnp.concatenate(parts, axis=0), preferred_element_type=jnp.float32
        ).reshape(4, 16, 128)
        window[h, :, 0:8] = field[:, 8:16]
        window[h, :, 8:24] = field
        window[h, :, 24:32] = field[:, 0:8]
    for txl in range(2):
        for k in range(4):
            if k == 0:
                sources = ((1, txl), (0, txl + 1))
            elif k == 3:
                sources = ((1, txl + 1), (0, txl + 2))
            else:
                sources = ((0, txl + 1), (1, txl + 1))
            for nd in range(4):
                for side, (h, tx) in enumerate(sources):
                    out[txl * 16 + k * 4 + nd, :, 128 * side : 128 * side + 128] = window[
                        h, tx, 6 + 4 * nd : 14 + 4 * nd, :
                    ]


def block_kernel(parity, weight, got, out, done):
    members = got.shape[0]
    chunk = 4
    shape = (chunk, 8, 256)
    lane = lax.broadcasted_iota(jnp.int32, shape, 2)
    left, right = lane % 16 == 0, lane % 16 == 15
    centre, w_low_x, w_high_x, w_low_y, w_high_y = [
        jnp.broadcast_to(weight[i][None], shape) for i in range(5)
    ]
    odd = parity[0] == 1
    for start in range(0, members, chunk):
        field = got[start : start + chunk]
        for _ in range(ITERS):
            low_x = pltpu.roll(field, 16, 2)
            high_x = pltpu.roll(field, 240, 2)
            edge = pltpu.roll(pltpu.roll(field, 241, 2), 1, 1)
            low_y = jnp.where(left, edge, pltpu.roll(field, 1, 2))
            edge = pltpu.roll(pltpu.roll(field, 15, 2), 7, 1)
            high_y = jnp.where(right, edge, pltpu.roll(field, 255, 2))
            field = (
                centre * field
                + w_low_x * low_x
                + w_high_x * high_x
                + w_low_y * low_y
                + w_high_y * high_y
            )
        mine = jnp.where(odd, pltpu.roll(field[:, :, :128], 64, 2), field[:, :, 128:])
        done[8 * start : 8 * (start + chunk), :] = mine.reshape(8 * chunk, 128)
    lane = lax.broadcasted_iota(jnp.int32, (members, 128), 1)
    pieces = [done[pl.ds(2 + a, members, stride=8), :] for a in range(4)]
    for i in range(4):
        line = pieces[0]
        for a in range(4):
            shift = (16 * (a - i)) % 128
            moved = pltpu.roll(pieces[a], shift, 1) if shift else pieces[a]
            line = moved if a == 0 else jnp.where(lane // 16 == a, moved, line)
        out[:, i, :] = line[:, :64]


def shared(value, count):
    return jnp.broadcast_to(value[None], (count, *value.shape))


def ring(count):
    forward = [(i, (i + 1) % count) for i in range(count)]
    return forward, [(b, a) for a, b in forward]


def per_device(
    noise,
    diagonal_tile_blocks,
    left_factors,
    right_factors,
    ranks,
    owner,
    courant_x,
    courant_number_second,
    upwind_x,
    upwind_y,
):
    wide, narrow = lax.axis_size("wide"), lax.axis_size("narrow")
    group = wide // narrow
    devices = wide * narrow
    w, n = lax.axis_index("wide"), lax.axis_index("narrow")
    plane = w // group
    rows, cols = ranks.shape
    rank_max = left_factors.shape[2]
    members = noise.shape[1]
    cells = noise.shape[2]
    f32 = jnp.float32

    swap = [
        ((z * group + r) * narrow + b, (b * group + r) * narrow + z)
        for z in range(narrow)
        for r in range(group)
        for b in range(narrow)
    ]
    planes = [[z * group + r for r in range(group)] for z in range(narrow)]
    slabs = [[z * group * narrow + i for i in range(group * narrow)] for z in range(narrow)]

    with jax.named_scope("noise_gather"):
        swapped = lax.ppermute(noise, BOTH, swap)
        swapped, right_factors, left_factors = lax.optimization_barrier(
            (swapped, right_factors, left_factors)
        )
        columns = lax.all_to_all(
            shared(swapped, group), "wide", 0, 0, axis_index_groups=planes, tiled=True
        ).reshape(group * rows, members, cells)

    with jax.named_scope("factor_fetch"):
        right_near, left_near = pl.pallas_call(
            fetch_kernel,
            out_shape=[pltpu.VMEM(right_factors.shape, right_factors.dtype)] * 2,
            in_specs=specs(pltpu.HBM, pltpu.HBM),
            out_specs=specs(VMEM, VMEM),
            scratch_shapes=[pltpu.SemaphoreType.DMA((2 * rows,))],
            compiler_params=limit(1),
            cost_estimate=pl.CostEstimate(
                flops=0, transcendentals=0, bytes_accessed=4 * right_factors.size
            ),
        )(far(right_factors), far(left_factors))

    with jax.named_scope("diagonal_gather"):
        own_diag = jnp.tril(diagonal_tile_blocks[0])
        diags = [own_diag] + [
            lax.ppermute(own_diag, "narrow", [(i, i ^ j) for i in range(narrow)])
            for j in range(1, narrow)
        ]

    with jax.named_scope("coefficient_halo"):
        signed = [
            jnp.where(flag == 1, value, -value)
            .reshape(rows, 4, 16)
            .transpose(1, 0, 2)
            .reshape(4, 64)
            for value, flag in ((courant_x, upwind_x), (courant_number_second, upwind_y))
        ]
        own = jnp.concatenate(signed, axis=1)
        forward, backward = ring(wide)
        own = jnp.concatenate(
            [lax.ppermute(own, "wide", forward), own, lax.ppermute(own, "wide", backward)], axis=0
        )
        forward, backward = ring(narrow)
        parity = (w % 2)[None].astype(jnp.int32)
        weight = pl.pallas_call(
            weight_kernel,
            out_shape=pltpu.VMEM((5, 8, 256), f32),
            in_specs=specs(SMEM, VMEM, VMEM, VMEM),
            out_specs=pl.BlockSpec(memory_space=VMEM),
            compiler_params=limit(2),
        )(
            parity,
            near(lax.ppermute(own, "narrow", forward)),
            near(own),
            near(lax.ppermute(own, "narrow", backward)),
        )

    with jax.named_scope("factors"):
        info = jnp.concatenate(
            [
                lax.dynamic_slice_in_dim(owner, w * rows, rows) - n * cols,
                n[None].astype(jnp.int32),
            ]
        )
        keep = (
            jnp.arange(rank_max, dtype=jnp.int32)[None, None, :] < ranks[:, :, None]
        ).astype(f32).reshape(rows, cols * rank_max)
        partial_sums = pl.pallas_call(
            factor_kernel,
            out_shape=pltpu.VMEM((devices, 8, 128), f32),
            in_specs=specs(SMEM, *[VMEM] * 8),
            out_specs=pl.BlockSpec(memory_space=VMEM),
            scratch_shapes=[
                pltpu.VMEM((rows, members, cols * rank_max), jnp.bfloat16),
                pltpu.VMEM((members * 8, 128), f32),
                pltpu.VMEM((rows, members, cells), f32),
            ],
            compiler_params=limit(8),
        )(
            info,
            near(keep),
            near(columns),
            right_near,
            left_near,
            *[near(d) for d in diags],
        )

    with jax.named_scope("member_exchange"):
        got = lax.all_to_all(partial_sums, BOTH, 0, 0, tiled=True)
        got, weight = lax.optimization_barrier((got, weight))

    with jax.named_scope("place"):
        bits = [(owner >> b) & 1 for b in range(7)]
        tile_y = bits[0] | bits[2] << 1 | bits[4] << 2 | bits[6] << 3
        tile_x = bits[1] | bits[3] << 1 | bits[5] << 2
        place = (tile_x * 16 + tile_y - 32 * plane.astype(jnp.int32) + 16) & 127
        blocks = pl.pallas_call(
            place_kernel,
            out_shape=pltpu.VMEM((members, 8, 256), f32),
            in_specs=specs(VMEM, VMEM),
            out_specs=pl.BlockSpec(memory_space=VMEM),
            scratch_shapes=[pltpu.VMEM((256, 128), f32), pltpu.VMEM((2, 4, 32, 128), f32)],
            compiler_params=limit(4),
        )(near(place[None]), near(got.reshape(wide, narrow, 8, 128)))

    with jax.named_scope("block_exchange"):
        mine = lax.all_to_all(blocks, BOTH, 0, 0, axis_index_groups=slabs, tiled=True)

    with jax.named_scope("stencil"):
        return pl.pallas_call(
            block_kernel,
            out_shape=jax.ShapeDtypeStruct((members, 4, 64), f32),
            in_specs=specs(SMEM, VMEM, VMEM),
            out_specs=pl.BlockSpec(memory_space=VMEM),
            scratch_shapes=[pltpu.VMEM((members * 8, 128), f32)],
            compiler_params=limit(4),
        )(parity, weight, near(mine))


def solution(mesh):
    placed = (
        P("wide", None, None),
        P(("wide", "narrow"), None, None),
        P("wide", "narrow", None, None),
        P("wide", "narrow", None, None),
        P("wide", "narrow"),
        P(),
        P("wide", "narrow"),
        P("wide", "narrow"),
        P("wide", "narrow"),
        P("wide", "narrow"),
    )
    return jax.shard_map(
        per_device, mesh=mesh, in_specs=placed, out_specs=P(None, "wide", "narrow"), check_vma=False
    )
```

```python
import functools

import jax
import jax.numpy as jnp
import numpy as np
from jax import lax
from jax.experimental import pallas as pl
from jax.experimental.pallas import tpu as pltpu
from jax.sharding import PartitionSpec as P

ITERS = 4
MIXING = 0.05
BOTH = ("wide", "narrow")
VMEM = pltpu.VMEM
SMEM = pltpu.SMEM
MIB = 1 << 20
CHUNKS = 8


def specs(*spaces):
    return [pl.BlockSpec(memory_space=space) for space in spaces]


def near(value):
    return pltpu.with_memory_space_constraint(value, VMEM)


def far(value):
    return pltpu.with_memory_space_constraint(value, pltpu.HBM)


def limit(mib):
    return pltpu.CompilerParams(vmem_limit_bytes=mib * MIB)


def factor_kernel(
    info,
    keep,
    noise,
    right_far,
    left_far,
    d0,
    d1,
    d2,
    d3,
    out,
    coeff,
    turned,
    own,
    right,
    left,
    right_done,
    left_done,
):
    rows, cols, rank_max, cells = right.shape
    members = noise.shape[1]
    each = cols // CHUNKS
    right_copies = [
        pltpu.make_async_copy(
            right_far.at[:, i * each : (i + 1) * each],
            right.at[:, i * each : (i + 1) * each],
            right_done.at[i],
        )
        for i in range(CHUNKS)
    ]
    left_copies = [
        pltpu.make_async_copy(left_far.at[p], left.at[p], left_done.at[p]) for p in range(rows)
    ]
    for copy in right_copies + left_copies:
        copy.start()
    for j, diag in enumerate((d0, d1, d2, d3)):
        row = info[rows] ^ j
        local = info[row]
        held = jnp.logical_and(local >= 0, local < cols)
        tile = noise[jnp.clip(local, 0, cols - 1)]
        term = lax.dot_general(
            tile, diag[...], (((1,), (1,)), ((), ())), preferred_element_type=jnp.float32
        )
        own[row] = jnp.where(held, term, 0.0)
    for c in range(cols):
        if c % each == 0:
            right_copies[c // each].wait()
        span = slice(c * rank_max, (c + 1) * rank_max)
        block = right[:, c].reshape(rows * rank_max, cells)
        product = lax.dot_general(
            noise[c], block, (((1,), (1,)), ((), ())), preferred_element_type=jnp.float32
        )
        for p in range(rows):
            piece = product[:, p * rank_max : (p + 1) * rank_max]
            piece = jnp.where(keep[p : p + 1, span] > 0, piece, 0.0)
            coeff[p, :, span] = piece.astype(jnp.bfloat16)
    for p in range(rows):
        left_copies[p].wait()
        total = own[p] + jnp.dot(
            coeff[p],
            left[p].reshape(cols * rank_max, cells),
            preferred_element_type=jnp.float32,
        )
        for g in range(members // 8):
            for h in range(2):
                turned[pl.ds(64 * g + 2 * p + h, 8, stride=8), :] = total[
                    8 * g : 8 * g + 8, 128 * h : 128 * h + 128
                ]
    for d in range(out.shape[0]):
        member = d % members
        out[d] = turned[8 * member : 8 * member + 8, :]


def weight_kernel(parity, low, own, high, out):
    lane = lax.broadcasted_iota(jnp.int32, (8, 128), 1)
    odd = parity[0] == 1
    pieces = [
        jnp.concatenate(
            [low[4 * q + 2 : 4 * q + 4, :], own[4 * q : 4 * q + 4, :], high[4 * q : 4 * q + 2, :]],
            axis=0,
        )
        for q in range(3)
    ]
    turned = [pltpu.roll(piece, 64, 1) for piece in pieces]
    zero = jnp.zeros((8, 128), jnp.float32)
    for h in range(2):
        signed = []
        for first, second in ((pieces, turned), (turned, pieces)):
            if h == 0:
                even_form = jnp.where(lane < 64, zero, second[0])
                odd_form = jnp.where(lane < 64, first[0], second[1])
            else:
                even_form = jnp.where(lane < 64, first[1], second[2])
                odd_form = jnp.where(lane < 64, first[2], zero)
            signed.append(jnp.where(odd, odd_form, even_form))
        cx, cy = signed
        span = slice(128 * h, 128 * h + 128)
        out[0, :, span] = 1.0 - jnp.abs(cx) - jnp.abs(cy) - 4.0 * MIXING
        out[1, :, span] = MIXING + jnp.maximum(cx, 0.0)
        out[2, :, span] = MIXING + jnp.maximum(-cx, 0.0)
        out[3, :, span] = MIXING + jnp.maximum(cy, 0.0)
        out[4, :, span] = MIXING + jnp.maximum(-cy, 0.0)


def place_kernel(place, got, out, summed, window):
    total = got[:, 0] + got[:, 1] + got[:, 2] + got[:, 3]
    summed[...] = total.reshape(256, 128)
    target = lax.broadcasted_iota(jnp.int32, (64, 128), 0)
    one_hot = jnp.where(target == place[...], 1.0, 0.0).astype(jnp.bfloat16)
    one_hot = jnp.concatenate([one_hot] * 3, axis=1)
    for h in range(2):
        rest = summed[pl.ds(h, 128, stride=2), :]
        parts = []
        for _ in range(3):
            part = rest.astype(jnp.bfloat16)
            parts.append(part)
            rest = rest - part.astype(jnp.float32)
        field = jnp.dot(
            one_hot, jnp.concatenate(parts, axis=0), preferred_element_type=jnp.float32
        ).reshape(4, 16, 128)
        window[h, :, 0:8] = field[:, 8:16]
        window[h, :, 8:24] = field
        window[h, :, 24:32] = field[:, 0:8]
    for txl in range(2):
        for k in range(4):
            if k == 0:
                sources = ((1, txl), (0, txl + 1))
            elif k == 3:
                sources = ((1, txl + 1), (0, txl + 2))
            else:
                sources = ((0, txl + 1), (1, txl + 1))
            for nd in range(4):
                for side, (h, tx) in enumerate(sources):
                    out[txl * 16 + k * 4 + nd, :, 128 * side : 128 * side + 128] = window[
                        h, tx, 6 + 4 * nd : 14 + 4 * nd, :
                    ]


def block_kernel(parity, weight, got, out, ping, pong, done):
    members = got.shape[0]
    chunk = 4
    shape = (chunk, 8, 256)
    lane = lax.broadcasted_iota(jnp.int32, shape, 2)
    left, right = lane % 16 == 0, lane % 16 == 15
    centre, w_low_x, w_high_x, w_low_y, w_high_y = [weight[i][None] for i in range(5)]
    odd = parity[0] == 1
    source = got
    for step in range(ITERS):
        target = (ping, pong)[step % 2]
        for start in range(0, members, chunk):
            field = source[start : start + chunk]
            low_x = pltpu.roll(field, 16, 2)
            high_x = pltpu.roll(field, 240, 2)
            low_y = pltpu.roll(jnp.where(right, pltpu.roll(high_x, 1, 1), field), 1, 2)
            high_y = pltpu.roll(jnp.where(left, pltpu.roll(low_x, 7, 1), field), 255, 2)
            field = (
                centre * field
                + w_low_x * low_x
                + w_high_x * high_x
                + w_low_y * low_y
                + w_high_y * high_y
            )
            if step < ITERS - 1:
                target[start : start + chunk] = field
            else:
                mine = jnp.where(odd, pltpu.roll(field[:, :, :128], 64, 2), field[:, :, 128:])
                done[8 * start : 8 * (start + chunk), :] = mine.reshape(8 * chunk, 128)
        source = target
    lane = lax.broadcasted_iota(jnp.int32, (members, 128), 1)
    pieces = [done[pl.ds(2 + a, members, stride=8), :] for a in range(4)]
    for i in range(4):
        line = pieces[0]
        for a in range(4):
            shift = (16 * (a - i)) % 128
            moved = pltpu.roll(pieces[a], shift, 1) if shift else pieces[a]
            line = moved if a == 0 else jnp.where(lane // 16 == a, moved, line)
        out[:, i, :] = line[:, :64]


def shared(value, count):
    return jnp.broadcast_to(value[None], (count, *value.shape))


def ring(count):
    forward = [(i, (i + 1) % count) for i in range(count)]
    return forward, [(b, a) for a, b in forward]


def per_device(
    noise,
    diagonal_tile_blocks,
    left_factors,
    right_factors,
    ranks,
    owner,
    courant_x,
    courant_number_second,
    upwind_x,
    upwind_y,
):
    wide, narrow = lax.axis_size("wide"), lax.axis_size("narrow")
    group = wide // narrow
    devices = wide * narrow
    w, n = lax.axis_index("wide"), lax.axis_index("narrow")
    plane = w // group
    rows, cols = ranks.shape
    rank_max = left_factors.shape[2]
    members = noise.shape[1]
    cells = noise.shape[2]
    f32 = jnp.float32

    swap = [
        ((z * group + r) * narrow + b, (b * group + r) * narrow + z)
        for z in range(narrow)
        for r in range(group)
        for b in range(narrow)
    ]
    planes = [[z * group + r for r in range(group)] for z in range(narrow)]
    slabs = [[z * group * narrow + i for i in range(group * narrow)] for z in range(narrow)]

    with jax.named_scope("noise_gather"):
        swapped = lax.ppermute(noise, BOTH, swap)
        sending, own_diag = lax.optimization_barrier((shared(swapped, group), diagonal_tile_blocks[0]))
        columns = lax.all_to_all(
            sending, "wide", 0, 0, axis_index_groups=planes, tiled=True
        ).reshape(group * rows, members, cells)

    with jax.named_scope("diagonal_gather"):
        own_diag = jnp.tril(own_diag)
        diags = [own_diag] + [
            lax.ppermute(own_diag, "narrow", [(i, i ^ j) for i in range(narrow)])
            for j in range(1, narrow)
        ]

    with jax.named_scope("coefficient_halo"):
        signed = [
            jnp.where(flag == 1, value, -value)
            .reshape(rows, 4, 16)
            .transpose(1, 0, 2)
            .reshape(4, 64)
            for value, flag in ((courant_x, upwind_x), (courant_number_second, upwind_y))
        ]
        own = jnp.concatenate(signed, axis=1)
        forward, backward = ring(wide)
        own = jnp.concatenate(
            [lax.ppermute(own, "wide", forward), own, lax.ppermute(own, "wide", backward)], axis=0
        )
        forward, backward = ring(narrow)
        parity = (w % 2)[None].astype(jnp.int32)
        weight = pl.pallas_call(
            weight_kernel,
            out_shape=pltpu.VMEM((5, 8, 256), f32),
            in_specs=specs(SMEM, VMEM, VMEM, VMEM),
            out_specs=pl.BlockSpec(memory_space=VMEM),
            compiler_params=limit(2),
        )(
            parity,
            near(lax.ppermute(own, "narrow", forward)),
            near(own),
            near(lax.ppermute(own, "narrow", backward)),
        )

    with jax.named_scope("factors"):
        info = jnp.concatenate(
            [
                lax.dynamic_slice_in_dim(owner, w * rows, rows) - n * cols,
                n[None].astype(jnp.int32),
            ]
        )
        keep = (
            jnp.arange(rank_max, dtype=jnp.int32)[None, None, :] < ranks[:, :, None]
        ).astype(f32).reshape(rows, cols * rank_max)
        partial_sums = pl.pallas_call(
            factor_kernel,
            out_shape=pltpu.VMEM((devices, 8, 128), f32),
            in_specs=specs(SMEM, VMEM, VMEM, pltpu.HBM, pltpu.HBM, *[VMEM] * 4),
            out_specs=pl.BlockSpec(memory_space=VMEM),
            scratch_shapes=[
                pltpu.VMEM((rows, members, cols * rank_max), jnp.bfloat16),
                pltpu.VMEM((members * 8, 128), f32),
                pltpu.VMEM((rows, members, cells), f32),
                pltpu.VMEM(right_factors.shape, right_factors.dtype),
                pltpu.VMEM(left_factors.shape, left_factors.dtype),
                pltpu.SemaphoreType.DMA((CHUNKS,)),
                pltpu.SemaphoreType.DMA((rows,)),
            ],
            compiler_params=limit(24),
        )(
            info,
            near(keep),
            near(columns),
            far(right_factors),
            far(left_factors),
            *[near(d) for d in diags],
        )

    with jax.named_scope("member_exchange"):
        got = lax.all_to_all(partial_sums, BOTH, 0, 0, tiled=True)

    with jax.named_scope("place"):
        bits = [(owner >> b) & 1 for b in range(7)]
        tile_y = bits[0] | bits[2] << 1 | bits[4] << 2 | bits[6] << 3
        tile_x = bits[1] | bits[3] << 1 | bits[5] << 2
        place = (tile_x * 16 + tile_y - 32 * plane.astype(jnp.int32) + 16) & 127
        blocks = pl.pallas_call(
            place_kernel,
            out_shape=pltpu.VMEM((members, 8, 256), f32),
            in_specs=specs(VMEM, VMEM),
            out_specs=pl.BlockSpec(memory_space=VMEM),
            scratch_shapes=[pltpu.VMEM((256, 128), f32), pltpu.VMEM((2, 4, 32, 128), f32)],
            compiler_params=limit(4),
        )(near(place[None]), near(got.reshape(wide, narrow, 8, 128)))

    with jax.named_scope("block_exchange"):
        mine = lax.all_to_all(blocks, BOTH, 0, 0, axis_index_groups=slabs, tiled=True)

    with jax.named_scope("stencil"):
        return pl.pallas_call(
            block_kernel,
            out_shape=jax.ShapeDtypeStruct((members, 4, 64), f32),
            in_specs=specs(SMEM, VMEM, VMEM),
            out_specs=pl.BlockSpec(memory_space=VMEM),
            scratch_shapes=[
                pltpu.VMEM((members, 8, 256), f32),
                pltpu.VMEM((members, 8, 256), f32),
                pltpu.VMEM((members * 8, 128), f32),
            ],
            compiler_params=limit(4),
        )(parity, weight, near(mine))


def solution(mesh):
    placed = (
        P("wide", None, None),
        P(("wide", "narrow"), None, None),
        P("wide", "narrow", None, None),
        P("wide", "narrow", None, None),
        P("wide", "narrow"),
        P(),
        P("wide", "narrow"),
        P("wide", "narrow"),
        P("wide", "narrow"),
        P("wide", "narrow"),
    )
    return jax.shard_map(
        per_device, mesh=mesh, in_specs=placed, out_specs=P(None, "wide", "narrow"), check_vma=False
    )
```

```python
import functools

import jax
import jax.numpy as jnp
import numpy as np
from jax import lax
from jax.experimental import pallas as pl
from jax.experimental.pallas import tpu as pltpu
from jax.sharding import PartitionSpec as P

ITERS = 4
MIXING = 0.05
BOTH = ("wide", "narrow")
VMEM = pltpu.VMEM
SMEM = pltpu.SMEM
MIB = 1 << 20


def specs(*spaces):
    return [pl.BlockSpec(memory_space=space) for space in spaces]


def near(value):
    return pltpu.with_memory_space_constraint(value, VMEM)


def far(value):
    return pltpu.with_memory_space_constraint(value, pltpu.HBM)


def limit(mib):
    return pltpu.CompilerParams(vmem_limit_bytes=mib * MIB)


def halves(count):
    return slice(0, count // 2), slice(count // 2, count)


def factor_kernel(
    owner,
    keep,
    right_far,
    left_far,
    diag_far,
    *rest,
):
    pieces, (out, noise, coeff, turned, right, left, diag, done) = rest[:-8], rest[-8:]
    rows, cols, rank_max, cells = right.shape
    members = noise.shape[1]
    each = cols // len(pieces)
    chunks = [slice(i * each, (i + 1) * each) for i in range(len(pieces))]
    pairs = [(right_far.at[:, span], right.at[:, span]) for span in chunks]
    pairs += [(left_far.at[p, span], left.at[p, span]) for p in range(rows) for span in halves(cols)]
    pairs += [(diag_far, diag)]
    copies = [
        pltpu.make_async_copy(source, target, done.at[i])
        for i, (source, target) in enumerate(pairs)
    ]
    ahead = 3
    for copy in copies[:ahead]:
        copy.start()

    def arrived(i):
        copies[i].wait()
        if i + ahead < len(copies):
            copies[i + ahead].start()

    w, n = lax.axis_index("wide"), lax.axis_index("narrow")
    place = w % len(pieces)
    for j, piece in enumerate(pieces):
        noise[pl.ds(each * (place ^ j), each)] = piece[...]
    for c in range(cols):
        if c % each == 0:
            arrived(c // each)
        span = slice(c * rank_max, (c + 1) * rank_max)
        block = right[:, c].reshape(rows * rank_max, cells)
        product = lax.dot_general(
            noise[c], block, (((1,), (1,)), ((), ())), preferred_element_type=jnp.float32
        )
        for p in range(rows):
            part = product[:, p * rank_max : (p + 1) * rank_max]
            part = jnp.where(keep[p : p + 1, span] > 0, part, 0.0)
            coeff[p, :, span] = part.astype(jnp.bfloat16)
    sums = []
    for p in range(rows):
        total = 0.0
        for i, span in enumerate(halves(cols)):
            arrived(len(chunks) + 2 * p + i)
            total = total + jnp.dot(
                coeff[p, :, rank_max * span.start : rank_max * span.stop],
                left[p, span].reshape(cols // 2 * rank_max, cells),
                preferred_element_type=jnp.float32,
            )
        sums.append(total)
    arrived(len(copies) - 1)
    for p, total in enumerate(sums):
        local = owner[rows * w + p] - cols * n
        held = jnp.logical_and(local >= 0, local < cols)
        term = lax.dot_general(
            noise[jnp.clip(local, 0, cols - 1)],
            diag[p].astype(jnp.bfloat16),
            (((1,), (1,)), ((), ())),
            preferred_element_type=jnp.float32,
        )
        total = total + jnp.where(held, term, 0.0)
        for g in range(members // 8):
            for h in range(2):
                turned[pl.ds(64 * g + 2 * p + h, 8, stride=8), :] = total[
                    8 * g : 8 * g + 8, 128 * h : 128 * h + 128
                ]
    for d in range(out.shape[0]):
        member = d % members
        out[d] = turned[8 * member : 8 * member + 8, :]


def weight_kernel(low, own, high, out):
    low, own, high = low[...], own[...], high[...]
    lane = lax.broadcasted_iota(jnp.int32, low.shape, 1)
    cx, cy = [
        jnp.where(
            lane < 16,
            pltpu.roll(low, edge, 1),
            jnp.where(lane < 80, pltpu.roll(own, middle, 1), pltpu.roll(high, edge, 1)),
        )
        for edge, middle in ((80, 16), (16, 80))
    ]
    weights = (
        1.0 - jnp.abs(cx) - jnp.abs(cy) - 4.0 * MIXING,
        MIXING + jnp.maximum(cx, 0.0),
        MIXING + jnp.maximum(-cx, 0.0),
        MIXING + jnp.maximum(cy, 0.0),
        MIXING + jnp.maximum(-cy, 0.0),
    )
    for i, weight in enumerate(weights):
        for row in range(12):
            out[i, row] = jnp.broadcast_to(weight[row : row + 1], (8, 128))


def place_kernel(place, got, out, summed, window):
    total = got[:, 0] + got[:, 1] + got[:, 2] + got[:, 3]
    summed[...] = total.reshape(256, 128)
    target = lax.broadcasted_iota(jnp.int32, (64, 128), 0)
    one_hot = jnp.where(target == place[...], 1.0, 0.0).astype(jnp.bfloat16)
    one_hot = jnp.concatenate([one_hot] * 3, axis=1)
    fields = []
    for h in range(2):
        rest = summed[pl.ds(h, 128, stride=2), :]
        parts = []
        for _ in range(3):
            part = rest.astype(jnp.bfloat16)
            parts.append(part)
            rest = rest - part.astype(jnp.float32)
        fields.append(
            jnp.dot(
                one_hot, jnp.concatenate(parts, axis=0), preferred_element_type=jnp.float32
            ).reshape(4, 16, 128)
        )
    shape = (8, 8, 128)
    sub = lax.broadcasted_iota(jnp.int32, shape, 1)
    group = lax.broadcasted_iota(jnp.int32, shape, 2) // 16
    sides = []
    for h in range(2):
        x = jnp.concatenate([f[:, 8 * h : 8 * h + 8] for f in fields], axis=1).reshape(shape)
        for bit in (1, 2, 4):
            in_sub, in_group = (sub & bit) != 0, (group & bit) != 0
            later = pltpu.roll(pltpu.roll(x, 8 - bit, 1), 16 * bit, 2)
            earlier = pltpu.roll(pltpu.roll(x, bit, 1), 128 - 16 * bit, 2)
            x = jnp.where(in_sub == in_group, x, jnp.where(in_group, later, earlier))
        sides.append(x.reshape(64, 128))
    lane = lax.broadcasted_iota(jnp.int32, (64, 128), 1)
    for nd in range(4):
        shift = 80 if nd % 2 else 16
        first, second = (sides[1], sides[0]) if nd in (0, 3) else (sides[0], sides[1])
        window[nd] = jnp.where(
            lane < shift, pltpu.roll(first, shift, 1), pltpu.roll(second, shift, 1)
        )
    for txl in range(2):
        for k in range(4):
            start = 12 + 16 * txl + 4 * k
            for nd in range(4):
                out[txl * 16 + k * 4 + nd] = window[nd, start : start + 16, :]


def block_kernel(weight, got, out):
    members = out.shape[0]
    for start in range(0, members, 8):
        field = {r: got[pl.ds(16 * start + r, 8, stride=16), :] for r in range(12)}
        for step in range(ITERS):
            field = {
                r: weight[0, r] * field[r]
                + weight[1, r] * field[r - 1]
                + weight[2, r] * field[r + 1]
                + weight[3, r] * pltpu.roll(field[r], 1, 1)
                + weight[4, r] * pltpu.roll(field[r], 127, 1)
                for r in range(1 + step, 11 - step)
            }
        for i in range(4):
            out[start : start + 8, i, :] = pltpu.roll(field[4 + i], 112, 1)[:, :64]


def ring(count):
    forward = [(i, (i + 1) % count) for i in range(count)]
    return forward, [(b, a) for a, b in forward]


def per_device(
    noise,
    diagonal_tile_blocks,
    left_factors,
    right_factors,
    ranks,
    owner,
    courant_x,
    courant_number_second,
    upwind_x,
    upwind_y,
):
    wide, narrow = lax.axis_size("wide"), lax.axis_size("narrow")
    group = wide // narrow
    devices = wide * narrow
    plane = lax.axis_index("wide") // group
    rows, cols = ranks.shape
    rank_max = left_factors.shape[2]
    members = noise.shape[1]
    cells = noise.shape[2]
    f32 = jnp.float32

    slabs = [[z * group * narrow + i for i in range(group * narrow)] for z in range(narrow)]

    with jax.named_scope("noise_gather"):
        pieces = [
            lax.ppermute(
                noise,
                BOTH,
                [
                    ((z * group + r) * narrow + b, (b * group + (r ^ j)) * narrow + z)
                    for z in range(narrow)
                    for r in range(group)
                    for b in range(narrow)
                ],
            )
            for j in range(group)
        ]

    with jax.named_scope("diagonal_gather"):
        diag = lax.all_gather(jnp.tril(diagonal_tile_blocks).astype(f32), "narrow", tiled=True)

    with jax.named_scope("coefficient_halo"):
        own = jnp.concatenate(
            [
                jnp.where(flag == 1, value, -value)
                for value, flag in ((courant_x, upwind_x), (courant_number_second, upwind_y))
            ],
            axis=1,
        )
        forward, backward = ring(wide)
        own = jnp.concatenate(
            [lax.ppermute(own, "wide", forward), own, lax.ppermute(own, "wide", backward)], axis=0
        )

    with jax.named_scope("factors"):
        keep = (
            jnp.arange(rank_max, dtype=jnp.int32)[None, None, :] < ranks[:, :, None]
        ).astype(f32).reshape(rows, cols * rank_max)
        partial_sums = pl.pallas_call(
            factor_kernel,
            out_shape=pltpu.VMEM((devices, 8, 128), f32),
            in_specs=specs(SMEM, VMEM, pltpu.HBM, pltpu.HBM, pltpu.HBM, *[VMEM] * group),
            out_specs=pl.BlockSpec(memory_space=VMEM),
            scratch_shapes=[
                pltpu.VMEM((cols, members, cells), noise.dtype),
                pltpu.VMEM((rows, members, cols * rank_max), jnp.bfloat16),
                pltpu.VMEM((members * 8, 128), f32),
                pltpu.VMEM(right_factors.shape, right_factors.dtype),
                pltpu.VMEM(left_factors.shape, left_factors.dtype),
                pltpu.VMEM(diag.shape, f32),
                pltpu.SemaphoreType.DMA((group + 2 * rows + 1,)),
            ],
            compiler_params=limit(28),
        )(
            owner,
            near(keep),
            far(right_factors),
            far(left_factors),
            far(diag),
            *[near(piece) for piece in pieces],
        )

    with jax.named_scope("member_exchange"):
        got = lax.all_to_all(partial_sums, BOTH, 0, 0, tiled=True)
        got, own = lax.optimization_barrier((got, own))

    with jax.named_scope("weights"):
        forward, backward = ring(narrow)
        weight = pl.pallas_call(
            weight_kernel,
            out_shape=pltpu.VMEM((5, 12, 8, 128), f32),
            in_specs=specs(VMEM, VMEM, VMEM),
            out_specs=pl.BlockSpec(memory_space=VMEM),
            compiler_params=limit(2),
        )(
            near(lax.ppermute(own, "narrow", forward)),
            near(own),
            near(lax.ppermute(own, "narrow", backward)),
        )

    with jax.named_scope("place"):
        bits = [(owner >> b) & 1 for b in range(7)]
        tile_y = bits[0] | bits[2] << 1 | bits[4] << 2 | bits[6] << 3
        tile_x = bits[1] | bits[3] << 1 | bits[5] << 2
        place = (tile_x * 16 + tile_y - 32 * plane.astype(jnp.int32) + 16) & 127
        blocks = pl.pallas_call(
            place_kernel,
            out_shape=pltpu.VMEM((members, 16, 128), f32),
            in_specs=specs(VMEM, VMEM),
            out_specs=pl.BlockSpec(memory_space=VMEM),
            scratch_shapes=[pltpu.VMEM((256, 128), f32), pltpu.VMEM((4, 64, 128), f32)],
            compiler_params=limit(4),
        )(near(place[None]), near(got.reshape(wide, narrow, 8, 128)))

    with jax.named_scope("block_exchange"):
        mine = lax.all_to_all(blocks, BOTH, 0, 0, axis_index_groups=slabs, tiled=True)

    with jax.named_scope("stencil"):
        return pl.pallas_call(
            block_kernel,
            out_shape=jax.ShapeDtypeStruct((members, 4, 64), f32),
            in_specs=specs(VMEM, VMEM),
            out_specs=pl.BlockSpec(memory_space=VMEM),
            compiler_params=limit(4),
        )(weight, near(mine.reshape(members * 16, 128)))


def solution(mesh):
    placed = (
        P("wide", None, None),
        P(("wide", "narrow"), None, None),
        P("wide", "narrow", None, None),
        P("wide", "narrow", None, None),
        P("wide", "narrow"),
        P(),
        P("wide", "narrow"),
        P("wide", "narrow"),
        P("wide", "narrow"),
        P("wide", "narrow"),
    )
    return jax.shard_map(
        per_device, mesh=mesh, in_specs=placed, out_specs=P(None, "wide", "narrow"), check_vma=False
    )
```

```python
import functools

import jax
import jax.numpy as jnp
import numpy as np
from jax import lax
from jax.experimental import pallas as pl
from jax.experimental.pallas import tpu as pltpu
from jax.sharding import PartitionSpec as P

ITERS = 4
MIXING = 0.05
BOTH = ("wide", "narrow")
VMEM = pltpu.VMEM
SMEM = pltpu.SMEM
MIB = 1 << 20
CHUNKS = 8


def specs(*spaces):
    return [pl.BlockSpec(memory_space=space) for space in spaces]


def near(value):
    return pltpu.with_memory_space_constraint(value, VMEM)


def far(value):
    return pltpu.with_memory_space_constraint(value, pltpu.HBM)


def limit(mib):
    return pltpu.CompilerParams(vmem_limit_bytes=mib * MIB)


def halves(count):
    return slice(0, count // 2), slice(count // 2, count)


def factor_kernel(
    owner,
    keep,
    noise,
    right_far,
    left_far,
    diag_far,
    d1,
    d2,
    d3,
    out,
    coeff,
    turned,
    own,
    right,
    left,
    d0,
    kept,
    done,
):
    rows, cols, rank_max, cells = right.shape
    members = noise.shape[1]
    each = cols // CHUNKS
    chunks = [slice(i * each, (i + 1) * each) for i in range(CHUNKS)]
    pairs = [(right_far.at[:, span], right.at[:, span]) for span in chunks]
    pairs += [(left_far.at[p, span], left.at[p, span]) for p in range(rows) for span in halves(cols)]
    pairs += [(diag_far, d0)]
    copies = [
        pltpu.make_async_copy(source, target, done.at[i])
        for i, (source, target) in enumerate(pairs)
    ]
    copies[-1].start()
    for copy in copies[:CHUNKS]:
        copy.start()
    copies[-1].wait()

    def arrived(i):
        copies[i].wait()
        if i + CHUNKS < len(copies) - 1:
            copies[i + CHUNKS].start()

    w, n = lax.axis_index("wide"), lax.axis_index("narrow")
    lower = lax.broadcasted_iota(jnp.int32, (cells, cells), 0) >= lax.broadcasted_iota(
        jnp.int32, (cells, cells), 1
    )
    for j, diag in enumerate((d0, d1, d2, d3)):
        row = n ^ j
        local = owner[rows * w + row] - cols * n
        held = jnp.logical_and(local >= 0, local < cols)
        kept[...] = jnp.where(lower, diag[...].astype(jnp.float32), 0.0).astype(jnp.bfloat16)
        term = lax.dot_general(
            noise[jnp.clip(local, 0, cols - 1)],
            kept[...],
            (((1,), (1,)), ((), ())),
            preferred_element_type=jnp.float32,
        )
        own[row] = jnp.where(held, term, 0.0)
    for c in range(cols):
        if c % each == 0:
            arrived(c // each)
        span = slice(c * rank_max, (c + 1) * rank_max)
        block = right[:, c].reshape(rows * rank_max, cells)
        product = lax.dot_general(
            noise[c], block, (((1,), (1,)), ((), ())), preferred_element_type=jnp.float32
        )
        for p in range(rows):
            part = product[:, p * rank_max : (p + 1) * rank_max]
            part = jnp.where(keep[p : p + 1, span] > 0, part, 0.0)
            coeff[p, :, span] = part.astype(jnp.bfloat16)
    for p in range(rows):
        total = own[p]
        for i, span in enumerate(halves(cols)):
            arrived(CHUNKS + 2 * p + i)
            total = total + jnp.dot(
                coeff[p, :, rank_max * span.start : rank_max * span.stop],
                left[p, span].reshape(cols // 2 * rank_max, cells),
                preferred_element_type=jnp.float32,
            )
        for g in range(members // 8):
            for h in range(2):
                turned[pl.ds(64 * g + 2 * p + h, 8, stride=8), :] = total[
                    8 * g : 8 * g + 8, 128 * h : 128 * h + 128
                ]
    for d in range(out.shape[0]):
        member = d % members
        out[d] = turned[8 * member : 8 * member + 8, :]


def weight_kernel(low, own, high, out):
    low, own, high = low[...], own[...], high[...]
    lane = lax.broadcasted_iota(jnp.int32, low.shape, 1)
    cx, cy = [
        jnp.where(
            lane < 16,
            pltpu.roll(low, edge, 1),
            jnp.where(lane < 80, pltpu.roll(own, middle, 1), pltpu.roll(high, edge, 1)),
        )
        for edge, middle in ((80, 16), (16, 80))
    ]
    weights = (
        1.0 - jnp.abs(cx) - jnp.abs(cy) - 4.0 * MIXING,
        MIXING + jnp.maximum(cx, 0.0),
        MIXING + jnp.maximum(-cx, 0.0),
        MIXING + jnp.maximum(cy, 0.0),
        MIXING + jnp.maximum(-cy, 0.0),
    )
    for i, weight in enumerate(weights):
        for row in range(12):
            out[i, row] = jnp.broadcast_to(weight[row : row + 1], (8, 128))


def place_kernel(place, got, out, summed, window):
    total = got[:, 0] + got[:, 1] + got[:, 2] + got[:, 3]
    summed[...] = total.reshape(256, 128)
    target = lax.broadcasted_iota(jnp.int32, (64, 128), 0)
    one_hot = jnp.where(target == place[...], 1.0, 0.0).astype(jnp.bfloat16)
    one_hot = jnp.concatenate([one_hot] * 3, axis=1)
    fields = []
    for h in range(2):
        rest = summed[pl.ds(h, 128, stride=2), :]
        parts = []
        for _ in range(3):
            part = rest.astype(jnp.bfloat16)
            parts.append(part)
            rest = rest - part.astype(jnp.float32)
        fields.append(
            jnp.dot(
                one_hot, jnp.concatenate(parts, axis=0), preferred_element_type=jnp.float32
            ).reshape(4, 16, 128)
        )
    shape = (8, 8, 128)
    sub = lax.broadcasted_iota(jnp.int32, shape, 1)
    group = lax.broadcasted_iota(jnp.int32, shape, 2) // 16
    sides = []
    for h in range(2):
        x = jnp.concatenate([f[:, 8 * h : 8 * h + 8] for f in fields], axis=1).reshape(shape)
        for bit in (1, 2, 4):
            in_sub, in_group = (sub & bit) != 0, (group & bit) != 0
            later = pltpu.roll(pltpu.roll(x, 8 - bit, 1), 16 * bit, 2)
            earlier = pltpu.roll(pltpu.roll(x, bit, 1), 128 - 16 * bit, 2)
            x = jnp.where(in_sub == in_group, x, jnp.where(in_group, later, earlier))
        sides.append(x.reshape(64, 128))
    lane = lax.broadcasted_iota(jnp.int32, (64, 128), 1)
    for nd in range(4):
        shift = 80 if nd % 2 else 16
        first, second = (sides[1], sides[0]) if nd in (0, 3) else (sides[0], sides[1])
        window[nd] = jnp.where(
            lane < shift, pltpu.roll(first, shift, 1), pltpu.roll(second, shift, 1)
        )
    for txl in range(2):
        for k in range(4):
            start = 12 + 16 * txl + 4 * k
            for nd in range(4):
                out[txl * 16 + k * 4 + nd] = window[nd, start : start + 16, :]


def block_kernel(weight, got, out):
    members = out.shape[0]
    for start in range(0, members, 8):
        field = {r: got[pl.ds(16 * start + r, 8, stride=16), :] for r in range(12)}
        for step in range(ITERS):
            field = {
                r: weight[0, r] * field[r]
                + weight[1, r] * field[r - 1]
                + weight[2, r] * field[r + 1]
                + weight[3, r] * pltpu.roll(field[r], 1, 1)
                + weight[4, r] * pltpu.roll(field[r], 127, 1)
                for r in range(1 + step, 11 - step)
            }
        for i in range(4):
            out[start : start + 8, i, :] = pltpu.roll(field[4 + i], 112, 1)[:, :64]


def ring(count):
    forward = [(i, (i + 1) % count) for i in range(count)]
    return forward, [(b, a) for a, b in forward]


def per_device(
    noise,
    diagonal_tile_blocks,
    left_factors,
    right_factors,
    ranks,
    owner,
    courant_x,
    courant_number_second,
    upwind_x,
    upwind_y,
):
    wide, narrow = lax.axis_size("wide"), lax.axis_size("narrow")
    group = wide // narrow
    devices = wide * narrow
    plane = lax.axis_index("wide") // group
    rows, cols = ranks.shape
    rank_max = left_factors.shape[2]
    members = noise.shape[1]
    cells = noise.shape[2]
    f32 = jnp.float32

    slabs = [[z * group * narrow + i for i in range(group * narrow)] for z in range(narrow)]

    swap = [
        ((z * group + r) * narrow + b, (b * group + r) * narrow + z)
        for z in range(narrow)
        for r in range(group)
        for b in range(narrow)
    ]
    planes = [[z * group + r for r in range(group)] for z in range(narrow)]

    with jax.named_scope("diagonal_gather"):
        own_diag = diagonal_tile_blocks[0]
        diags = [own_diag] + [
            lax.ppermute(own_diag, "narrow", [(i, i ^ j) for i in range(narrow)])
            for j in range(1, narrow)
        ]

    with jax.named_scope("noise_gather"):
        swapped = lax.ppermute(noise, BOTH, swap)
        sending = jnp.broadcast_to(swapped[None], (group, *swapped.shape))
        columns = lax.all_to_all(
            sending, "wide", 0, 0, axis_index_groups=planes, tiled=True
        ).reshape(cols, members, cells)

    with jax.named_scope("coefficient_halo"):
        own = jnp.concatenate(
            [
                jnp.where(flag == 1, value, -value)
                for value, flag in ((courant_x, upwind_x), (courant_number_second, upwind_y))
            ],
            axis=1,
        )
        sending, own = lax.optimization_barrier((sending, own))
        forward, backward = ring(wide)
        own = jnp.concatenate(
            [lax.ppermute(own, "wide", forward), own, lax.ppermute(own, "wide", backward)], axis=0
        )
        columns, own = lax.optimization_barrier((columns, own))

    with jax.named_scope("factors"):
        keep = (
            jnp.arange(rank_max, dtype=jnp.int32)[None, None, :] < ranks[:, :, None]
        ).astype(f32).reshape(rows, cols * rank_max)
        partial_sums = pl.pallas_call(
            factor_kernel,
            out_shape=pltpu.VMEM((devices, 8, 128), f32),
            in_specs=specs(SMEM, VMEM, VMEM, *[pltpu.HBM] * 3, *[VMEM] * (narrow - 1)),
            out_specs=pl.BlockSpec(memory_space=VMEM),
            scratch_shapes=[
                pltpu.VMEM((rows, members, cols * rank_max), jnp.bfloat16),
                pltpu.VMEM((members * 8, 128), f32),
                pltpu.VMEM((rows, members, cells), f32),
                pltpu.VMEM(right_factors.shape, right_factors.dtype),
                pltpu.VMEM(left_factors.shape, left_factors.dtype),
                pltpu.VMEM(own_diag.shape, own_diag.dtype),
                pltpu.VMEM(own_diag.shape, own_diag.dtype),
                pltpu.SemaphoreType.DMA((CHUNKS + 2 * rows + 1,)),
            ],
            compiler_params=limit(24),
        )(
            far(owner),
            near(keep),
            near(columns),
            far(right_factors),
            far(left_factors),
            far(diags[0]),
            *[near(d) for d in diags[1:]],
        )

    with jax.named_scope("member_exchange"):
        got = lax.all_to_all(partial_sums, BOTH, 0, 0, tiled=True)
        got, own = lax.optimization_barrier((got, own))

    with jax.named_scope("weights"):
        forward, backward = ring(narrow)
        weight = pl.pallas_call(
            weight_kernel,
            out_shape=pltpu.VMEM((5, 12, 8, 128), f32),
            in_specs=specs(VMEM, VMEM, VMEM),
            out_specs=pl.BlockSpec(memory_space=VMEM),
            compiler_params=limit(2),
        )(
            near(lax.ppermute(own, "narrow", forward)),
            near(own),
            near(lax.ppermute(own, "narrow", backward)),
        )

    with jax.named_scope("place"):
        bits = [(owner >> b) & 1 for b in range(7)]
        tile_y = bits[0] | bits[2] << 1 | bits[4] << 2 | bits[6] << 3
        tile_x = bits[1] | bits[3] << 1 | bits[5] << 2
        place = (tile_x * 16 + tile_y - 32 * plane.astype(jnp.int32) + 16) & 127
        blocks = pl.pallas_call(
            place_kernel,
            out_shape=pltpu.VMEM((members, 16, 128), f32),
            in_specs=specs(VMEM, VMEM),
            out_specs=pl.BlockSpec(memory_space=VMEM),
            scratch_shapes=[pltpu.VMEM((256, 128), f32), pltpu.VMEM((4, 64, 128), f32)],
            compiler_params=limit(4),
        )(near(place[None]), near(got.reshape(wide, narrow, 8, 128)))

    with jax.named_scope("block_exchange"):
        mine = lax.all_to_all(blocks, BOTH, 0, 0, axis_index_groups=slabs, tiled=True)

    with jax.named_scope("stencil"):
        return pl.pallas_call(
            block_kernel,
            out_shape=jax.ShapeDtypeStruct((members, 4, 64), f32),
            in_specs=specs(VMEM, VMEM),
            out_specs=pl.BlockSpec(memory_space=VMEM),
            compiler_params=limit(4),
        )(weight, near(mine.reshape(members * 16, 128)))


def solution(mesh):
    placed = (
        P("wide", None, None),
        P(("wide", "narrow"), None, None),
        P("wide", "narrow", None, None),
        P("wide", "narrow", None, None),
        P("wide", "narrow"),
        P(),
        P("wide", "narrow"),
        P("wide", "narrow"),
        P("wide", "narrow"),
        P("wide", "narrow"),
    )
    return jax.shard_map(
        per_device, mesh=mesh, in_specs=placed, out_specs=P(None, "wide", "narrow"), check_vma=False
    )
```

```python
import functools

import jax
import jax.numpy as jnp
import numpy as np
from jax import lax
from jax.experimental import pallas as pl
from jax.experimental.pallas import tpu as pltpu
from jax.sharding import PartitionSpec as P

ITERS = 4
MIXING = 0.05
BOTH = ("wide", "narrow")
VMEM = pltpu.VMEM
SMEM = pltpu.SMEM
MIB = 1 << 20
CHUNKS = 8


def specs(*spaces):
    return [pl.BlockSpec(memory_space=space) for space in spaces]


def near(value):
    return pltpu.with_memory_space_constraint(value, VMEM)


def far(value):
    return pltpu.with_memory_space_constraint(value, pltpu.HBM)


def limit(mib):
    return pltpu.CompilerParams(vmem_limit_bytes=mib * MIB)


def halves(count):
    return slice(0, count // 2), slice(count // 2, count)


def diagonal_term(owner, noise, block, row, cols, rows):
    local = owner[rows * lax.axis_index("wide") + row] - cols * lax.axis_index("narrow")
    held = jnp.logical_and(local >= 0, local < cols)
    term = lax.dot_general(
        noise[jnp.clip(local, 0, cols - 1)],
        block[...],
        (((1,), (1,)), ((), ())),
        preferred_element_type=jnp.float32,
    )
    return jnp.where(held, term, 0.0)


def lower_part(block):
    shape = block.shape
    lower = lax.broadcasted_iota(jnp.int32, shape, 0) >= lax.broadcasted_iota(jnp.int32, shape, 1)
    return jnp.where(lower, block.astype(jnp.float32), 0.0).astype(jnp.bfloat16)


def factor_kernel(
    owner,
    keep,
    noise,
    right_far,
    left_far,
    diag_far,
    out,
    coeff,
    own,
    right,
    left,
    diag,
    kept,
    done,
):
    rows, cols, rank_max, cells = right.shape
    each = cols // CHUNKS
    chunks = [slice(i * each, (i + 1) * each) for i in range(CHUNKS)]
    pairs = [(right_far.at[:, span], right.at[:, span]) for span in chunks]
    pairs += [(left_far.at[p, span], left.at[p, span]) for p in range(rows) for span in halves(cols)]
    pairs += [(diag_far, diag)]
    copies = [
        pltpu.make_async_copy(source, target, done.at[i])
        for i, (source, target) in enumerate(pairs)
    ]
    for copy in copies[:CHUNKS]:
        copy.start()

    def arrived(i):
        copies[i].wait()
        copies[i + CHUNKS].start()

    for c in range(cols):
        if c % each == 0:
            arrived(c // each)
        span = slice(c * rank_max, (c + 1) * rank_max)
        block = right[:, c].reshape(rows * rank_max, cells)
        product = lax.dot_general(
            noise[c], block, (((1,), (1,)), ((), ())), preferred_element_type=jnp.float32
        )
        for p in range(rows):
            part = product[:, p * rank_max : (p + 1) * rank_max]
            part = jnp.where(keep[p : p + 1, span] > 0, part, 0.0)
            coeff[p, :, span] = part.astype(jnp.bfloat16)
        if c == cols - 1:
            copies[CHUNKS + 2 * rows].start()
            own[...] = jnp.zeros_like(own)
    for p in range(rows):
        total = 0.0
        for i, span in enumerate(halves(cols)):
            copies[CHUNKS + 2 * p + i].wait()
            if p == 0 and i == 1:
                copies[CHUNKS + 2 * rows].wait()
                kept[...] = lower_part(diag[...])
                row = lax.axis_index("narrow")
                own[row] = diagonal_term(owner, noise, kept, row, cols, rows)
            total = total + jnp.dot(
                coeff[p, :, rank_max * span.start : rank_max * span.stop],
                left[p, span].reshape(cols // 2 * rank_max, cells),
                preferred_element_type=jnp.float32,
            )
        out[p] = total + own[p]


def finish_kernel(owner, noise, sums, d1, d2, d3, out, turned, own, kept):
    rows, members, cells = sums.shape
    cols = noise.shape[0]
    own[...] = sums[...]
    for j, diag in enumerate((d1, d2, d3)):
        kept[j] = lower_part(diag[...])
    for j in range(rows - 1):
        row = lax.axis_index("narrow") ^ (j + 1)
        own[row] = own[row] + diagonal_term(owner, noise, kept.at[j], row, cols, rows)
    for p in range(rows):
        for g in range(members // 8):
            for h in range(2):
                turned[pl.ds(64 * g + 2 * p + h, 8, stride=8), :] = own[
                    p, 8 * g : 8 * g + 8, 128 * h : 128 * h + 128
                ]
    for d in range(out.shape[0]):
        member = d % members
        out[d] = turned[8 * member : 8 * member + 8, :]


def weight_kernel(low, own, high, out):
    low, own, high = low[...], own[...], high[...]
    lane = lax.broadcasted_iota(jnp.int32, low.shape, 1)
    cx, cy = [
        jnp.where(
            lane < 16,
            pltpu.roll(low, edge, 1),
            jnp.where(lane < 80, pltpu.roll(own, middle, 1), pltpu.roll(high, edge, 1)),
        )
        for edge, middle in ((80, 16), (16, 80))
    ]
    weights = (
        1.0 - jnp.abs(cx) - jnp.abs(cy) - 4.0 * MIXING,
        MIXING + jnp.maximum(cx, 0.0),
        MIXING + jnp.maximum(-cx, 0.0),
        MIXING + jnp.maximum(cy, 0.0),
        MIXING + jnp.maximum(-cy, 0.0),
    )
    for i, weight in enumerate(weights):
        for row in range(12):
            out[i, row] = jnp.broadcast_to(weight[row : row + 1], (8, 128))


def place_kernel(place, got, out, summed, window):
    total = got[:, 0] + got[:, 1] + got[:, 2] + got[:, 3]
    summed[...] = total.reshape(256, 128)
    target = lax.broadcasted_iota(jnp.int32, (64, 128), 0)
    one_hot = jnp.where(target == place[...], 1.0, 0.0).astype(jnp.bfloat16)
    one_hot = jnp.concatenate([one_hot] * 3, axis=1)
    fields = []
    for h in range(2):
        rest = summed[pl.ds(h, 128, stride=2), :]
        parts = []
        for _ in range(3):
            part = rest.astype(jnp.bfloat16)
            parts.append(part)
            rest = rest - part.astype(jnp.float32)
        fields.append(
            jnp.dot(
                one_hot, jnp.concatenate(parts, axis=0), preferred_element_type=jnp.float32
            ).reshape(4, 16, 128)
        )
    shape = (8, 8, 128)
    sub = lax.broadcasted_iota(jnp.int32, shape, 1)
    group = lax.broadcasted_iota(jnp.int32, shape, 2) // 16
    sides = []
    for h in range(2):
        x = jnp.concatenate([f[:, 8 * h : 8 * h + 8] for f in fields], axis=1).reshape(shape)
        for bit in (1, 2, 4):
            in_sub, in_group = (sub & bit) != 0, (group & bit) != 0
            later = pltpu.roll(pltpu.roll(x, 8 - bit, 1), 16 * bit, 2)
            earlier = pltpu.roll(pltpu.roll(x, bit, 1), 128 - 16 * bit, 2)
            x = jnp.where(in_sub == in_group, x, jnp.where(in_group, later, earlier))
        sides.append(x.reshape(64, 128))
    lane = lax.broadcasted_iota(jnp.int32, (64, 128), 1)
    for nd in range(4):
        shift = 80 if nd % 2 else 16
        first, second = (sides[1], sides[0]) if nd in (0, 3) else (sides[0], sides[1])
        window[nd] = jnp.where(
            lane < shift, pltpu.roll(first, shift, 1), pltpu.roll(second, shift, 1)
        )
    for txl in range(2):
        for k in range(4):
            start = 12 + 16 * txl + 4 * k
            for nd in range(4):
                out[txl * 16 + k * 4 + nd] = window[nd, start : start + 16, :]


def block_kernel(weight, got, out):
    members = out.shape[0]
    for start in range(0, members, 8):
        field = {r: got[pl.ds(16 * start + r, 8, stride=16), :] for r in range(12)}
        for step in range(ITERS):
            field = {
                r: weight[0, r] * field[r]
                + weight[1, r] * field[r - 1]
                + weight[2, r] * field[r + 1]
                + weight[3, r] * pltpu.roll(field[r], 1, 1)
                + weight[4, r] * pltpu.roll(field[r], 127, 1)
                for r in range(1 + step, 11 - step)
            }
        for i in range(4):
            out[start : start + 8, i, :] = pltpu.roll(field[4 + i], 112, 1)[:, :64]


def ring(count):
    forward = [(i, (i + 1) % count) for i in range(count)]
    return forward, [(b, a) for a, b in forward]


def per_device(
    noise,
    diagonal_tile_blocks,
    left_factors,
    right_factors,
    ranks,
    owner,
    courant_x,
    courant_number_second,
    upwind_x,
    upwind_y,
):
    wide, narrow = lax.axis_size("wide"), lax.axis_size("narrow")
    group = wide // narrow
    devices = wide * narrow
    plane = lax.axis_index("wide") // group
    rows, cols = ranks.shape
    rank_max = left_factors.shape[2]
    members = noise.shape[1]
    cells = noise.shape[2]
    f32 = jnp.float32

    slabs = [[z * group * narrow + i for i in range(group * narrow)] for z in range(narrow)]

    swap = [
        ((z * group + r) * narrow + b, (b * group + r) * narrow + z)
        for z in range(narrow)
        for r in range(group)
        for b in range(narrow)
    ]
    planes = [[z * group + r for r in range(group)] for z in range(narrow)]

    with jax.named_scope("noise_gather"):
        swapped = lax.ppermute(noise, BOTH, swap)
        sending = jnp.broadcast_to(swapped[None], (group, *swapped.shape))
        columns = lax.all_to_all(
            sending, "wide", 0, 0, axis_index_groups=planes, tiled=True
        ).reshape(cols, members, cells)

    with jax.named_scope("coefficient_halo"):
        own = jnp.concatenate(
            [
                jnp.where(flag == 1, value, -value)
                for value, flag in ((courant_x, upwind_x), (courant_number_second, upwind_y))
            ],
            axis=1,
        )
        columns, own, own_diag = lax.optimization_barrier((columns, own, diagonal_tile_blocks[0]))
        forward, backward = ring(wide)
        own = jnp.concatenate(
            [lax.ppermute(own, "wide", forward), own, lax.ppermute(own, "wide", backward)], axis=0
        )

    with jax.named_scope("diagonal_gather"):
        diags = [
            lax.ppermute(own_diag, "narrow", [(i, i ^ j) for i in range(narrow)])
            for j in range(1, narrow)
        ]

    with jax.named_scope("factors"):
        keep = (
            jnp.arange(rank_max, dtype=jnp.int32)[None, None, :] < ranks[:, :, None]
        ).astype(f32).reshape(rows, cols * rank_max)
        columns = near(columns)
        sums = pl.pallas_call(
            factor_kernel,
            out_shape=pltpu.VMEM((rows, members, cells), f32),
            in_specs=specs(SMEM, VMEM, VMEM, *[pltpu.HBM] * 3),
            out_specs=pl.BlockSpec(memory_space=VMEM),
            scratch_shapes=[
                pltpu.VMEM((rows, members, cols * rank_max), jnp.bfloat16),
                pltpu.VMEM((rows, members, cells), f32),
                pltpu.VMEM(right_factors.shape, right_factors.dtype),
                pltpu.VMEM(left_factors.shape, left_factors.dtype),
                pltpu.VMEM((cells, cells), own_diag.dtype),
                pltpu.VMEM((cells, cells), own_diag.dtype),
                pltpu.SemaphoreType.DMA((CHUNKS + 2 * rows + 1,)),
            ],
            compiler_params=limit(24),
            cost_estimate=pl.CostEstimate(
                flops=0, transcendentals=0, bytes_accessed=4 * right_factors.size
            ),
        )(
            far(owner),
            near(keep),
            columns,
            far(right_factors),
            far(left_factors),
            far(diagonal_tile_blocks[0]),
        )
        partial_sums = pl.pallas_call(
            finish_kernel,
            out_shape=pltpu.VMEM((devices, 8, 128), f32),
            in_specs=specs(SMEM, *[VMEM] * 5),
            out_specs=pl.BlockSpec(memory_space=VMEM),
            scratch_shapes=[
                pltpu.VMEM((members * 8, 128), f32),
                pltpu.VMEM((rows, members, cells), f32),
                pltpu.VMEM((narrow - 1, cells, cells), own_diag.dtype),
            ],
            compiler_params=limit(4),
        )(far(owner), columns, sums, *[near(d) for d in diags])

    with jax.named_scope("member_exchange"):
        partial_sums, own = lax.optimization_barrier((partial_sums, own))
        got = lax.all_to_all(partial_sums, BOTH, 0, 0, tiled=True)

    with jax.named_scope("weights"):
        forward, backward = ring(narrow)
        weight = pl.pallas_call(
            weight_kernel,
            out_shape=pltpu.VMEM((5, 12, 8, 128), f32),
            in_specs=specs(VMEM, VMEM, VMEM),
            out_specs=pl.BlockSpec(memory_space=VMEM),
            compiler_params=limit(2),
        )(
            near(lax.ppermute(own, "narrow", forward)),
            near(own),
            near(lax.ppermute(own, "narrow", backward)),
        )

    with jax.named_scope("place"):
        bits = [(owner >> b) & 1 for b in range(7)]
        tile_y = bits[0] | bits[2] << 1 | bits[4] << 2 | bits[6] << 3
        tile_x = bits[1] | bits[3] << 1 | bits[5] << 2
        place = (tile_x * 16 + tile_y - 32 * plane.astype(jnp.int32) + 16) & 127
        blocks = pl.pallas_call(
            place_kernel,
            out_shape=pltpu.VMEM((members, 16, 128), f32),
            in_specs=specs(VMEM, VMEM),
            out_specs=pl.BlockSpec(memory_space=VMEM),
            scratch_shapes=[pltpu.VMEM((256, 128), f32), pltpu.VMEM((4, 64, 128), f32)],
            compiler_params=limit(4),
        )(near(place[None]), near(got.reshape(wide, narrow, 8, 128)))

    with jax.named_scope("block_exchange"):
        mine = lax.all_to_all(blocks, BOTH, 0, 0, axis_index_groups=slabs, tiled=True)

    with jax.named_scope("stencil"):
        return pl.pallas_call(
            block_kernel,
            out_shape=jax.ShapeDtypeStruct((members, 4, 64), f32),
            in_specs=specs(VMEM, VMEM),
            out_specs=pl.BlockSpec(memory_space=VMEM),
            compiler_params=limit(4),
        )(weight, near(mine.reshape(members * 16, 128)))


def solution(mesh):
    placed = (
        P("wide", None, None),
        P(("wide", "narrow"), None, None),
        P("wide", "narrow", None, None),
        P("wide", "narrow", None, None),
        P("wide", "narrow"),
        P(),
        P("wide", "narrow"),
        P("wide", "narrow"),
        P("wide", "narrow"),
        P("wide", "narrow"),
    )
    return jax.shard_map(
        per_device, mesh=mesh, in_specs=placed, out_specs=P(None, "wide", "narrow"), check_vma=False
    )
```

```python
import functools

import jax
import jax.numpy as jnp
import numpy as np
from jax import lax
from jax.experimental import pallas as pl
from jax.experimental.pallas import tpu as pltpu
from jax.sharding import PartitionSpec as P

ITERS = 4
MIXING = 0.05
BOTH = ("wide", "narrow")
VMEM = pltpu.VMEM
SMEM = pltpu.SMEM
MIB = 1 << 20
CHUNKS = 8


def specs(*spaces):
    return [pl.BlockSpec(memory_space=space) for space in spaces]


def near(value):
    return pltpu.with_memory_space_constraint(value, VMEM)


def far(value):
    return pltpu.with_memory_space_constraint(value, pltpu.HBM)


def limit(mib):
    return pltpu.CompilerParams(vmem_limit_bytes=mib * MIB)


def halves(count):
    return slice(0, count // 2), slice(count // 2, count)


def factor_kernel(
    owner,
    keep,
    noise,
    right_far,
    left_far,
    diag_far,
    d1,
    d2,
    d3,
    out,
    coeff,
    turned,
    own,
    right,
    left,
    d0,
    kept,
    done,
):
    rows, cols, rank_max, cells = right.shape
    members = noise.shape[1]
    each = cols // CHUNKS
    chunks = [slice(i * each, (i + 1) * each) for i in range(CHUNKS)]
    pairs = [(right_far.at[:, span], right.at[:, span]) for span in chunks]
    pairs += [(left_far.at[p, span], left.at[p, span]) for p in range(rows) for span in halves(cols)]
    pairs += [(diag_far, d0)]
    copies = [
        pltpu.make_async_copy(source, target, done.at[i])
        for i, (source, target) in enumerate(pairs)
    ]
    copies[-1].start()
    for copy in copies[:CHUNKS]:
        copy.start()
    copies[-1].wait()

    def arrived(i):
        copies[i].wait()
        if i + CHUNKS < len(copies) - 1:
            copies[i + CHUNKS].start()

    w, n = lax.axis_index("wide"), lax.axis_index("narrow")
    lower = lax.broadcasted_iota(jnp.int32, (cells, cells), 0) >= lax.broadcasted_iota(
        jnp.int32, (cells, cells), 1
    )
    for j, diag in enumerate((d0, d1, d2, d3)):
        row = n ^ j
        local = owner[rows * w + row] - cols * n
        held = jnp.logical_and(local >= 0, local < cols)
        kept[...] = jnp.where(lower, diag[...].astype(jnp.float32), 0.0).astype(jnp.bfloat16)
        term = lax.dot_general(
            noise[jnp.clip(local, 0, cols - 1)],
            kept[...],
            (((1,), (1,)), ((), ())),
            preferred_element_type=jnp.float32,
        )
        own[row] = jnp.where(held, term, 0.0)
    for c in range(cols):
        if c % each == 0:
            arrived(c // each)
        span = slice(c * rank_max, (c + 1) * rank_max)
        block = right[:, c].reshape(rows * rank_max, cells)
        product = lax.dot_general(
            noise[c], block, (((1,), (1,)), ((), ())), preferred_element_type=jnp.float32
        )
        for p in range(rows):
            part = product[:, p * rank_max : (p + 1) * rank_max]
            part = jnp.where(keep[p : p + 1, span] > 0, part, 0.0)
            coeff[p, :, span] = part.astype(jnp.bfloat16)
    for p in range(rows):
        total = own[p]
        for i, span in enumerate(halves(cols)):
            arrived(CHUNKS + 2 * p + i)
            total = total + jnp.dot(
                coeff[p, :, rank_max * span.start : rank_max * span.stop],
                left[p, span].reshape(cols // 2 * rank_max, cells),
                preferred_element_type=jnp.float32,
            )
        for g in range(members // 8):
            for h in range(2):
                turned[pl.ds(64 * g + 2 * p + h, 8, stride=8), :] = total[
                    8 * g : 8 * g + 8, 128 * h : 128 * h + 128
                ]
    for d in range(out.shape[0]):
        member = d % members
        out[d] = turned[8 * member : 8 * member + 8, :]


def weight_kernel(low, own, high, out):
    low, own, high = low[...], own[...], high[...]
    lane = lax.broadcasted_iota(jnp.int32, low.shape, 1)
    cx, cy = [
        jnp.where(
            lane < 16,
            pltpu.roll(low, edge, 1),
            jnp.where(lane < 80, pltpu.roll(own, middle, 1), pltpu.roll(high, edge, 1)),
        )
        for edge, middle in ((80, 16), (16, 80))
    ]
    weights = (
        1.0 - jnp.abs(cx) - jnp.abs(cy) - 4.0 * MIXING,
        MIXING + jnp.maximum(cx, 0.0),
        MIXING + jnp.maximum(-cx, 0.0),
        MIXING + jnp.maximum(cy, 0.0),
        MIXING + jnp.maximum(-cy, 0.0),
    )
    for i, weight in enumerate(weights):
        for row in range(12):
            out[i, row] = jnp.broadcast_to(weight[row : row + 1], (8, 128))


def place_kernel(place, got, out, summed, window):
    total = got[:, 0] + got[:, 1] + got[:, 2] + got[:, 3]
    summed[...] = total.reshape(256, 128)
    target = lax.broadcasted_iota(jnp.int32, (64, 128), 0)
    one_hot = jnp.where(target == place[...], 1.0, 0.0).astype(jnp.bfloat16)
    one_hot = jnp.concatenate([one_hot] * 3, axis=1)
    fields = []
    for h in range(2):
        rest = summed[pl.ds(h, 128, stride=2), :]
        parts = []
        for _ in range(3):
            part = rest.astype(jnp.bfloat16)
            parts.append(part)
            rest = rest - part.astype(jnp.float32)
        fields.append(
            jnp.dot(
                one_hot, jnp.concatenate(parts, axis=0), preferred_element_type=jnp.float32
            ).reshape(4, 16, 128)
        )
    shape = (8, 8, 128)
    sub = lax.broadcasted_iota(jnp.int32, shape, 1)
    group = lax.broadcasted_iota(jnp.int32, shape, 2) // 16
    sides = []
    for h in range(2):
        x = jnp.concatenate([f[:, 8 * h : 8 * h + 8] for f in fields], axis=1).reshape(shape)
        for bit in (1, 2, 4):
            in_sub, in_group = (sub & bit) != 0, (group & bit) != 0
            later = pltpu.roll(pltpu.roll(x, 8 - bit, 1), 16 * bit, 2)
            earlier = pltpu.roll(pltpu.roll(x, bit, 1), 128 - 16 * bit, 2)
            x = jnp.where(in_sub == in_group, x, jnp.where(in_group, later, earlier))
        sides.append(x.reshape(64, 128))
    lane = lax.broadcasted_iota(jnp.int32, (64, 128), 1)
    for nd in range(4):
        shift = 80 if nd % 2 else 16
        first, second = (sides[1], sides[0]) if nd in (0, 3) else (sides[0], sides[1])
        window[nd] = jnp.where(
            lane < shift, pltpu.roll(first, shift, 1), pltpu.roll(second, shift, 1)
        )
    for txl in range(2):
        for k in range(4):
            start = 12 + 16 * txl + 4 * k
            for nd in range(4):
                out[txl * 16 + k * 4 + nd] = window[nd, start : start + 16, :]


def block_kernel(weight, got, out):
    members = out.shape[0]
    for start in range(0, members, 8):
        field = {r: got[pl.ds(16 * start + r, 8, stride=16), :] for r in range(12)}
        for step in range(ITERS):
            field = {
                r: weight[0, r] * field[r]
                + weight[1, r] * field[r - 1]
                + weight[2, r] * field[r + 1]
                + weight[3, r] * pltpu.roll(field[r], 1, 1)
                + weight[4, r] * pltpu.roll(field[r], 127, 1)
                for r in range(1 + step, 11 - step)
            }
        for i in range(4):
            out[start : start + 8, i, :] = pltpu.roll(field[4 + i], 112, 1)[:, :64]


def ring(count):
    forward = [(i, (i + 1) % count) for i in range(count)]
    return forward, [(b, a) for a, b in forward]


def per_device(
    noise,
    diagonal_tile_blocks,
    left_factors,
    right_factors,
    ranks,
    owner,
    courant_x,
    courant_number_second,
    upwind_x,
    upwind_y,
):
    wide, narrow = lax.axis_size("wide"), lax.axis_size("narrow")
    group = wide // narrow
    devices = wide * narrow
    plane = lax.axis_index("wide") // group
    rows, cols = ranks.shape
    rank_max = left_factors.shape[2]
    members = noise.shape[1]
    cells = noise.shape[2]
    f32 = jnp.float32

    slabs = [[z * group * narrow + i for i in range(group * narrow)] for z in range(narrow)]

    def server(plane_to, source):
        return source ^ (3, 1, 0, 2)[(plane_to - source) % 4]

    swap = [
        ((s * group + r) * narrow + server(z, s), (z * group + r) * narrow + s)
        for s in range(narrow)
        for r in range(group)
        for z in range(narrow)
    ]
    planes = [[z * group + r for r in range(group)] for z in range(narrow)]

    with jax.named_scope("diagonal_gather"):
        own_diag = diagonal_tile_blocks[0]
        beside, across = [[(i, i ^ j) for i in range(narrow)] for j in (1, 2)]
        opposite = lax.ppermute(own_diag, "narrow", across)
        diags = [
            own_diag,
            lax.ppermute(own_diag, "narrow", beside),
            opposite,
            lax.ppermute(opposite, "narrow", beside),
        ]

    with jax.named_scope("noise_gather"):
        swapped = lax.ppermute(noise, BOTH, swap)

    with jax.named_scope("coefficient_halo"):
        own = jnp.concatenate(
            [
                jnp.where(flag == 1, value, -value)
                for value, flag in ((courant_x, upwind_x), (courant_number_second, upwind_y))
            ],
            axis=1,
        )
        forward, backward = ring(wide)
        own = jnp.concatenate(
            [lax.ppermute(own, "wide", forward), own, lax.ppermute(own, "wide", backward)], axis=0
        )

    with jax.named_scope("noise_gather"):
        sending = jnp.broadcast_to(swapped[None], (group, *swapped.shape))
        sending, own = lax.optimization_barrier((sending, own))
        columns = lax.all_to_all(
            sending, "wide", 0, 0, axis_index_groups=planes, tiled=True
        ).reshape(cols, members, cells)

    with jax.named_scope("factors"):
        keep = (
            jnp.arange(rank_max, dtype=jnp.int32)[None, None, :] < ranks[:, :, None]
        ).astype(f32).reshape(rows, cols * rank_max)
        partial_sums = pl.pallas_call(
            factor_kernel,
            out_shape=pltpu.VMEM((devices, 8, 128), f32),
            in_specs=specs(SMEM, VMEM, VMEM, *[pltpu.HBM] * 3, *[VMEM] * (narrow - 1)),
            out_specs=pl.BlockSpec(memory_space=VMEM),
            scratch_shapes=[
                pltpu.VMEM((rows, members, cols * rank_max), jnp.bfloat16),
                pltpu.VMEM((members * 8, 128), f32),
                pltpu.VMEM((rows, members, cells), f32),
                pltpu.VMEM(right_factors.shape, right_factors.dtype),
                pltpu.VMEM(left_factors.shape, left_factors.dtype),
                pltpu.VMEM(own_diag.shape, own_diag.dtype),
                pltpu.VMEM(own_diag.shape, own_diag.dtype),
                pltpu.SemaphoreType.DMA((CHUNKS + 2 * rows + 1,)),
            ],
            compiler_params=limit(24),
        )(
            far(owner),
            near(keep),
            near(columns),
            far(right_factors),
            far(left_factors),
            far(diags[0]),
            *[near(d) for d in diags[1:]],
        )

    with jax.named_scope("member_exchange"):
        got = lax.all_to_all(partial_sums, BOTH, 0, 0, tiled=True)
        got, own = lax.optimization_barrier((got, own))

    with jax.named_scope("weights"):
        forward, backward = ring(narrow)
        weight = pl.pallas_call(
            weight_kernel,
            out_shape=pltpu.VMEM((5, 12, 8, 128), f32),
            in_specs=specs(VMEM, VMEM, VMEM),
            out_specs=pl.BlockSpec(memory_space=VMEM),
            compiler_params=limit(2),
        )(
            near(lax.ppermute(own, "narrow", forward)),
            near(own),
            near(lax.ppermute(own, "narrow", backward)),
        )

    with jax.named_scope("place"):
        bits = [(owner >> b) & 1 for b in range(7)]
        tile_y = bits[0] | bits[2] << 1 | bits[4] << 2 | bits[6] << 3
        tile_x = bits[1] | bits[3] << 1 | bits[5] << 2
        place = (tile_x * 16 + tile_y - 32 * plane.astype(jnp.int32) + 16) & 127
        blocks = pl.pallas_call(
            place_kernel,
            out_shape=pltpu.VMEM((members, 16, 128), f32),
            in_specs=specs(VMEM, VMEM),
            out_specs=pl.BlockSpec(memory_space=VMEM),
            scratch_shapes=[pltpu.VMEM((256, 128), f32), pltpu.VMEM((4, 64, 128), f32)],
            compiler_params=limit(4),
        )(near(place[None]), near(got.reshape(wide, narrow, 8, 128)))

    with jax.named_scope("block_exchange"):
        mine = lax.all_to_all(blocks, BOTH, 0, 0, axis_index_groups=slabs, tiled=True)

    with jax.named_scope("stencil"):
        return pl.pallas_call(
            block_kernel,
            out_shape=jax.ShapeDtypeStruct((members, 4, 64), f32),
            in_specs=specs(VMEM, VMEM),
            out_specs=pl.BlockSpec(memory_space=VMEM),
            compiler_params=limit(4),
        )(weight, near(mine.reshape(members * 16, 128)))


def solution(mesh):
    placed = (
        P("wide", None, None),
        P(("wide", "narrow"), None, None),
        P("wide", "narrow", None, None),
        P("wide", "narrow", None, None),
        P("wide", "narrow"),
        P(),
        P("wide", "narrow"),
        P("wide", "narrow"),
        P("wide", "narrow"),
        P("wide", "narrow"),
    )
    return jax.shard_map(
        per_device, mesh=mesh, in_specs=placed, out_specs=P(None, "wide", "narrow"), check_vma=False
    )
```

```python
import functools

import jax
import jax.numpy as jnp
import numpy as np
from jax import lax
from jax.experimental import pallas as pl
from jax.experimental.pallas import tpu as pltpu
from jax.sharding import PartitionSpec as P

ITERS = 4
MIXING = 0.05
BOTH = ("wide", "narrow")
VMEM = pltpu.VMEM
SMEM = pltpu.SMEM
MIB = 1 << 20
CHUNKS = 8


def specs(*spaces):
    return [pl.BlockSpec(memory_space=space) for space in spaces]


def near(value):
    return pltpu.with_memory_space_constraint(value, VMEM)


def far(value):
    return pltpu.with_memory_space_constraint(value, pltpu.HBM)


def limit(mib):
    return pltpu.CompilerParams(vmem_limit_bytes=mib * MIB)


def halves(count):
    return slice(0, count // 2), slice(count // 2, count)


def factor_kernel(
    owner,
    keep,
    noise,
    right_far,
    left_far,
    diag_far,
    d1,
    d2,
    d3,
    out,
    coeff,
    turned,
    own,
    right,
    left,
    d0,
    kept,
    done,
):
    rows, cols, rank_max, cells = right.shape
    members = noise.shape[1]
    each = cols // CHUNKS
    chunks = [slice(i * each, (i + 1) * each) for i in range(CHUNKS)]
    pairs = [(right_far.at[:, span], right.at[:, span]) for span in chunks]
    pairs += [(left_far.at[p, span], left.at[p, span]) for p in range(rows) for span in halves(cols)]
    pairs += [(diag_far, d0)]
    copies = [
        pltpu.make_async_copy(source, target, done.at[i])
        for i, (source, target) in enumerate(pairs)
    ]
    copies[-1].start()
    for copy in copies[:CHUNKS]:
        copy.start()
    copies[-1].wait()

    def arrived(i):
        copies[i].wait()
        if i + CHUNKS < len(copies) - 1:
            copies[i + CHUNKS].start()

    w, n = lax.axis_index("wide"), lax.axis_index("narrow")
    lower = lax.broadcasted_iota(jnp.int32, (cells, cells), 0) >= lax.broadcasted_iota(
        jnp.int32, (cells, cells), 1
    )
    for j, diag in enumerate((d0, d1, d2, d3)):
        row = n ^ j
        local = owner[rows * w + row] - cols * n
        held = jnp.logical_and(local >= 0, local < cols)
        kept[...] = jnp.where(lower, diag[...].astype(jnp.float32), 0.0).astype(jnp.bfloat16)
        term = lax.dot_general(
            noise[jnp.clip(local, 0, cols - 1)],
            kept[...],
            (((1,), (1,)), ((), ())),
            preferred_element_type=jnp.float32,
        )
        own[row] = jnp.where(held, term, 0.0)
    for c in range(cols):
        if c % each == 0:
            arrived(c // each)
        span = slice(c * rank_max, (c + 1) * rank_max)
        block = right[:, c].reshape(rows * rank_max, cells)
        product = lax.dot_general(
            noise[c], block, (((1,), (1,)), ((), ())), preferred_element_type=jnp.float32
        )
        for p in range(rows):
            part = product[:, p * rank_max : (p + 1) * rank_max]
            part = jnp.where(keep[p : p + 1, span] > 0, part, 0.0)
            coeff[p, :, span] = part.astype(jnp.bfloat16)
    for p in range(rows):
        total = own[p]
        for i, span in enumerate(halves(cols)):
            arrived(CHUNKS + 2 * p + i)
            total = total + jnp.dot(
                coeff[p, :, rank_max * span.start : rank_max * span.stop],
                left[p, span].reshape(cols // 2 * rank_max, cells),
                preferred_element_type=jnp.float32,
            )
        for g in range(members // 8):
            for h in range(2):
                turned[pl.ds(64 * g + 2 * p + h, 8, stride=8), :] = total[
                    8 * g : 8 * g + 8, 128 * h : 128 * h + 128
                ]
    for d in range(out.shape[0]):
        member = d % members
        out[d] = turned[8 * member : 8 * member + 8, :]


def set_weights(low, own, high, weight):
    lane = lax.broadcasted_iota(jnp.int32, low.shape, 1)
    cx, cy = [
        jnp.where(
            lane < 16,
            pltpu.roll(low, edge, 1),
            jnp.where(lane < 80, pltpu.roll(own, middle, 1), pltpu.roll(high, edge, 1)),
        )
        for edge, middle in ((80, 16), (16, 80))
    ]
    weights = (
        1.0 - jnp.abs(cx) - jnp.abs(cy) - 4.0 * MIXING,
        MIXING + jnp.maximum(cx, 0.0),
        MIXING + jnp.maximum(-cx, 0.0),
        MIXING + jnp.maximum(cy, 0.0),
        MIXING + jnp.maximum(-cy, 0.0),
    )
    for i, value in enumerate(weights):
        for row in range(1, 11):
            weight[i, row] = jnp.broadcast_to(value[row : row + 1], (8, 128))


def place_kernel(place, got, own, forwarded, out, summed, window):
    total = got[:, 0] + got[:, 1] + got[:, 2] + got[:, 3]
    summed[...] = total.reshape(256, 128)
    target = lax.broadcasted_iota(jnp.int32, (64, 128), 0)
    one_hot = jnp.where(target == place[...], 1.0, 0.0).astype(jnp.bfloat16)
    one_hot = jnp.concatenate([one_hot] * 3, axis=1)
    fields = []
    for h in range(2):
        rest = summed[pl.ds(h, 128, stride=2), :]
        parts = []
        for _ in range(3):
            part = rest.astype(jnp.bfloat16)
            parts.append(part)
            rest = rest - part.astype(jnp.float32)
        fields.append(
            jnp.dot(
                one_hot, jnp.concatenate(parts, axis=0), preferred_element_type=jnp.float32
            ).reshape(4, 16, 128)
        )
    shape = (8, 8, 128)
    sub = lax.broadcasted_iota(jnp.int32, shape, 1)
    group = lax.broadcasted_iota(jnp.int32, shape, 2) // 16
    sides = []
    for h in range(2):
        x = jnp.concatenate([f[:, 8 * h : 8 * h + 8] for f in fields], axis=1).reshape(shape)
        for bit in (1, 2, 4):
            in_sub, in_group = (sub & bit) != 0, (group & bit) != 0
            later = pltpu.roll(pltpu.roll(x, 8 - bit, 1), 16 * bit, 2)
            earlier = pltpu.roll(pltpu.roll(x, bit, 1), 128 - 16 * bit, 2)
            x = jnp.where(in_sub == in_group, x, jnp.where(in_group, later, earlier))
        sides.append(x.reshape(64, 128))
    lane = lax.broadcasted_iota(jnp.int32, (64, 128), 1)
    for nd in range(4):
        shift = 80 if nd % 2 else 16
        first, second = (sides[1], sides[0]) if nd in (0, 3) else (sides[0], sides[1])
        window[nd] = jnp.where(
            lane < shift, pltpu.roll(first, shift, 1), pltpu.roll(second, shift, 1)
        )
    first = lax.axis_index("wide") % 8 == 0
    edge = jnp.where(first, forwarded[0:3], forwarded[1:4])
    edge = jnp.concatenate([pltpu.roll(edge, 96 - 32 * q, 1) for q in range(4)], axis=0)
    free = lax.broadcasted_iota(jnp.int32, (12, 128), 1) >= 96
    for txl in range(2):
        for k in range(4):
            start = 12 + 16 * txl + 4 * k
            for nd in range(4):
                d = txl * 16 + k * 4 + nd
                out[d, 0:12] = jnp.where(free, edge, window[nd, start : start + 12, :])
                out[d, 12:16] = own[...]


def block_kernel(slots, got, out, weight):
    members = out.shape[0]
    r = lax.axis_index("wide") % 8
    n = lax.axis_index("narrow")
    lane = lax.broadcasted_iota(jnp.int32, (3, 128), 1)

    def across(slot):
        edge = jnp.zeros((3, 128), jnp.float32)
        for q in range(4):
            moved = pltpu.roll(slots[slot, 3 * q : 3 * q + 3, :], (32 * q + 32) % 128, 1)
            edge = jnp.where(lane // 32 == q, moved, edge)
        return edge

    zero = jnp.zeros((1, 128), jnp.float32)
    around = []
    for step in (3, 0, 1):
        column = (n + step) % 4
        below = slots[jnp.maximum(r - 1, 0) * 4 + column, 13:16, :]
        above = slots[jnp.minimum(r + 1, 7) * 4 + column, 12:15, :]
        below = jnp.where(r == 0, across(28 + column), below)
        above = jnp.where(r == 7, across(column), above)
        around.append(
            jnp.concatenate([zero, below, slots[r * 4 + column, 12:16, :], above, zero], axis=0)
        )
    set_weights(*around, weight)
    for start in range(0, members, 8):
        field = {r: got[pl.ds(16 * start + r, 8, stride=16), :] for r in range(12)}
        for step in range(ITERS):
            field = {
                r: weight[0, r] * field[r]
                + weight[1, r] * field[r - 1]
                + weight[2, r] * field[r + 1]
                + weight[3, r] * pltpu.roll(field[r], 1, 1)
                + weight[4, r] * pltpu.roll(field[r], 127, 1)
                for r in range(1 + step, 11 - step)
            }
        for i in range(4):
            out[start : start + 8, i, :] = pltpu.roll(field[4 + i], 112, 1)[:, :64]


def per_device(
    noise,
    diagonal_tile_blocks,
    left_factors,
    right_factors,
    ranks,
    owner,
    courant_x,
    courant_number_second,
    upwind_x,
    upwind_y,
):
    wide, narrow = lax.axis_size("wide"), lax.axis_size("narrow")
    group = wide // narrow
    devices = wide * narrow
    plane = lax.axis_index("wide") // group
    rows, cols = ranks.shape
    rank_max = left_factors.shape[2]
    members = noise.shape[1]
    cells = noise.shape[2]
    f32 = jnp.float32

    slabs = [[z * group * narrow + i for i in range(group * narrow)] for z in range(narrow)]

    def server(plane_to, source):
        return source ^ (3, 1, 0, 2)[(plane_to - source) % 4]

    swap = [
        ((s * group + r) * narrow + server(z, s), (z * group + r) * narrow + s)
        for s in range(narrow)
        for r in range(group)
        for z in range(narrow)
    ]
    planes = [[z * group + r for r in range(group)] for z in range(narrow)]

    with jax.named_scope("diagonal_gather"):
        own_diag = diagonal_tile_blocks[0]
        beside, across = [[(i, i ^ j) for i in range(narrow)] for j in (1, 2)]
        opposite = lax.ppermute(own_diag, "narrow", across)
        diags = [
            own_diag,
            lax.ppermute(own_diag, "narrow", beside),
            opposite,
            lax.ppermute(opposite, "narrow", beside),
        ]

    with jax.named_scope("noise_gather"):
        swapped = lax.ppermute(noise, BOTH, swap)

    with jax.named_scope("coefficient_halo"):
        own = jnp.concatenate(
            [
                jnp.where(flag == 1, value, -value)
                for value, flag in ((courant_x, upwind_x), (courant_number_second, upwind_y))
            ],
            axis=1,
        )
        last = group - 1
        forwarded = lax.ppermute(
            own,
            BOTH,
            [
                ((z * group + r) * narrow + b, ((z + step) % narrow * group + r) * narrow + b)
                for z in range(narrow)
                for r, step in ((0, -1), (last, 1))
                for b in range(narrow)
            ],
        )

    with jax.named_scope("noise_gather"):
        sending = jnp.broadcast_to(swapped[None], (group, *swapped.shape))
        sending, forwarded = lax.optimization_barrier((sending, forwarded))
        columns = lax.all_to_all(
            sending, "wide", 0, 0, axis_index_groups=planes, tiled=True
        ).reshape(cols, members, cells)

    with jax.named_scope("factors"):
        keep = (
            jnp.arange(rank_max, dtype=jnp.int32)[None, None, :] < ranks[:, :, None]
        ).astype(f32).reshape(rows, cols * rank_max)
        partial_sums = pl.pallas_call(
            factor_kernel,
            out_shape=pltpu.VMEM((devices, 8, 128), f32),
            in_specs=specs(SMEM, VMEM, VMEM, *[pltpu.HBM] * 3, *[VMEM] * (narrow - 1)),
            out_specs=pl.BlockSpec(memory_space=VMEM),
            scratch_shapes=[
                pltpu.VMEM((rows, members, cols * rank_max), jnp.bfloat16),
                pltpu.VMEM((members * 8, 128), f32),
                pltpu.VMEM((rows, members, cells), f32),
                pltpu.VMEM(right_factors.shape, right_factors.dtype),
                pltpu.VMEM(left_factors.shape, left_factors.dtype),
                pltpu.VMEM(own_diag.shape, own_diag.dtype),
                pltpu.VMEM(own_diag.shape, own_diag.dtype),
                pltpu.SemaphoreType.DMA((CHUNKS + 2 * rows + 1,)),
            ],
            compiler_params=limit(24),
        )(
            far(owner),
            near(keep),
            near(columns),
            far(right_factors),
            far(left_factors),
            far(diags[0]),
            *[near(d) for d in diags[1:]],
        )

    with jax.named_scope("member_exchange"):
        got = lax.all_to_all(partial_sums, BOTH, 0, 0, tiled=True)

    with jax.named_scope("place"):
        bits = [(owner >> b) & 1 for b in range(7)]
        tile_y = bits[0] | bits[2] << 1 | bits[4] << 2 | bits[6] << 3
        tile_x = bits[1] | bits[3] << 1 | bits[5] << 2
        place = (tile_x * 16 + tile_y - 32 * plane.astype(jnp.int32) + 16) & 127
        blocks = pl.pallas_call(
            place_kernel,
            out_shape=pltpu.VMEM((members, 16, 128), f32),
            in_specs=specs(*[VMEM] * 4),
            out_specs=pl.BlockSpec(memory_space=VMEM),
            scratch_shapes=[pltpu.VMEM((256, 128), f32), pltpu.VMEM((4, 64, 128), f32)],
            compiler_params=limit(4),
        )(near(place[None]), near(got.reshape(wide, narrow, 8, 128)), near(own), near(forwarded))

    with jax.named_scope("block_exchange"):
        mine = lax.all_to_all(blocks, BOTH, 0, 0, axis_index_groups=slabs, tiled=True)

    with jax.named_scope("stencil"):
        return pl.pallas_call(
            block_kernel,
            out_shape=jax.ShapeDtypeStruct((members, 4, 64), f32),
            in_specs=specs(VMEM, VMEM),
            out_specs=pl.BlockSpec(memory_space=VMEM),
            scratch_shapes=[pltpu.VMEM((5, 12, 8, 128), f32)],
            compiler_params=limit(4),
        )(near(mine), near(mine.reshape(members * 16, 128)))


def solution(mesh):
    placed = (
        P("wide", None, None),
        P(("wide", "narrow"), None, None),
        P("wide", "narrow", None, None),
        P("wide", "narrow", None, None),
        P("wide", "narrow"),
        P(),
        P("wide", "narrow"),
        P("wide", "narrow"),
        P("wide", "narrow"),
        P("wide", "narrow"),
    )
    return jax.shard_map(
        per_device, mesh=mesh, in_specs=placed, out_specs=P(None, "wide", "narrow"), check_vma=False
    )
```

```python
import functools

import jax
import jax.numpy as jnp
import numpy as np
from jax import lax
from jax.experimental import pallas as pl
from jax.experimental.pallas import tpu as pltpu
from jax.sharding import PartitionSpec as P

ITERS = 4
MIXING = 0.05
BOTH = ("wide", "narrow")
VMEM = pltpu.VMEM
SMEM = pltpu.SMEM
MIB = 1 << 20
CHUNKS = 8


def specs(*spaces):
    return [pl.BlockSpec(memory_space=space) for space in spaces]


def near(value):
    return pltpu.with_memory_space_constraint(value, VMEM)


def far(value):
    return pltpu.with_memory_space_constraint(value, pltpu.HBM)


def limit(mib):
    return pltpu.CompilerParams(vmem_limit_bytes=mib * MIB)


def halves(count):
    return slice(0, count // 2), slice(count // 2, count)


def factor_kernel(
    owner,
    keep,
    noise,
    right_far,
    left_far,
    diag_far,
    d1,
    d2,
    d3,
    out,
    coeff,
    turned,
    own,
    right,
    left,
    d0,
    kept,
    done,
):
    rows, cols, rank_max, cells = right.shape
    members = noise.shape[1]
    each = cols // CHUNKS
    chunks = [slice(i * each, (i + 1) * each) for i in range(CHUNKS)]
    pairs = [(right_far.at[:, span], right.at[:, span]) for span in chunks]
    pairs += [(left_far.at[p, span], left.at[p, span]) for p in range(rows) for span in halves(cols)]
    pairs += [(diag_far, d0)]
    copies = [
        pltpu.make_async_copy(source, target, done.at[i])
        for i, (source, target) in enumerate(pairs)
    ]
    copies[-1].start()
    for copy in copies[:CHUNKS]:
        copy.start()
    copies[-1].wait()

    def arrived(i):
        copies[i].wait()
        if i + CHUNKS < len(copies) - 1:
            copies[i + CHUNKS].start()

    w, n = lax.axis_index("wide"), lax.axis_index("narrow")
    lower = lax.broadcasted_iota(jnp.int32, (cells, cells), 0) >= lax.broadcasted_iota(
        jnp.int32, (cells, cells), 1
    )
    for j, diag in enumerate((d0, d1, d2, d3)):
        row = n ^ j
        local = owner[rows * w + row] - cols * n
        held = jnp.logical_and(local >= 0, local < cols)
        kept[...] = jnp.where(lower, diag[...].astype(jnp.float32), 0.0).astype(jnp.bfloat16)
        term = lax.dot_general(
            noise[jnp.clip(local, 0, cols - 1)],
            kept[...],
            (((1,), (1,)), ((), ())),
            preferred_element_type=jnp.float32,
        )
        own[row] = jnp.where(held, term, 0.0)
    for c in range(cols):
        if c % each == 0:
            arrived(c // each)
        span = slice(c * rank_max, (c + 1) * rank_max)
        block = right[:, c].reshape(rows * rank_max, cells)
        product = lax.dot_general(
            noise[c], block, (((1,), (1,)), ((), ())), preferred_element_type=jnp.float32
        )
        for p in range(rows):
            part = product[:, p * rank_max : (p + 1) * rank_max]
            part = jnp.where(keep[p : p + 1, span] > 0, part, 0.0)
            coeff[p, :, span] = part.astype(jnp.bfloat16)
    for p in range(rows):
        total = own[p]
        for i, span in enumerate(halves(cols)):
            arrived(CHUNKS + 2 * p + i)
            total = total + jnp.dot(
                coeff[p, :, rank_max * span.start : rank_max * span.stop],
                left[p, span].reshape(cols // 2 * rank_max, cells),
                preferred_element_type=jnp.float32,
            )
        for g in range(members // 8):
            for h in range(2):
                turned[pl.ds(64 * g + 2 * p + h, 8, stride=8), :] = total[
                    8 * g : 8 * g + 8, 128 * h : 128 * h + 128
                ]
    for d in range(out.shape[0]):
        member = d % members
        out[d] = turned[8 * member : 8 * member + 8, :]


def set_weights(low, own, high, weight):
    lane = lax.broadcasted_iota(jnp.int32, low.shape, 1)
    cx, cy = [
        jnp.where(
            lane < 16,
            pltpu.roll(low, edge, 1),
            jnp.where(lane < 80, pltpu.roll(own, middle, 1), pltpu.roll(high, edge, 1)),
        )
        for edge, middle in ((80, 16), (16, 80))
    ]
    weights = (
        1.0 - jnp.abs(cx) - jnp.abs(cy) - 4.0 * MIXING,
        MIXING + jnp.maximum(cx, 0.0),
        MIXING + jnp.maximum(-cx, 0.0),
        MIXING + jnp.maximum(cy, 0.0),
        MIXING + jnp.maximum(-cy, 0.0),
    )
    for i, value in enumerate(weights):
        for row in range(1, 11):
            weight[i, row] = jnp.broadcast_to(value[row : row + 1], (8, 128))


def place_kernel(place, got, own, forwarded, out, summed, window):
    total = got[:, 0] + got[:, 1] + got[:, 2] + got[:, 3]
    summed[...] = total.reshape(256, 128)
    target = lax.broadcasted_iota(jnp.int32, (64, 128), 0)
    one_hot = jnp.where(target == place[...], 1.0, 0.0).astype(jnp.bfloat16)
    one_hot = jnp.concatenate([one_hot] * 3, axis=1)
    fields = []
    for h in range(2):
        rest = summed[pl.ds(h, 128, stride=2), :]
        parts = []
        for _ in range(3):
            part = rest.astype(jnp.bfloat16)
            parts.append(part)
            rest = rest - part.astype(jnp.float32)
        fields.append(
            jnp.dot(
                one_hot, jnp.concatenate(parts, axis=0), preferred_element_type=jnp.float32
            ).reshape(4, 16, 128)
        )
    shape = (8, 8, 128)
    sub = lax.broadcasted_iota(jnp.int32, shape, 1)
    group = lax.broadcasted_iota(jnp.int32, shape, 2) // 16
    sides = []
    for h in range(2):
        x = jnp.concatenate([f[:, 8 * h : 8 * h + 8] for f in fields], axis=1).reshape(shape)
        for bit in (1, 2, 4):
            in_sub, in_group = (sub & bit) != 0, (group & bit) != 0
            later = pltpu.roll(pltpu.roll(x, 8 - bit, 1), 16 * bit, 2)
            earlier = pltpu.roll(pltpu.roll(x, bit, 1), 128 - 16 * bit, 2)
            x = jnp.where(in_sub == in_group, x, jnp.where(in_group, later, earlier))
        sides.append(x.reshape(64, 128))
    lane = lax.broadcasted_iota(jnp.int32, (64, 128), 1)
    for nd in range(4):
        shift = 80 if nd % 2 else 16
        first, second = (sides[1], sides[0]) if nd in (0, 3) else (sides[0], sides[1])
        window[nd] = jnp.where(
            lane < shift, pltpu.roll(first, shift, 1), pltpu.roll(second, shift, 1)
        )
    first = lax.axis_index("wide") % 8 == 0
    edge = jnp.where(first, forwarded[0:3], forwarded[1:4])
    edge = jnp.concatenate([pltpu.roll(edge, 96 - 32 * q, 1) for q in range(4)], axis=0)
    free = lax.broadcasted_iota(jnp.int32, (12, 128), 1) >= 96
    for txl in range(2):
        for k in range(4):
            start = 12 + 16 * txl + 4 * k
            for nd in range(4):
                d = txl * 16 + k * 4 + nd
                out[d, 0:12] = jnp.where(free, edge, window[nd, start : start + 12, :])
                out[d, 12:16] = own[...]


def block_kernel(slots, got, out, weight):
    members = out.shape[0]
    r = lax.axis_index("wide") % 8
    n = lax.axis_index("narrow")
    lane = lax.broadcasted_iota(jnp.int32, (3, 128), 1)

    def across(slot):
        edge = jnp.zeros((3, 128), jnp.float32)
        for q in range(4):
            moved = pltpu.roll(slots[slot, 3 * q : 3 * q + 3, :], (32 * q + 32) % 128, 1)
            edge = jnp.where(lane // 32 == q, moved, edge)
        return edge

    zero = jnp.zeros((1, 128), jnp.float32)
    around = []
    for step in (3, 0, 1):
        column = (n + step) % 4
        below = slots[jnp.maximum(r - 1, 0) * 4 + column, 13:16, :]
        above = slots[jnp.minimum(r + 1, 7) * 4 + column, 12:15, :]
        below = jnp.where(r == 0, across(28 + column), below)
        above = jnp.where(r == 7, across(column), above)
        around.append(
            jnp.concatenate([zero, below, slots[r * 4 + column, 12:16, :], above, zero], axis=0)
        )
    set_weights(*around, weight)
    for start in range(0, members, 8):
        field = {r: got[pl.ds(16 * start + r, 8, stride=16), :] for r in range(12)}
        for step in range(ITERS):
            field = {
                r: weight[0, r] * field[r]
                + weight[1, r] * field[r - 1]
                + weight[2, r] * field[r + 1]
                + weight[3, r] * pltpu.roll(field[r], 1, 1)
                + weight[4, r] * pltpu.roll(field[r], 127, 1)
                for r in range(1 + step, 11 - step)
            }
        for i in range(4):
            out[start : start + 8, i, :] = pltpu.roll(field[4 + i], 112, 1)[:, :64]


def per_device(
    noise,
    diagonal_tile_blocks,
    left_factors,
    right_factors,
    ranks,
    owner,
    courant_x,
    courant_number_second,
    upwind_x,
    upwind_y,
):
    wide, narrow = lax.axis_size("wide"), lax.axis_size("narrow")
    group = wide // narrow
    devices = wide * narrow
    plane = lax.axis_index("wide") // group
    rows, cols = ranks.shape
    rank_max = left_factors.shape[2]
    members = noise.shape[1]
    cells = noise.shape[2]
    f32 = jnp.float32

    slabs = [[z * group * narrow + i for i in range(group * narrow)] for z in range(narrow)]

    def server(plane_to, source):
        return source ^ (3, 1, 0, 2)[(plane_to - source) % 4]

    swap = [
        ((s * group + r) * narrow + server(z, s), (z * group + r) * narrow + s)
        for s in range(narrow)
        for r in range(group)
        for z in range(narrow)
    ]
    planes = [[z * group + r for r in range(group)] for z in range(narrow)]

    with jax.named_scope("diagonal_gather"):
        own_diag = diagonal_tile_blocks[0]
        beside, across = [[(i, i ^ j) for i in range(narrow)] for j in (1, 2)]
        opposite = lax.ppermute(own_diag, "narrow", across)
        diags = [
            own_diag,
            lax.ppermute(own_diag, "narrow", beside),
            opposite,
            lax.ppermute(opposite, "narrow", beside),
        ]

    with jax.named_scope("noise_gather"):
        swapped = lax.ppermute(noise, BOTH, swap)

    with jax.named_scope("coefficient_halo"):
        own = jnp.concatenate(
            [
                jnp.where(flag == 1, value, -value)
                for value, flag in ((courant_x, upwind_x), (courant_number_second, upwind_y))
            ],
            axis=1,
        )
        last = group - 1
        forwarded = lax.ppermute(
            own,
            BOTH,
            [
                ((z * group + r) * narrow + b, ((z + step) % narrow * group + r) * narrow + b)
                for z in range(narrow)
                for r, step in ((0, -1), (last, 1))
                for b in range(narrow)
            ],
        )

    with jax.named_scope("noise_gather"):
        sending = jnp.broadcast_to(swapped[None], (group, *swapped.shape))
        columns = lax.all_to_all(
            sending, "wide", 0, 0, axis_index_groups=planes, tiled=True
        ).reshape(cols, members, cells)

    with jax.named_scope("factors"):
        keep = (
            jnp.arange(rank_max, dtype=jnp.int32)[None, None, :] < ranks[:, :, None]
        ).astype(f32).reshape(rows, cols * rank_max)
        partial_sums = pl.pallas_call(
            factor_kernel,
            out_shape=pltpu.VMEM((devices, 8, 128), f32),
            in_specs=specs(SMEM, VMEM, VMEM, *[pltpu.HBM] * 3, *[VMEM] * (narrow - 1)),
            out_specs=pl.BlockSpec(memory_space=VMEM),
            scratch_shapes=[
                pltpu.VMEM((rows, members, cols * rank_max), jnp.bfloat16),
                pltpu.VMEM((members * 8, 128), f32),
                pltpu.VMEM((rows, members, cells), f32),
                pltpu.VMEM(right_factors.shape, right_factors.dtype),
                pltpu.VMEM(left_factors.shape, left_factors.dtype),
                pltpu.VMEM(own_diag.shape, own_diag.dtype),
                pltpu.VMEM(own_diag.shape, own_diag.dtype),
                pltpu.SemaphoreType.DMA((CHUNKS + 2 * rows + 1,)),
            ],
            compiler_params=limit(24),
        )(
            far(owner),
            near(keep),
            near(columns),
            far(right_factors),
            far(left_factors),
            far(diags[0]),
            *[near(d) for d in diags[1:]],
        )

    with jax.named_scope("member_exchange"):
        got = lax.all_to_all(partial_sums, BOTH, 0, 0, tiled=True)

    with jax.named_scope("place"):
        bits = [(owner >> b) & 1 for b in range(7)]
        tile_y = bits[0] | bits[2] << 1 | bits[4] << 2 | bits[6] << 3
        tile_x = bits[1] | bits[3] << 1 | bits[5] << 2
        place = (tile_x * 16 + tile_y - 32 * plane.astype(jnp.int32) + 16) & 127
        blocks = pl.pallas_call(
            place_kernel,
            out_shape=pltpu.VMEM((members, 16, 128), f32),
            in_specs=specs(*[VMEM] * 4),
            out_specs=pl.BlockSpec(memory_space=VMEM),
            scratch_shapes=[pltpu.VMEM((256, 128), f32), pltpu.VMEM((4, 64, 128), f32)],
            compiler_params=limit(4),
        )(near(place[None]), near(got.reshape(wide, narrow, 8, 128)), near(own), near(forwarded))

    with jax.named_scope("block_exchange"):
        mine = lax.all_to_all(blocks, BOTH, 0, 0, axis_index_groups=slabs, tiled=True)

    with jax.named_scope("stencil"):
        return pl.pallas_call(
            block_kernel,
            out_shape=jax.ShapeDtypeStruct((members, 4, 64), f32),
            in_specs=specs(VMEM, VMEM),
            out_specs=pl.BlockSpec(memory_space=VMEM),
            scratch_shapes=[pltpu.VMEM((5, 12, 8, 128), f32)],
            compiler_params=limit(4),
        )(near(mine), near(mine.reshape(members * 16, 128)))


def solution(mesh):
    placed = (
        P("wide", None, None),
        P(("wide", "narrow"), None, None),
        P("wide", "narrow", None, None),
        P("wide", "narrow", None, None),
        P("wide", "narrow"),
        P(),
        P("wide", "narrow"),
        P("wide", "narrow"),
        P("wide", "narrow"),
        P("wide", "narrow"),
    )
    return jax.shard_map(
        per_device, mesh=mesh, in_specs=placed, out_specs=P(None, "wide", "narrow"), check_vma=False
    )
```

```python
import functools

import jax
import jax.numpy as jnp
import numpy as np
from jax import lax
from jax.experimental import pallas as pl
from jax.experimental.pallas import tpu as pltpu
from jax.sharding import PartitionSpec as P

ITERS = 4
MIXING = 0.05
BOTH = ("wide", "narrow")
VMEM = pltpu.VMEM
SMEM = pltpu.SMEM
MIB = 1 << 20
CHUNKS = 8


def specs(*spaces):
    return [pl.BlockSpec(memory_space=space) for space in spaces]


def near(value):
    return pltpu.with_memory_space_constraint(value, VMEM)


def far(value):
    return pltpu.with_memory_space_constraint(value, pltpu.HBM)


def limit(mib):
    return pltpu.CompilerParams(vmem_limit_bytes=mib * MIB)


def halves(count):
    return slice(0, count // 2), slice(count // 2, count)


def factor_kernel(
    owner,
    keep,
    noise,
    right_far,
    left_far,
    diag_far,
    d1,
    d2,
    d3,
    out,
    coeff,
    turned,
    own,
    right,
    left,
    d0,
    kept,
    done,
):
    rows, cols, rank_max, cells = right.shape
    members = noise.shape[1]
    each = cols // CHUNKS
    chunks = [slice(i * each, (i + 1) * each) for i in range(CHUNKS)]
    pairs = [(right_far.at[:, span], right.at[:, span]) for span in chunks]
    pairs += [(left_far.at[p, span], left.at[p, span]) for p in range(rows) for span in halves(cols)]
    pairs += [(diag_far, d0)]
    copies = [
        pltpu.make_async_copy(source, target, done.at[i])
        for i, (source, target) in enumerate(pairs)
    ]
    copies[-1].start()
    for copy in copies[:CHUNKS]:
        copy.start()
    copies[-1].wait()

    def arrived(i):
        copies[i].wait()
        if i + CHUNKS < len(copies) - 1:
            copies[i + CHUNKS].start()

    w, n = lax.axis_index("wide"), lax.axis_index("narrow")
    lower = lax.broadcasted_iota(jnp.int32, (cells, cells), 0) >= lax.broadcasted_iota(
        jnp.int32, (cells, cells), 1
    )
    for j, diag in enumerate((d0, d1, d2, d3)):
        row = n ^ j
        local = owner[rows * w + row] - cols * n
        held = jnp.logical_and(local >= 0, local < cols)
        kept[...] = jnp.where(lower, diag[...].astype(jnp.float32), 0.0).astype(jnp.bfloat16)
        term = lax.dot_general(
            noise[jnp.clip(local, 0, cols - 1)],
            kept[...],
            (((1,), (1,)), ((), ())),
            preferred_element_type=jnp.float32,
        )
        own[row] = jnp.where(held, term, 0.0)
    for c in range(cols):
        if c % each == 0:
            arrived(c // each)
        span = slice(c * rank_max, (c + 1) * rank_max)
        block = right[:, c].reshape(rows * rank_max, cells)
        product = lax.dot_general(
            noise[c], block, (((1,), (1,)), ((), ())), preferred_element_type=jnp.float32
        )
        for p in range(rows):
            part = product[:, p * rank_max : (p + 1) * rank_max]
            part = jnp.where(keep[p : p + 1, span] > 0, part, 0.0)
            coeff[p, :, span] = part.astype(jnp.bfloat16)
    for p in range(rows):
        total = own[p]
        for i, span in enumerate(halves(cols)):
            arrived(CHUNKS + 2 * p + i)
            total = total + jnp.dot(
                coeff[p, :, rank_max * span.start : rank_max * span.stop],
                left[p, span].reshape(cols // 2 * rank_max, cells),
                preferred_element_type=jnp.float32,
            )
        for g in range(members // 8):
            for h in range(2):
                turned[pl.ds(64 * g + 2 * p + h, 8, stride=8), :] = total[
                    8 * g : 8 * g + 8, 128 * h : 128 * h + 128
                ]
    for d in range(out.shape[0]):
        member = d % members
        out[d] = turned[8 * member : 8 * member + 8, :]


def set_weights(low, own, high, weight):
    lane = lax.broadcasted_iota(jnp.int32, low.shape, 1)
    cx, cy = [
        jnp.where(
            lane < 16,
            pltpu.roll(low, edge, 1),
            jnp.where(lane < 80, pltpu.roll(own, middle, 1), pltpu.roll(high, edge, 1)),
        )
        for edge, middle in ((80, 16), (16, 80))
    ]
    weights = (
        1.0 - jnp.abs(cx) - jnp.abs(cy) - 4.0 * MIXING,
        MIXING + jnp.maximum(cx, 0.0),
        MIXING + jnp.maximum(-cx, 0.0),
        MIXING + jnp.maximum(cy, 0.0),
        MIXING + jnp.maximum(-cy, 0.0),
    )
    for i, value in enumerate(weights):
        for row in range(1, 11):
            weight[i, row] = jnp.broadcast_to(value[row : row + 1], (8, 128))


def place_kernel(place, got, own, forwarded, out, summed, window):
    total = got[:, 0] + got[:, 1] + got[:, 2] + got[:, 3]
    summed[...] = total.reshape(256, 128)
    target = lax.broadcasted_iota(jnp.int32, (64, 128), 0)
    one_hot = jnp.where(target == place[...], 1.0, 0.0).astype(jnp.bfloat16)
    one_hot = jnp.concatenate([one_hot] * 3, axis=1)
    fields = []
    for h in range(2):
        rest = summed[pl.ds(h, 128, stride=2), :]
        parts = []
        for _ in range(3):
            part = rest.astype(jnp.bfloat16)
            parts.append(part)
            rest = rest - part.astype(jnp.float32)
        fields.append(
            jnp.dot(
                one_hot, jnp.concatenate(parts, axis=0), preferred_element_type=jnp.float32
            ).reshape(4, 16, 128)
        )
    shape = (8, 8, 128)
    sub = lax.broadcasted_iota(jnp.int32, shape, 1)
    group = lax.broadcasted_iota(jnp.int32, shape, 2) // 16
    sides = []
    for h in range(2):
        x = jnp.concatenate([f[:, 8 * h : 8 * h + 8] for f in fields], axis=1).reshape(shape)
        for bit in (1, 2, 4):
            in_sub, in_group = (sub & bit) != 0, (group & bit) != 0
            later = pltpu.roll(pltpu.roll(x, 8 - bit, 1), 16 * bit, 2)
            earlier = pltpu.roll(pltpu.roll(x, bit, 1), 128 - 16 * bit, 2)
            x = jnp.where(in_sub == in_group, x, jnp.where(in_group, later, earlier))
        sides.append(x.reshape(64, 128))
    lane = lax.broadcasted_iota(jnp.int32, (64, 128), 1)
    for nd in range(4):
        shift = 80 if nd % 2 else 16
        first, second = (sides[1], sides[0]) if nd in (0, 3) else (sides[0], sides[1])
        window[nd] = jnp.where(
            lane < shift, pltpu.roll(first, shift, 1), pltpu.roll(second, shift, 1)
        )
    first = lax.axis_index("wide") % 8 == 0
    edge = jnp.where(first, forwarded[0:3], forwarded[1:4])
    edge = jnp.concatenate([pltpu.roll(edge, 96 - 32 * q, 1) for q in range(4)], axis=0)
    free = lax.broadcasted_iota(jnp.int32, (12, 128), 1) >= 96
    for txl in range(2):
        for k in range(4):
            start = 12 + 16 * txl + 4 * k
            for nd in range(4):
                d = txl * 16 + k * 4 + nd
                out[d, 0:12] = jnp.where(free, edge, window[nd, start : start + 12, :])
                out[d, 12:16] = own[...]


def block_kernel(slots, got, out, weight):
    members = out.shape[0]
    r = lax.axis_index("wide") % 8
    n = lax.axis_index("narrow")
    lane = lax.broadcasted_iota(jnp.int32, (3, 128), 1)

    def across(slot):
        edge = jnp.zeros((3, 128), jnp.float32)
        for q in range(4):
            moved = pltpu.roll(slots[slot, 3 * q : 3 * q + 3, :], (32 * q + 32) % 128, 1)
            edge = jnp.where(lane // 32 == q, moved, edge)
        return edge

    zero = jnp.zeros((1, 128), jnp.float32)
    around = []
    for step in (3, 0, 1):
        column = (n + step) % 4
        below = slots[jnp.maximum(r - 1, 0) * 4 + column, 13:16, :]
        above = slots[jnp.minimum(r + 1, 7) * 4 + column, 12:15, :]
        below = jnp.where(r == 0, across(28 + column), below)
        above = jnp.where(r == 7, across(column), above)
        around.append(
            jnp.concatenate([zero, below, slots[r * 4 + column, 12:16, :], above, zero], axis=0)
        )
    set_weights(*around, weight)
    for start in range(0, members, 8):
        field = {r: got[pl.ds(16 * start + r, 8, stride=16), :] for r in range(12)}
        for step in range(ITERS):
            field = {
                r: weight[0, r] * field[r]
                + weight[1, r] * field[r - 1]
                + weight[2, r] * field[r + 1]
                + weight[3, r] * pltpu.roll(field[r], 1, 1)
                + weight[4, r] * pltpu.roll(field[r], 127, 1)
                for r in range(1 + step, 11 - step)
            }
        for i in range(4):
            out[start : start + 8, i, :] = pltpu.roll(field[4 + i], 112, 1)[:, :64]


def per_device(
    noise,
    diagonal_tile_blocks,
    left_factors,
    right_factors,
    ranks,
    owner,
    courant_x,
    courant_number_second,
    upwind_x,
    upwind_y,
):
    wide, narrow = lax.axis_size("wide"), lax.axis_size("narrow")
    group = wide // narrow
    devices = wide * narrow
    plane = lax.axis_index("wide") // group
    rows, cols = ranks.shape
    rank_max = left_factors.shape[2]
    members = noise.shape[1]
    cells = noise.shape[2]
    f32 = jnp.float32

    slabs = [[z * group * narrow + i for i in range(group * narrow)] for z in range(narrow)]

    def server(plane_to, source):
        return source ^ (3, 1, 0, 2)[(plane_to - source) % 4]

    swaps = [
        [
            ((s * group + r) * narrow + server(z, s), (z * group + (r ^ flip)) * narrow + s)
            for s in range(narrow)
            for r in range(group)
            for z in range(narrow)
        ]
        for flip in (0, 1)
    ]
    lines = [[z * group + 2 * y + x for y in range(group // 2)] for z in range(narrow) for x in (0, 1)]

    with jax.named_scope("diagonal_gather"):
        own_diag = diagonal_tile_blocks[0]
        beside, across = [[(i, i ^ j) for i in range(narrow)] for j in (1, 2)]
        opposite = lax.ppermute(own_diag, "narrow", across)
        diags = [
            own_diag,
            lax.ppermute(own_diag, "narrow", beside),
            opposite,
            lax.ppermute(opposite, "narrow", beside),
        ]

    with jax.named_scope("noise_gather"):
        swapped, partner = [lax.ppermute(noise, BOTH, swap) for swap in swaps]

    with jax.named_scope("coefficient_halo"):
        own = jnp.concatenate(
            [
                jnp.where(flag == 1, value, -value)
                for value, flag in ((courant_x, upwind_x), (courant_number_second, upwind_y))
            ],
            axis=1,
        )
        last = group - 1
        forwarded = lax.ppermute(
            own,
            BOTH,
            [
                ((z * group + r) * narrow + b, ((z + step) % narrow * group + r) * narrow + b)
                for z in range(narrow)
                for r, step in ((0, -1), (last, 1))
                for b in range(narrow)
            ],
        )

    with jax.named_scope("noise_gather"):
        odd = lax.axis_index("wide") % 2 == 1
        both = jnp.stack(
            [jnp.where(odd, partner, swapped), jnp.where(odd, swapped, partner)]
        )
        sending = jnp.broadcast_to(both[None], (group // 2, *both.shape))
        columns = lax.all_to_all(
            sending, "wide", 0, 0, axis_index_groups=lines, tiled=True
        ).reshape(cols, members, cells)

    with jax.named_scope("factors"):
        keep = (
            jnp.arange(rank_max, dtype=jnp.int32)[None, None, :] < ranks[:, :, None]
        ).astype(f32).reshape(rows, cols * rank_max)
        partial_sums = pl.pallas_call(
            factor_kernel,
            out_shape=pltpu.VMEM((devices, 8, 128), f32),
            in_specs=specs(SMEM, VMEM, VMEM, *[pltpu.HBM] * 3, *[VMEM] * (narrow - 1)),
            out_specs=pl.BlockSpec(memory_space=VMEM),
            scratch_shapes=[
                pltpu.VMEM((rows, members, cols * rank_max), jnp.bfloat16),
                pltpu.VMEM((members * 8, 128), f32),
                pltpu.VMEM((rows, members, cells), f32),
                pltpu.VMEM(right_factors.shape, right_factors.dtype),
                pltpu.VMEM(left_factors.shape, left_factors.dtype),
                pltpu.VMEM(own_diag.shape, own_diag.dtype),
                pltpu.VMEM(own_diag.shape, own_diag.dtype),
                pltpu.SemaphoreType.DMA((CHUNKS + 2 * rows + 1,)),
            ],
            compiler_params=limit(24),
        )(
            far(owner),
            near(keep),
            near(columns),
            far(right_factors),
            far(left_factors),
            far(diags[0]),
            *[near(d) for d in diags[1:]],
        )

    with jax.named_scope("member_exchange"):
        got = lax.all_to_all(partial_sums, BOTH, 0, 0, tiled=True)

    with jax.named_scope("place"):
        bits = [(owner >> b) & 1 for b in range(7)]
        tile_y = bits[0] | bits[2] << 1 | bits[4] << 2 | bits[6] << 3
        tile_x = bits[1] | bits[3] << 1 | bits[5] << 2
        place = (tile_x * 16 + tile_y - 32 * plane.astype(jnp.int32) + 16) & 127
        blocks = pl.pallas_call(
            place_kernel,
            out_shape=pltpu.VMEM((members, 16, 128), f32),
            in_specs=specs(*[VMEM] * 4),
            out_specs=pl.BlockSpec(memory_space=VMEM),
            scratch_shapes=[pltpu.VMEM((256, 128), f32), pltpu.VMEM((4, 64, 128), f32)],
            compiler_params=limit(4),
        )(near(place[None]), near(got.reshape(wide, narrow, 8, 128)), near(own), near(forwarded))

    with jax.named_scope("block_exchange"):
        mine = lax.all_to_all(blocks, BOTH, 0, 0, axis_index_groups=slabs, tiled=True)

    with jax.named_scope("stencil"):
        return pl.pallas_call(
            block_kernel,
            out_shape=jax.ShapeDtypeStruct((members, 4, 64), f32),
            in_specs=specs(VMEM, VMEM),
            out_specs=pl.BlockSpec(memory_space=VMEM),
            scratch_shapes=[pltpu.VMEM((5, 12, 8, 128), f32)],
            compiler_params=limit(4),
        )(near(mine), near(mine.reshape(members * 16, 128)))


def solution(mesh):
    placed = (
        P("wide", None, None),
        P(("wide", "narrow"), None, None),
        P("wide", "narrow", None, None),
        P("wide", "narrow", None, None),
        P("wide", "narrow"),
        P(),
        P("wide", "narrow"),
        P("wide", "narrow"),
        P("wide", "narrow"),
        P("wide", "narrow"),
    )
    return jax.shard_map(
        per_device, mesh=mesh, in_specs=placed, out_specs=P(None, "wide", "narrow"), check_vma=False
    )
```

```python
import functools

import jax
import jax.numpy as jnp
import numpy as np
from jax import lax
from jax.experimental import pallas as pl
from jax.experimental.pallas import tpu as pltpu
from jax.sharding import PartitionSpec as P

ITERS = 4
MIXING = 0.05
BOTH = ("wide", "narrow")
VMEM = pltpu.VMEM
SMEM = pltpu.SMEM
MIB = 1 << 20
CHUNKS = 8
EARLY = 8


def specs(*spaces):
    return [pl.BlockSpec(memory_space=space) for space in spaces]


def near(value):
    return pltpu.with_memory_space_constraint(value, VMEM)


def far(value):
    return pltpu.with_memory_space_constraint(value, pltpu.HBM)


def limit(mib):
    return pltpu.CompilerParams(vmem_limit_bytes=mib * MIB)


def halves(count):
    return slice(0, count // 2), slice(count // 2, count)


def fetch_kernel(right_far, diag_far, right, diag, done):
    rows, count = right.shape[:2]
    copies = [
        pltpu.make_async_copy(right_far.at[p, 0:count], right.at[p], done.at[p]) for p in range(rows)
    ]
    copies.append(pltpu.make_async_copy(diag_far, diag, done.at[rows]))
    for copy in copies:
        copy.start()
    for copy in copies:
        copy.wait()


def factor_kernel(
    owner,
    keep,
    noise,
    early,
    d0,
    right_far,
    left_far,
    d1,
    d2,
    d3,
    out,
    coeff,
    turned,
    own,
    right,
    left,
    kept,
    done,
):
    rows, cols, rank_max, cells = left.shape
    members = noise.shape[1]
    each = cols // CHUNKS
    ahead = EARLY // each
    chunks = [slice(i * each, (i + 1) * each) for i in range(ahead, CHUNKS)]
    pairs = [
        (right_far.at[:, span], right.at[:, span.start - EARLY : span.stop - EARLY])
        for span in chunks
    ]
    pairs += [(left_far.at[p, span], left.at[p, span]) for p in range(rows) for span in halves(cols)]
    copies = [
        pltpu.make_async_copy(source, target, done.at[i])
        for i, (source, target) in enumerate(pairs)
    ]
    for copy in copies[:CHUNKS]:
        copy.start()

    def arrived(i):
        copies[i].wait()
        if i + CHUNKS < len(copies):
            copies[i + CHUNKS].start()

    w, n = lax.axis_index("wide"), lax.axis_index("narrow")
    lower = lax.broadcasted_iota(jnp.int32, (cells, cells), 0) >= lax.broadcasted_iota(
        jnp.int32, (cells, cells), 1
    )
    for j, diag in enumerate((d0, d1, d2, d3)):
        row = n ^ j
        local = owner[rows * w + row] - cols * n
        held = jnp.logical_and(local >= 0, local < cols)
        kept[...] = jnp.where(lower, diag[...].astype(jnp.float32), 0.0).astype(jnp.bfloat16)
        term = lax.dot_general(
            noise[jnp.clip(local, 0, cols - 1)],
            kept[...],
            (((1,), (1,)), ((), ())),
            preferred_element_type=jnp.float32,
        )
        own[row] = jnp.where(held, term, 0.0)
    for c in range(cols):
        if c >= EARLY and c % each == 0:
            arrived(c // each - ahead)
        span = slice(c * rank_max, (c + 1) * rank_max)
        block = (early[:, c] if c < EARLY else right[:, c - EARLY]).reshape(rows * rank_max, cells)
        product = lax.dot_general(
            noise[c], block, (((1,), (1,)), ((), ())), preferred_element_type=jnp.float32
        )
        for p in range(rows):
            part = product[:, p * rank_max : (p + 1) * rank_max]
            part = jnp.where(keep[p : p + 1, span] > 0, part, 0.0)
            coeff[p, :, span] = part.astype(jnp.bfloat16)
    for p in range(rows):
        total = own[p]
        for i, span in enumerate(halves(cols)):
            arrived(len(chunks) + 2 * p + i)
            total = total + jnp.dot(
                coeff[p, :, rank_max * span.start : rank_max * span.stop],
                left[p, span].reshape(cols // 2 * rank_max, cells),
                preferred_element_type=jnp.float32,
            )
        for g in range(members // 8):
            for h in range(2):
                turned[pl.ds(64 * g + 2 * p + h, 8, stride=8), :] = total[
                    8 * g : 8 * g + 8, 128 * h : 128 * h + 128
                ]
    for d in range(out.shape[0]):
        member = d % members
        out[d] = turned[8 * member : 8 * member + 8, :]


def set_weights(low, own, high, weight):
    lane = lax.broadcasted_iota(jnp.int32, low.shape, 1)
    cx, cy = [
        jnp.where(
            lane < 16,
            pltpu.roll(low, edge, 1),
            jnp.where(lane < 80, pltpu.roll(own, middle, 1), pltpu.roll(high, edge, 1)),
        )
        for edge, middle in ((80, 16), (16, 80))
    ]
    weights = (
        1.0 - jnp.abs(cx) - jnp.abs(cy) - 4.0 * MIXING,
        MIXING + jnp.maximum(cx, 0.0),
        MIXING + jnp.maximum(-cx, 0.0),
        MIXING + jnp.maximum(cy, 0.0),
        MIXING + jnp.maximum(-cy, 0.0),
    )
    for i, value in enumerate(weights):
        for row in range(1, 11):
            weight[i, row] = jnp.broadcast_to(value[row : row + 1], (8, 128))


def place_kernel(place, got, own, forwarded, out, summed, window):
    total = got[:, 0] + got[:, 1] + got[:, 2] + got[:, 3]
    summed[...] = total.reshape(256, 128)
    target = lax.broadcasted_iota(jnp.int32, (64, 128), 0)
    one_hot = jnp.where(target == place[...], 1.0, 0.0).astype(jnp.bfloat16)
    one_hot = jnp.concatenate([one_hot] * 3, axis=1)
    fields = []
    for h in range(2):
        rest = summed[pl.ds(h, 128, stride=2), :]
        parts = []
        for _ in range(3):
            part = rest.astype(jnp.bfloat16)
            parts.append(part)
            rest = rest - part.astype(jnp.float32)
        fields.append(
            jnp.dot(
                one_hot, jnp.concatenate(parts, axis=0), preferred_element_type=jnp.float32
            ).reshape(4, 16, 128)
        )
    shape = (8, 8, 128)
    sub = lax.broadcasted_iota(jnp.int32, shape, 1)
    group = lax.broadcasted_iota(jnp.int32, shape, 2) // 16
    sides = []
    for h in range(2):
        x = jnp.concatenate([f[:, 8 * h : 8 * h + 8] for f in fields], axis=1).reshape(shape)
        for bit in (1, 2, 4):
            in_sub, in_group = (sub & bit) != 0, (group & bit) != 0
            later = pltpu.roll(pltpu.roll(x, 8 - bit, 1), 16 * bit, 2)
            earlier = pltpu.roll(pltpu.roll(x, bit, 1), 128 - 16 * bit, 2)
            x = jnp.where(in_sub == in_group, x, jnp.where(in_group, later, earlier))
        sides.append(x.reshape(64, 128))
    lane = lax.broadcasted_iota(jnp.int32, (64, 128), 1)
    for nd in range(4):
        shift = 80 if nd % 2 else 16
        first, second = (sides[1], sides[0]) if nd in (0, 3) else (sides[0], sides[1])
        window[nd] = jnp.where(
            lane < shift, pltpu.roll(first, shift, 1), pltpu.roll(second, shift, 1)
        )
    first = lax.axis_index("wide") % 8 == 0
    edge = jnp.where(first, forwarded[0:3], forwarded[1:4])
    edge = jnp.concatenate([pltpu.roll(edge, 96 - 32 * q, 1) for q in range(4)], axis=0)
    free = lax.broadcasted_iota(jnp.int32, (12, 128), 1) >= 96
    for txl in range(2):
        for k in range(4):
            start = 12 + 16 * txl + 4 * k
            for nd in range(4):
                d = txl * 16 + k * 4 + nd
                out[d, 0:12] = jnp.where(free, edge, window[nd, start : start + 12, :])
                out[d, 12:16] = own[...]


def block_kernel(slots, got, out, weight):
    members = out.shape[0]
    r = lax.axis_index("wide") % 8
    n = lax.axis_index("narrow")
    lane = lax.broadcasted_iota(jnp.int32, (3, 128), 1)

    def across(slot):
        edge = jnp.zeros((3, 128), jnp.float32)
        for q in range(4):
            moved = pltpu.roll(slots[slot, 3 * q : 3 * q + 3, :], (32 * q + 32) % 128, 1)
            edge = jnp.where(lane // 32 == q, moved, edge)
        return edge

    zero = jnp.zeros((1, 128), jnp.float32)
    around = []
    for step in (3, 0, 1):
        column = (n + step) % 4
        below = slots[jnp.maximum(r - 1, 0) * 4 + column, 13:16, :]
        above = slots[jnp.minimum(r + 1, 7) * 4 + column, 12:15, :]
        below = jnp.where(r == 0, across(28 + column), below)
        above = jnp.where(r == 7, across(column), above)
        around.append(
            jnp.concatenate([zero, below, slots[r * 4 + column, 12:16, :], above, zero], axis=0)
        )
    set_weights(*around, weight)
    for start in range(0, members, 8):
        field = {r: got[pl.ds(16 * start + r, 8, stride=16), :] for r in range(12)}
        for step in range(ITERS):
            field = {
                r: weight[0, r] * field[r]
                + weight[1, r] * field[r - 1]
                + weight[2, r] * field[r + 1]
                + weight[3, r] * pltpu.roll(field[r], 1, 1)
                + weight[4, r] * pltpu.roll(field[r], 127, 1)
                for r in range(1 + step, 11 - step)
            }
        for i in range(4):
            out[start : start + 8, i, :] = pltpu.roll(field[4 + i], 112, 1)[:, :64]


def per_device(
    noise,
    diagonal_tile_blocks,
    left_factors,
    right_factors,
    ranks,
    owner,
    courant_x,
    courant_number_second,
    upwind_x,
    upwind_y,
):
    wide, narrow = lax.axis_size("wide"), lax.axis_size("narrow")
    group = wide // narrow
    devices = wide * narrow
    plane = lax.axis_index("wide") // group
    rows, cols = ranks.shape
    rank_max = left_factors.shape[2]
    members = noise.shape[1]
    cells = noise.shape[2]
    f32 = jnp.float32

    slabs = [[z * group * narrow + i for i in range(group * narrow)] for z in range(narrow)]

    def server(plane_to, source):
        return source ^ (3, 1, 0, 2)[(plane_to - source) % 4]

    swaps = [
        [
            ((s * group + r) * narrow + server(z, s), (z * group + (r ^ flip)) * narrow + s)
            for s in range(narrow)
            for r in range(group)
            for z in range(narrow)
        ]
        for flip in (0, 1)
    ]
    lines = [[z * group + 2 * y + x for y in range(group // 2)] for z in range(narrow) for x in (0, 1)]

    with jax.named_scope("diagonal_gather"):
        own_diag = diagonal_tile_blocks[0]
        beside, across = [[(i, i ^ j) for i in range(narrow)] for j in (1, 2)]
        opposite = lax.ppermute(own_diag, "narrow", across)
        diags = [
            own_diag,
            lax.ppermute(own_diag, "narrow", beside),
            opposite,
            lax.ppermute(opposite, "narrow", beside),
        ]

    with jax.named_scope("noise_gather"):
        swapped, partner = [lax.ppermute(noise, BOTH, swap) for swap in swaps]

    with jax.named_scope("coefficient_halo"):
        own = jnp.concatenate(
            [
                jnp.where(flag == 1, value, -value)
                for value, flag in ((courant_x, upwind_x), (courant_number_second, upwind_y))
            ],
            axis=1,
        )
        last = group - 1
        forwarded = lax.ppermute(
            own,
            BOTH,
            [
                ((z * group + r) * narrow + b, ((z + step) % narrow * group + r) * narrow + b)
                for z in range(narrow)
                for r, step in ((0, -1), (last, 1))
                for b in range(narrow)
            ],
        )

    with jax.named_scope("noise_gather"):
        odd = lax.axis_index("wide") % 2 == 1
        both = jnp.stack(
            [jnp.where(odd, partner, swapped), jnp.where(odd, swapped, partner)]
        )
        sending = jnp.broadcast_to(both[None], (group // 2, *both.shape))
        sending, right_factors, own_diag = lax.optimization_barrier(
            (sending, right_factors, own_diag)
        )
        early, first_diag = pl.pallas_call(
            fetch_kernel,
            out_shape=[
                pltpu.VMEM((rows, EARLY, rank_max, cells), right_factors.dtype),
                pltpu.VMEM(own_diag.shape, own_diag.dtype),
            ],
            in_specs=specs(pltpu.HBM, pltpu.HBM),
            out_specs=specs(VMEM, VMEM),
            scratch_shapes=[pltpu.SemaphoreType.DMA((rows + 1,))],
            compiler_params=limit(1),
            cost_estimate=pl.CostEstimate(
                flops=0, transcendentals=0, bytes_accessed=rows * EARLY * rank_max * cells * 4
            ),
        )(far(right_factors), far(own_diag))
        columns = lax.all_to_all(
            sending, "wide", 0, 0, axis_index_groups=lines, tiled=True
        ).reshape(cols, members, cells)

    with jax.named_scope("factors"):
        keep = (
            jnp.arange(rank_max, dtype=jnp.int32)[None, None, :] < ranks[:, :, None]
        ).astype(f32).reshape(rows, cols * rank_max)
        partial_sums = pl.pallas_call(
            factor_kernel,
            out_shape=pltpu.VMEM((devices, 8, 128), f32),
            in_specs=specs(SMEM, *[VMEM] * 4, *[pltpu.HBM] * 2, *[VMEM] * (narrow - 1)),
            out_specs=pl.BlockSpec(memory_space=VMEM),
            scratch_shapes=[
                pltpu.VMEM((rows, members, cols * rank_max), jnp.bfloat16),
                pltpu.VMEM((members * 8, 128), f32),
                pltpu.VMEM((rows, members, cells), f32),
                pltpu.VMEM((rows, cols - EARLY, rank_max, cells), right_factors.dtype),
                pltpu.VMEM(left_factors.shape, left_factors.dtype),
                pltpu.VMEM(own_diag.shape, own_diag.dtype),
                pltpu.SemaphoreType.DMA((CHUNKS + 2 * rows,)),
            ],
            compiler_params=limit(24),
        )(
            far(owner),
            near(keep),
            near(columns),
            early,
            first_diag,
            far(right_factors),
            far(left_factors),
            *[near(d) for d in diags[1:]],
        )

    with jax.named_scope("member_exchange"):
        got = lax.all_to_all(partial_sums, BOTH, 0, 0, tiled=True)

    with jax.named_scope("place"):
        bits = [(owner >> b) & 1 for b in range(7)]
        tile_y = bits[0] | bits[2] << 1 | bits[4] << 2 | bits[6] << 3
        tile_x = bits[1] | bits[3] << 1 | bits[5] << 2
        place = (tile_x * 16 + tile_y - 32 * plane.astype(jnp.int32) + 16) & 127
        blocks = pl.pallas_call(
            place_kernel,
            out_shape=pltpu.VMEM((members, 16, 128), f32),
            in_specs=specs(*[VMEM] * 4),
            out_specs=pl.BlockSpec(memory_space=VMEM),
            scratch_shapes=[pltpu.VMEM((256, 128), f32), pltpu.VMEM((4, 64, 128), f32)],
            compiler_params=limit(4),
        )(near(place[None]), near(got.reshape(wide, narrow, 8, 128)), near(own), near(forwarded))

    with jax.named_scope("block_exchange"):
        mine = lax.all_to_all(blocks, BOTH, 0, 0, axis_index_groups=slabs, tiled=True)

    with jax.named_scope("stencil"):
        return pl.pallas_call(
            block_kernel,
            out_shape=jax.ShapeDtypeStruct((members, 4, 64), f32),
            in_specs=specs(VMEM, VMEM),
            out_specs=pl.BlockSpec(memory_space=VMEM),
            scratch_shapes=[pltpu.VMEM((5, 12, 8, 128), f32)],
            compiler_params=limit(4),
        )(near(mine), near(mine.reshape(members * 16, 128)))


def solution(mesh):
    placed = (
        P("wide", None, None),
        P(("wide", "narrow"), None, None),
        P("wide", "narrow", None, None),
        P("wide", "narrow", None, None),
        P("wide", "narrow"),
        P(),
        P("wide", "narrow"),
        P("wide", "narrow"),
        P("wide", "narrow"),
        P("wide", "narrow"),
    )
    return jax.shard_map(
        per_device, mesh=mesh, in_specs=placed, out_specs=P(None, "wide", "narrow"), check_vma=False
    )
```

```python
import functools

import jax
import jax.numpy as jnp
import numpy as np
from jax import lax
from jax.experimental import pallas as pl
from jax.experimental.pallas import tpu as pltpu
from jax.sharding import PartitionSpec as P

ITERS = 4
MIXING = 0.05
BOTH = ("wide", "narrow")
VMEM = pltpu.VMEM
SMEM = pltpu.SMEM
MIB = 1 << 20
CHUNKS = 8
EARLY = 8


def specs(*spaces):
    return [pl.BlockSpec(memory_space=space) for space in spaces]


def near(value):
    return pltpu.with_memory_space_constraint(value, VMEM)


def far(value):
    return pltpu.with_memory_space_constraint(value, pltpu.HBM)


def limit(mib):
    return pltpu.CompilerParams(vmem_limit_bytes=mib * MIB)


def halves(count):
    return slice(0, count // 2), slice(count // 2, count)


def fetch_kernel(right_far, diag_far, right, diag, done):
    rows, count = right.shape[:2]
    copies = [
        pltpu.make_async_copy(right_far.at[p, 0:count], right.at[p], done.at[p]) for p in range(rows)
    ]
    copies.append(pltpu.make_async_copy(diag_far, diag, done.at[rows]))
    for copy in copies:
        copy.start()
    for copy in copies:
        copy.wait()


def factor_kernel(
    owner,
    keep,
    noise,
    early,
    d0,
    right_far,
    left_far,
    d1,
    d2,
    d3,
    out,
    coeff,
    turned,
    own,
    right,
    left,
    kept,
    done,
    sent,
):
    rows, cols, rank_max, cells = left.shape
    members = noise.shape[1]
    each = cols // CHUNKS
    ahead = EARLY // each
    chunks = [slice(i * each, (i + 1) * each) for i in range(ahead, CHUNKS)]
    pairs = [
        (right_far.at[:, span], right.at[:, span.start - EARLY : span.stop - EARLY])
        for span in chunks
    ]
    pairs += [(left_far.at[p, span], left.at[p, span]) for p in range(rows) for span in halves(cols)]
    copies = [
        pltpu.make_async_copy(source, target, done.at[i])
        for i, (source, target) in enumerate(pairs)
    ]
    for copy in copies[:CHUNKS]:
        copy.start()

    def arrived(i):
        copies[i].wait()
        if i + CHUNKS < len(copies):
            copies[i + CHUNKS].start()

    w, n = lax.axis_index("wide"), lax.axis_index("narrow")
    lower = lax.broadcasted_iota(jnp.int32, (cells, cells), 0) >= lax.broadcasted_iota(
        jnp.int32, (cells, cells), 1
    )
    for j, diag in enumerate((d0, d1, d2, d3)):
        row = n ^ j
        local = owner[rows * w + row] - cols * n
        held = jnp.logical_and(local >= 0, local < cols)
        kept[j] = jnp.where(lower, diag[...].astype(jnp.float32), 0.0).astype(jnp.bfloat16)
        term = lax.dot_general(
            noise[jnp.clip(local, 0, cols - 1)],
            kept[j],
            (((1,), (1,)), ((), ())),
            preferred_element_type=jnp.float32,
        )
        own[row] = jnp.where(held, term, 0.0)
    for c in range(cols):
        if c >= EARLY and c % each == 0:
            arrived(c // each - ahead)
        span = slice(c * rank_max, (c + 1) * rank_max)
        block = (early[:, c] if c < EARLY else right[:, c - EARLY]).reshape(rows * rank_max, cells)
        product = lax.dot_general(
            noise[c], block, (((1,), (1,)), ((), ())), preferred_element_type=jnp.float32
        )
        for p in range(rows):
            part = product[:, p * rank_max : (p + 1) * rank_max]
            part = jnp.where(keep[p : p + 1, span] > 0, part, 0.0)
            coeff[p, :, span] = part.astype(jnp.bfloat16)
    for p in range(rows):
        total = own[p]
        for i, span in enumerate(halves(cols)):
            arrived(len(chunks) + 2 * p + i)
            total = total + jnp.dot(
                coeff[p, :, rank_max * span.start : rank_max * span.stop],
                left[p, span].reshape(cols // 2 * rank_max, cells),
                preferred_element_type=jnp.float32,
            )
        for g in range(members // 8):
            for h in range(2):
                turned[pl.ds(64 * g + 2 * p + h, 8, stride=8), :] = total[
                    8 * g : 8 * g + 8, 128 * h : 128 * h + 128
                ]
    sends = [
        pltpu.make_async_copy(turned, out.at[i], sent.at[i]) for i in range(out.shape[0])
    ]
    for send in sends:
        send.start()
    for send in sends:
        send.wait()


def set_weights(low, own, high, weight):
    lane = lax.broadcasted_iota(jnp.int32, low.shape, 1)
    cx, cy = [
        jnp.where(
            lane < 16,
            pltpu.roll(low, edge, 1),
            jnp.where(lane < 80, pltpu.roll(own, middle, 1), pltpu.roll(high, edge, 1)),
        )
        for edge, middle in ((80, 16), (16, 80))
    ]
    weights = (
        1.0 - jnp.abs(cx) - jnp.abs(cy) - 4.0 * MIXING,
        MIXING + jnp.maximum(cx, 0.0),
        MIXING + jnp.maximum(-cx, 0.0),
        MIXING + jnp.maximum(cy, 0.0),
        MIXING + jnp.maximum(-cy, 0.0),
    )
    for i, value in enumerate(weights):
        for row in range(1, 11):
            weight[i, row] = jnp.broadcast_to(value[row : row + 1], (8, 128))


def place_kernel(place, got, own, forwarded, out, summed, window):
    total = got[:, 0] + got[:, 1] + got[:, 2] + got[:, 3]
    summed[...] = total.reshape(256, 128)
    target = lax.broadcasted_iota(jnp.int32, (64, 128), 0)
    one_hot = jnp.where(target == place[...], 1.0, 0.0).astype(jnp.bfloat16)
    one_hot = jnp.concatenate([one_hot] * 3, axis=1)
    fields = []
    for h in range(2):
        rest = summed[pl.ds(h, 128, stride=2), :]
        parts = []
        for _ in range(3):
            part = rest.astype(jnp.bfloat16)
            parts.append(part)
            rest = rest - part.astype(jnp.float32)
        fields.append(
            jnp.dot(
                one_hot, jnp.concatenate(parts, axis=0), preferred_element_type=jnp.float32
            ).reshape(4, 16, 128)
        )
    shape = (8, 8, 128)
    sub = lax.broadcasted_iota(jnp.int32, shape, 1)
    group = lax.broadcasted_iota(jnp.int32, shape, 2) // 16
    sides = []
    for h in range(2):
        x = jnp.concatenate([f[:, 8 * h : 8 * h + 8] for f in fields], axis=1).reshape(shape)
        for bit in (1, 2, 4):
            in_sub, in_group = (sub & bit) != 0, (group & bit) != 0
            later = pltpu.roll(pltpu.roll(x, 8 - bit, 1), 16 * bit, 2)
            earlier = pltpu.roll(pltpu.roll(x, bit, 1), 128 - 16 * bit, 2)
            x = jnp.where(in_sub == in_group, x, jnp.where(in_group, later, earlier))
        sides.append(x.reshape(64, 128))
    lane = lax.broadcasted_iota(jnp.int32, (64, 128), 1)
    for nd in range(4):
        shift = 80 if nd % 2 else 16
        first, second = (sides[1], sides[0]) if nd in (0, 3) else (sides[0], sides[1])
        window[nd] = jnp.where(
            lane < shift, pltpu.roll(first, shift, 1), pltpu.roll(second, shift, 1)
        )
    first = lax.axis_index("wide") % 8 == 0
    edge = jnp.where(first, forwarded[0:3], forwarded[1:4])
    edge = jnp.concatenate([pltpu.roll(edge, 96 - 32 * q, 1) for q in range(4)], axis=0)
    free = lax.broadcasted_iota(jnp.int32, (12, 128), 1) >= 96
    for txl in range(2):
        for k in range(4):
            start = 12 + 16 * txl + 4 * k
            for nd in range(4):
                d = txl * 16 + k * 4 + nd
                out[d, 0:12] = jnp.where(free, edge, window[nd, start : start + 12, :])
                out[d, 12:16] = own[...]


def block_kernel(slots, got, out, weight):
    members = out.shape[0]
    r = lax.axis_index("wide") % 8
    n = lax.axis_index("narrow")
    lane = lax.broadcasted_iota(jnp.int32, (3, 128), 1)

    def across(slot):
        edge = jnp.zeros((3, 128), jnp.float32)
        for q in range(4):
            moved = pltpu.roll(slots[slot, 3 * q : 3 * q + 3, :], (32 * q + 32) % 128, 1)
            edge = jnp.where(lane // 32 == q, moved, edge)
        return edge

    zero = jnp.zeros((1, 128), jnp.float32)
    around = []
    for step in (3, 0, 1):
        column = (n + step) % 4
        below = slots[jnp.maximum(r - 1, 0) * 4 + column, 13:16, :]
        above = slots[jnp.minimum(r + 1, 7) * 4 + column, 12:15, :]
        below = jnp.where(r == 0, across(28 + column), below)
        above = jnp.where(r == 7, across(column), above)
        around.append(
            jnp.concatenate([zero, below, slots[r * 4 + column, 12:16, :], above, zero], axis=0)
        )
    set_weights(*around, weight)
    for start in range(0, members, 8):
        field = {r: got[pl.ds(16 * start + r, 8, stride=16), :] for r in range(12)}
        for step in range(ITERS):
            field = {
                r: weight[0, r] * field[r]
                + weight[1, r] * field[r - 1]
                + weight[2, r] * field[r + 1]
                + weight[3, r] * pltpu.roll(field[r], 1, 1)
                + weight[4, r] * pltpu.roll(field[r], 127, 1)
                for r in range(1 + step, 11 - step)
            }
        for i in range(4):
            out[start : start + 8, i, :] = pltpu.roll(field[4 + i], 112, 1)[:, :64]


def per_device(
    noise,
    diagonal_tile_blocks,
    left_factors,
    right_factors,
    ranks,
    owner,
    courant_x,
    courant_number_second,
    upwind_x,
    upwind_y,
):
    wide, narrow = lax.axis_size("wide"), lax.axis_size("narrow")
    group = wide // narrow
    devices = wide * narrow
    plane = lax.axis_index("wide") // group
    rows, cols = ranks.shape
    rank_max = left_factors.shape[2]
    members = noise.shape[1]
    cells = noise.shape[2]
    f32 = jnp.float32

    slabs = [[z * group * narrow + i for i in range(group * narrow)] for z in range(narrow)]

    def server(plane_to, source):
        return source ^ (3, 1, 0, 2)[(plane_to - source) % 4]

    swaps = [
        [
            ((s * group + r) * narrow + server(z, s), (z * group + (r ^ flip)) * narrow + s)
            for s in range(narrow)
            for r in range(group)
            for z in range(narrow)
        ]
        for flip in (0, 1)
    ]
    lines = [[z * group + 2 * y + x for y in range(group // 2)] for z in range(narrow) for x in (0, 1)]

    with jax.named_scope("diagonal_gather"):
        own_diag = diagonal_tile_blocks[0]
        beside, across = [[(i, i ^ j) for i in range(narrow)] for j in (1, 2)]
        opposite = lax.ppermute(own_diag, "narrow", across)
        diags = [
            own_diag,
            lax.ppermute(own_diag, "narrow", beside),
            opposite,
            lax.ppermute(opposite, "narrow", beside),
        ]

    with jax.named_scope("noise_gather"):
        swapped, partner = [lax.ppermute(noise, BOTH, swap) for swap in swaps]

    with jax.named_scope("coefficient_halo"):
        own = jnp.concatenate(
            [
                jnp.where(flag == 1, value, -value)
                for value, flag in ((courant_x, upwind_x), (courant_number_second, upwind_y))
            ],
            axis=1,
        )
        last = group - 1
        forwarded = lax.ppermute(
            own,
            BOTH,
            [
                ((z * group + r) * narrow + b, ((z + step) % narrow * group + r) * narrow + b)
                for z in range(narrow)
                for r, step in ((0, -1), (last, 1))
                for b in range(narrow)
            ],
        )

    with jax.named_scope("noise_gather"):
        odd = lax.axis_index("wide") % 2 == 1
        both = jnp.stack(
            [jnp.where(odd, partner, swapped), jnp.where(odd, swapped, partner)]
        )
        sending = jnp.broadcast_to(both[None], (group // 2, *both.shape))
        sending, right_factors, own_diag = lax.optimization_barrier(
            (sending, right_factors, own_diag)
        )
        early, first_diag = pl.pallas_call(
            fetch_kernel,
            out_shape=[
                pltpu.VMEM((rows, EARLY, rank_max, cells), right_factors.dtype),
                pltpu.VMEM(own_diag.shape, own_diag.dtype),
            ],
            in_specs=specs(pltpu.HBM, pltpu.HBM),
            out_specs=specs(VMEM, VMEM),
            scratch_shapes=[pltpu.SemaphoreType.DMA((rows + 1,))],
            compiler_params=limit(1),
            cost_estimate=pl.CostEstimate(
                flops=0, transcendentals=0, bytes_accessed=rows * EARLY * rank_max * cells * 4
            ),
        )(far(right_factors), far(own_diag))
        columns = lax.all_to_all(
            sending, "wide", 0, 0, axis_index_groups=lines, tiled=True
        ).reshape(cols, members, cells)

    with jax.named_scope("factors"):
        keep = (
            jnp.arange(rank_max, dtype=jnp.int32)[None, None, :] < ranks[:, :, None]
        ).astype(f32).reshape(rows, cols * rank_max)
        partial_sums = pl.pallas_call(
            factor_kernel,
            out_shape=pltpu.HBM((devices // members, members * 8, 128), f32),
            in_specs=specs(SMEM, *[VMEM] * 4, *[pltpu.HBM] * 2, *[VMEM] * (narrow - 1)),
            out_specs=pl.BlockSpec(memory_space=pltpu.HBM),
            scratch_shapes=[
                pltpu.VMEM((rows, members, cols * rank_max), jnp.bfloat16),
                pltpu.VMEM((members * 8, 128), f32),
                pltpu.VMEM((rows, members, cells), f32),
                pltpu.VMEM((rows, cols - EARLY, rank_max, cells), right_factors.dtype),
                pltpu.VMEM(left_factors.shape, left_factors.dtype),
                pltpu.VMEM((rows, *own_diag.shape), own_diag.dtype),
                pltpu.SemaphoreType.DMA((CHUNKS + 2 * rows,)),
                pltpu.SemaphoreType.DMA((devices // members,)),
            ],
            compiler_params=limit(24),
        )(
            far(owner),
            near(keep),
            near(columns),
            early,
            first_diag,
            far(right_factors),
            far(left_factors),
            *[near(d) for d in diags[1:]],
        )

    with jax.named_scope("member_exchange"):
        partial_sums = partial_sums.reshape(devices, 8, 128)
        got = lax.all_to_all(partial_sums, BOTH, 0, 0, tiled=True)

    with jax.named_scope("place"):
        bits = [(owner >> b) & 1 for b in range(7)]
        tile_y = bits[0] | bits[2] << 1 | bits[4] << 2 | bits[6] << 3
        tile_x = bits[1] | bits[3] << 1 | bits[5] << 2
        place = (tile_x * 16 + tile_y - 32 * plane.astype(jnp.int32) + 16) & 127
        blocks = pl.pallas_call(
            place_kernel,
            out_shape=pltpu.VMEM((members, 16, 128), f32),
            in_specs=specs(*[VMEM] * 4),
            out_specs=pl.BlockSpec(memory_space=VMEM),
            scratch_shapes=[pltpu.VMEM((256, 128), f32), pltpu.VMEM((4, 64, 128), f32)],
            compiler_params=limit(4),
        )(near(place[None]), near(got.reshape(wide, narrow, 8, 128)), near(own), near(forwarded))

    with jax.named_scope("block_exchange"):
        mine = lax.all_to_all(blocks, BOTH, 0, 0, axis_index_groups=slabs, tiled=True)

    with jax.named_scope("stencil"):
        return pl.pallas_call(
            block_kernel,
            out_shape=jax.ShapeDtypeStruct((members, 4, 64), f32),
            in_specs=specs(VMEM, VMEM),
            out_specs=pl.BlockSpec(memory_space=VMEM),
            scratch_shapes=[pltpu.VMEM((5, 12, 8, 128), f32)],
            compiler_params=limit(4),
        )(near(mine), near(mine.reshape(members * 16, 128)))


def solution(mesh):
    placed = (
        P("wide", None, None),
        P(("wide", "narrow"), None, None),
        P("wide", "narrow", None, None),
        P("wide", "narrow", None, None),
        P("wide", "narrow"),
        P(),
        P("wide", "narrow"),
        P("wide", "narrow"),
        P("wide", "narrow"),
        P("wide", "narrow"),
    )
    return jax.shard_map(
        per_device, mesh=mesh, in_specs=placed, out_specs=P(None, "wide", "narrow"), check_vma=False
    )
```

```python
import functools

import jax
import jax.numpy as jnp
import numpy as np
from jax import lax
from jax.experimental import pallas as pl
from jax.experimental.pallas import tpu as pltpu
from jax.sharding import PartitionSpec as P

ITERS = 4
MIXING = 0.05
BOTH = ("wide", "narrow")
VMEM = pltpu.VMEM
SMEM = pltpu.SMEM
MIB = 1 << 20
CHUNKS = 8
EARLY = 8


def specs(*spaces):
    return [pl.BlockSpec(memory_space=space) for space in spaces]


def near(value):
    return pltpu.with_memory_space_constraint(value, VMEM)


def far(value):
    return pltpu.with_memory_space_constraint(value, pltpu.HBM)


def limit(mib):
    return pltpu.CompilerParams(vmem_limit_bytes=mib * MIB)


def halves(count):
    return slice(0, count // 2), slice(count // 2, count)


def spread_kernel(mine, partner, out, done):
    odd = lax.axis_index("wide") % 2
    copies = [
        pltpu.make_async_copy(source, out.at[i, odd ^ j], done.at[i, j])
        for i in range(out.shape[0])
        for j, source in enumerate((mine, partner))
    ]
    for copy in copies:
        copy.start()
    for copy in copies:
        copy.wait()


def fetch_kernel(right_far, diag_far, right, diag, done):
    rows, count = right.shape[:2]
    copies = [
        pltpu.make_async_copy(right_far.at[p, 0:count], right.at[p], done.at[p]) for p in range(rows)
    ]
    copies.append(pltpu.make_async_copy(diag_far, diag, done.at[rows]))
    for copy in copies:
        copy.start()
    for copy in copies:
        copy.wait()


def factor_kernel(
    owner,
    keep,
    noise,
    early,
    d0,
    right_far,
    left_far,
    d1,
    d2,
    d3,
    out,
    coeff,
    turned,
    own,
    right,
    left,
    kept,
    done,
):
    rows, cols, rank_max, cells = left.shape
    members = noise.shape[1]
    each = cols // CHUNKS
    ahead = EARLY // each
    chunks = [slice(i * each, (i + 1) * each) for i in range(ahead, CHUNKS)]
    pairs = [
        (right_far.at[:, span], right.at[:, span.start - EARLY : span.stop - EARLY])
        for span in chunks
    ]
    pairs += [(left_far.at[p, span], left.at[p, span]) for p in range(rows) for span in halves(cols)]
    copies = [
        pltpu.make_async_copy(source, target, done.at[i])
        for i, (source, target) in enumerate(pairs)
    ]
    for copy in copies[:CHUNKS]:
        copy.start()

    def arrived(i):
        copies[i].wait()
        if i + CHUNKS < len(copies):
            copies[i + CHUNKS].start()

    w, n = lax.axis_index("wide"), lax.axis_index("narrow")
    lower = lax.broadcasted_iota(jnp.int32, (cells, cells), 0) >= lax.broadcasted_iota(
        jnp.int32, (cells, cells), 1
    )
    for j, diag in enumerate((d0, d1, d2, d3)):
        row = n ^ j
        local = owner[rows * w + row] - cols * n
        held = jnp.logical_and(local >= 0, local < cols)
        kept[...] = jnp.where(lower, diag[...].astype(jnp.float32), 0.0).astype(jnp.bfloat16)
        term = lax.dot_general(
            noise[jnp.clip(local, 0, cols - 1)],
            kept[...],
            (((1,), (1,)), ((), ())),
            preferred_element_type=jnp.float32,
        )
        own[row] = jnp.where(held, term, 0.0)
    for c in range(cols):
        if c >= EARLY and c % each == 0:
            arrived(c // each - ahead)
        span = slice(c * rank_max, (c + 1) * rank_max)
        block = (early[:, c] if c < EARLY else right[:, c - EARLY]).reshape(rows * rank_max, cells)
        product = lax.dot_general(
            noise[c], block, (((1,), (1,)), ((), ())), preferred_element_type=jnp.float32
        )
        for p in range(rows):
            part = product[:, p * rank_max : (p + 1) * rank_max]
            part = jnp.where(keep[p : p + 1, span] > 0, part, 0.0)
            coeff[p, :, span] = part.astype(jnp.bfloat16)
    for p in range(rows):
        total = own[p]
        for i, span in enumerate(halves(cols)):
            arrived(len(chunks) + 2 * p + i)
            total = total + jnp.dot(
                coeff[p, :, rank_max * span.start : rank_max * span.stop],
                left[p, span].reshape(cols // 2 * rank_max, cells),
                preferred_element_type=jnp.float32,
            )
        for g in range(members // 8):
            for h in range(2):
                turned[pl.ds(64 * g + 2 * p + h, 8, stride=8), :] = total[
                    8 * g : 8 * g + 8, 128 * h : 128 * h + 128
                ]
    for d in range(out.shape[0]):
        member = d % members
        out[d] = turned[8 * member : 8 * member + 8, :]


def set_weights(low, own, high, weight):
    lane = lax.broadcasted_iota(jnp.int32, low.shape, 1)
    cx, cy = [
        jnp.where(
            lane < 16,
            pltpu.roll(low, edge, 1),
            jnp.where(lane < 80, pltpu.roll(own, middle, 1), pltpu.roll(high, edge, 1)),
        )
        for edge, middle in ((80, 16), (16, 80))
    ]
    weights = (
        1.0 - jnp.abs(cx) - jnp.abs(cy) - 4.0 * MIXING,
        MIXING + jnp.maximum(cx, 0.0),
        MIXING + jnp.maximum(-cx, 0.0),
        MIXING + jnp.maximum(cy, 0.0),
        MIXING + jnp.maximum(-cy, 0.0),
    )
    for i, value in enumerate(weights):
        for row in range(1, 11):
            weight[i, row] = jnp.broadcast_to(value[row : row + 1], (8, 128))


def place_kernel(place, got, own, forwarded, out, summed, window):
    total = got[:, 0] + got[:, 1] + got[:, 2] + got[:, 3]
    summed[...] = total.reshape(256, 128)
    target = lax.broadcasted_iota(jnp.int32, (64, 128), 0)
    one_hot = jnp.where(target == place[...], 1.0, 0.0).astype(jnp.bfloat16)
    one_hot = jnp.concatenate([one_hot] * 3, axis=1)
    fields = []
    for h in range(2):
        rest = summed[pl.ds(h, 128, stride=2), :]
        parts = []
        for _ in range(3):
            part = rest.astype(jnp.bfloat16)
            parts.append(part)
            rest = rest - part.astype(jnp.float32)
        fields.append(
            jnp.dot(
                one_hot, jnp.concatenate(parts, axis=0), preferred_element_type=jnp.float32
            ).reshape(4, 16, 128)
        )
    shape = (8, 8, 128)
    sub = lax.broadcasted_iota(jnp.int32, shape, 1)
    group = lax.broadcasted_iota(jnp.int32, shape, 2) // 16
    sides = []
    for h in range(2):
        x = jnp.concatenate([f[:, 8 * h : 8 * h + 8] for f in fields], axis=1).reshape(shape)
        for bit in (1, 2, 4):
            in_sub, in_group = (sub & bit) != 0, (group & bit) != 0
            later = pltpu.roll(pltpu.roll(x, 8 - bit, 1), 16 * bit, 2)
            earlier = pltpu.roll(pltpu.roll(x, bit, 1), 128 - 16 * bit, 2)
            x = jnp.where(in_sub == in_group, x, jnp.where(in_group, later, earlier))
        sides.append(x.reshape(64, 128))
    lane = lax.broadcasted_iota(jnp.int32, (64, 128), 1)
    for nd in range(4):
        shift = 80 if nd % 2 else 16
        first, second = (sides[1], sides[0]) if nd in (0, 3) else (sides[0], sides[1])
        window[nd] = jnp.where(
            lane < shift, pltpu.roll(first, shift, 1), pltpu.roll(second, shift, 1)
        )
    first = lax.axis_index("wide") % 8 == 0
    edge = jnp.where(first, forwarded[0:3], forwarded[1:4])
    edge = jnp.concatenate([pltpu.roll(edge, 96 - 32 * q, 1) for q in range(4)], axis=0)
    free = lax.broadcasted_iota(jnp.int32, (12, 128), 1) >= 96
    for txl in range(2):
        for k in range(4):
            start = 12 + 16 * txl + 4 * k
            for nd in range(4):
                d = txl * 16 + k * 4 + nd
                out[d, 0:12] = jnp.where(free, edge, window[nd, start : start + 12, :])
                out[d, 12:16] = own[...]


def block_kernel(slots, got, out, weight):
    members = out.shape[0]
    r = lax.axis_index("wide") % 8
    n = lax.axis_index("narrow")
    lane = lax.broadcasted_iota(jnp.int32, (3, 128), 1)

    def across(slot):
        edge = jnp.zeros((3, 128), jnp.float32)
        for q in range(4):
            moved = pltpu.roll(slots[slot, 3 * q : 3 * q + 3, :], (32 * q + 32) % 128, 1)
            edge = jnp.where(lane // 32 == q, moved, edge)
        return edge

    zero = jnp.zeros((1, 128), jnp.float32)
    around = []
    for step in (3, 0, 1):
        column = (n + step) % 4
        below = slots[jnp.maximum(r - 1, 0) * 4 + column, 13:16, :]
        above = slots[jnp.minimum(r + 1, 7) * 4 + column, 12:15, :]
        below = jnp.where(r == 0, across(28 + column), below)
        above = jnp.where(r == 7, across(column), above)
        around.append(
            jnp.concatenate([zero, below, slots[r * 4 + column, 12:16, :], above, zero], axis=0)
        )
    set_weights(*around, weight)
    for start in range(0, members, 8):
        field = {r: got[pl.ds(16 * start + r, 8, stride=16), :] for r in range(12)}
        for step in range(ITERS):
            field = {
                r: weight[0, r] * field[r]
                + weight[1, r] * field[r - 1]
                + weight[2, r] * field[r + 1]
                + weight[3, r] * pltpu.roll(field[r], 1, 1)
                + weight[4, r] * pltpu.roll(field[r], 127, 1)
                for r in range(1 + step, 11 - step)
            }
        for i in range(4):
            out[start : start + 8, i, :] = pltpu.roll(field[4 + i], 112, 1)[:, :64]


def per_device(
    noise,
    diagonal_tile_blocks,
    left_factors,
    right_factors,
    ranks,
    owner,
    courant_x,
    courant_number_second,
    upwind_x,
    upwind_y,
):
    wide, narrow = lax.axis_size("wide"), lax.axis_size("narrow")
    group = wide // narrow
    devices = wide * narrow
    plane = lax.axis_index("wide") // group
    rows, cols = ranks.shape
    rank_max = left_factors.shape[2]
    members = noise.shape[1]
    cells = noise.shape[2]
    f32 = jnp.float32

    slabs = [[z * group * narrow + i for i in range(group * narrow)] for z in range(narrow)]

    def server(plane_to, source):
        return source ^ (3, 1, 0, 2)[(plane_to - source) % 4]

    swaps = [
        [
            ((s * group + r) * narrow + server(z, s), (z * group + (r ^ flip)) * narrow + s)
            for s in range(narrow)
            for r in range(group)
            for z in range(narrow)
        ]
        for flip in (0, 1)
    ]
    lines = [[z * group + 2 * y + x for y in range(group // 2)] for z in range(narrow) for x in (0, 1)]

    with jax.named_scope("diagonal_gather"):
        own_diag = diagonal_tile_blocks[0]
        beside, across = [[(i, i ^ j) for i in range(narrow)] for j in (1, 2)]
        opposite = lax.ppermute(own_diag, "narrow", across)
        diags = [
            own_diag,
            lax.ppermute(own_diag, "narrow", beside),
            opposite,
            lax.ppermute(opposite, "narrow", beside),
        ]

    with jax.named_scope("noise_gather"):
        swapped, partner = [lax.ppermute(noise, BOTH, swap) for swap in swaps]

    with jax.named_scope("coefficient_halo"):
        own = jnp.concatenate(
            [
                jnp.where(flag == 1, value, -value)
                for value, flag in ((courant_x, upwind_x), (courant_number_second, upwind_y))
            ],
            axis=1,
        )
        last = group - 1
        forwarded = lax.ppermute(
            own,
            BOTH,
            [
                ((z * group + r) * narrow + b, ((z + step) % narrow * group + r) * narrow + b)
                for z in range(narrow)
                for r, step in ((0, -1), (last, 1))
                for b in range(narrow)
            ],
        )

    with jax.named_scope("noise_gather"):
        sending = pl.pallas_call(
            spread_kernel,
            out_shape=pltpu.HBM((group // 2, 2, *noise.shape), noise.dtype),
            in_specs=specs(VMEM, VMEM),
            out_specs=pl.BlockSpec(memory_space=pltpu.HBM),
            scratch_shapes=[pltpu.SemaphoreType.DMA((group // 2, 2))],
            compiler_params=limit(1),
        )(near(swapped), near(partner))
        sending, right_factors, own_diag = lax.optimization_barrier(
            (sending, right_factors, own_diag)
        )
        early, first_diag = pl.pallas_call(
            fetch_kernel,
            out_shape=[
                pltpu.VMEM((rows, EARLY, rank_max, cells), right_factors.dtype),
                pltpu.VMEM(own_diag.shape, own_diag.dtype),
            ],
            in_specs=specs(pltpu.HBM, pltpu.HBM),
            out_specs=specs(VMEM, VMEM),
            scratch_shapes=[pltpu.SemaphoreType.DMA((rows + 1,))],
            compiler_params=limit(1),
            cost_estimate=pl.CostEstimate(
                flops=0, transcendentals=0, bytes_accessed=rows * EARLY * rank_max * cells * 4
            ),
        )(far(right_factors), far(own_diag))
        columns = lax.all_to_all(
            sending, "wide", 0, 0, axis_index_groups=lines, tiled=True
        ).reshape(cols, members, cells)

    with jax.named_scope("factors"):
        keep = (
            jnp.arange(rank_max, dtype=jnp.int32)[None, None, :] < ranks[:, :, None]
        ).astype(f32).reshape(rows, cols * rank_max)
        partial_sums = pl.pallas_call(
            factor_kernel,
            out_shape=pltpu.VMEM((devices, 8, 128), f32),
            in_specs=specs(SMEM, *[VMEM] * 4, *[pltpu.HBM] * 2, *[VMEM] * (narrow - 1)),
            out_specs=pl.BlockSpec(memory_space=VMEM),
            scratch_shapes=[
                pltpu.VMEM((rows, members, cols * rank_max), jnp.bfloat16),
                pltpu.VMEM((members * 8, 128), f32),
                pltpu.VMEM((rows, members, cells), f32),
                pltpu.VMEM((rows, cols - EARLY, rank_max, cells), right_factors.dtype),
                pltpu.VMEM(left_factors.shape, left_factors.dtype),
                pltpu.VMEM(own_diag.shape, own_diag.dtype),
                pltpu.SemaphoreType.DMA((CHUNKS + 2 * rows,)),
            ],
            compiler_params=limit(24),
        )(
            far(owner),
            near(keep),
            near(columns),
            early,
            first_diag,
            far(right_factors),
            far(left_factors),
            *[near(d) for d in diags[1:]],
        )

    with jax.named_scope("member_exchange"):
        got = lax.all_to_all(partial_sums, BOTH, 0, 0, tiled=True)

    with jax.named_scope("place"):
        bits = [(owner >> b) & 1 for b in range(7)]
        tile_y = bits[0] | bits[2] << 1 | bits[4] << 2 | bits[6] << 3
        tile_x = bits[1] | bits[3] << 1 | bits[5] << 2
        place = (tile_x * 16 + tile_y - 32 * plane.astype(jnp.int32) + 16) & 127
        blocks = pl.pallas_call(
            place_kernel,
            out_shape=pltpu.VMEM((members, 16, 128), f32),
            in_specs=specs(*[VMEM] * 4),
            out_specs=pl.BlockSpec(memory_space=VMEM),
            scratch_shapes=[pltpu.VMEM((256, 128), f32), pltpu.VMEM((4, 64, 128), f32)],
            compiler_params=limit(4),
        )(near(place[None]), near(got.reshape(wide, narrow, 8, 128)), near(own), near(forwarded))

    with jax.named_scope("block_exchange"):
        mine = lax.all_to_all(blocks, BOTH, 0, 0, axis_index_groups=slabs, tiled=True)

    with jax.named_scope("stencil"):
        return pl.pallas_call(
            block_kernel,
            out_shape=jax.ShapeDtypeStruct((members, 4, 64), f32),
            in_specs=specs(VMEM, VMEM),
            out_specs=pl.BlockSpec(memory_space=VMEM),
            scratch_shapes=[pltpu.VMEM((5, 12, 8, 128), f32)],
            compiler_params=limit(4),
        )(near(mine), near(mine.reshape(members * 16, 128)))


def solution(mesh):
    placed = (
        P("wide", None, None),
        P(("wide", "narrow"), None, None),
        P("wide", "narrow", None, None),
        P("wide", "narrow", None, None),
        P("wide", "narrow"),
        P(),
        P("wide", "narrow"),
        P("wide", "narrow"),
        P("wide", "narrow"),
        P("wide", "narrow"),
    )
    return jax.shard_map(
        per_device, mesh=mesh, in_specs=placed, out_specs=P(None, "wide", "narrow"), check_vma=False
    )
```

```python
import functools

import jax
import jax.numpy as jnp
import numpy as np
from jax import lax
from jax.experimental import pallas as pl
from jax.experimental.pallas import tpu as pltpu
from jax.sharding import PartitionSpec as P

ITERS = 4
MIXING = 0.05
BOTH = ("wide", "narrow")
VMEM = pltpu.VMEM
SMEM = pltpu.SMEM
MIB = 1 << 20
CHUNKS = 8
EARLY = 8


def specs(*spaces):
    return [pl.BlockSpec(memory_space=space) for space in spaces]


def near(value):
    return pltpu.with_memory_space_constraint(value, VMEM)


def far(value):
    return pltpu.with_memory_space_constraint(value, pltpu.HBM)


def limit(mib):
    return pltpu.CompilerParams(vmem_limit_bytes=mib * MIB)


def halves(count):
    return slice(0, count // 2), slice(count // 2, count)


def fetch_kernel(right_far, diag_far, right, diag, done):
    rows, count = right.shape[:2]
    copies = [
        pltpu.make_async_copy(right_far.at[p, 0:count], right.at[p], done.at[p]) for p in range(rows)
    ]
    copies.append(pltpu.make_async_copy(diag_far, diag, done.at[rows]))
    for copy in copies:
        copy.start()
    for copy in copies:
        copy.wait()


def factor_kernel(
    owner,
    keep,
    noise,
    early,
    d0,
    right_far,
    left_far,
    d1,
    d2,
    d3,
    out,
    coeff,
    turned,
    own,
    right,
    left,
    kept,
    done,
):
    rows, cols, rank_max, cells = left.shape
    members = noise.shape[1]
    each = cols // CHUNKS
    ahead = EARLY // each
    chunks = [slice(i * each, (i + 1) * each) for i in range(ahead, CHUNKS)]
    pairs = [
        (right_far.at[:, span], right.at[:, span.start - EARLY : span.stop - EARLY])
        for span in chunks
    ]
    pairs += [(left_far.at[p, span], left.at[p, span]) for p in range(rows) for span in halves(cols)]
    copies = [
        pltpu.make_async_copy(source, target, done.at[i])
        for i, (source, target) in enumerate(pairs)
    ]
    for copy in copies[:CHUNKS]:
        copy.start()

    def arrived(i):
        copies[i].wait()
        if i + CHUNKS < len(copies):
            copies[i + CHUNKS].start()

    w, n = lax.axis_index("wide"), lax.axis_index("narrow")
    lower = lax.broadcasted_iota(jnp.int32, (cells, cells), 0) >= lax.broadcasted_iota(
        jnp.int32, (cells, cells), 1
    )
    for j, diag in enumerate((d0, d1, d2, d3)):
        row = n ^ j
        local = owner[rows * w + row] - cols * n
        held = jnp.logical_and(local >= 0, local < cols)
        kept[...] = jnp.where(lower, diag[...].astype(jnp.float32), 0.0).astype(jnp.bfloat16)
        term = lax.dot_general(
            noise[jnp.clip(local, 0, cols - 1)],
            kept[...],
            (((1,), (1,)), ((), ())),
            preferred_element_type=jnp.float32,
        )
        own[row] = jnp.where(held, term, 0.0)
    for c in range(cols):
        if c >= EARLY and c % each == 0:
            arrived(c // each - ahead)
        span = slice(c * rank_max, (c + 1) * rank_max)
        block = (early[:, c] if c < EARLY else right[:, c - EARLY]).reshape(rows * rank_max, cells)
        product = lax.dot_general(
            noise[c], block, (((1,), (1,)), ((), ())), preferred_element_type=jnp.float32
        )
        for p in range(rows):
            part = product[:, p * rank_max : (p + 1) * rank_max]
            part = jnp.where(keep[p : p + 1, span] > 0, part, 0.0)
            coeff[p, :, span] = part.astype(jnp.bfloat16)
    for p in range(rows):
        total = own[p]
        for i, span in enumerate(halves(cols)):
            arrived(len(chunks) + 2 * p + i)
            total = total + jnp.dot(
                coeff[p, :, rank_max * span.start : rank_max * span.stop],
                left[p, span].reshape(cols // 2 * rank_max, cells),
                preferred_element_type=jnp.float32,
            )
        for g in range(members // 8):
            for h in range(2):
                turned[pl.ds(64 * g + 2 * p + h, 8, stride=8), :] = total[
                    8 * g : 8 * g + 8, 128 * h : 128 * h + 128
                ]
    for d in range(out.shape[0]):
        member = d % members
        out[d] = turned[8 * member : 8 * member + 8, :]


def set_weights(low, own, high, weight):
    lane = lax.broadcasted_iota(jnp.int32, low.shape, 1)
    cx, cy = [
        jnp.where(
            lane < 16,
            pltpu.roll(low, edge, 1),
            jnp.where(lane < 80, pltpu.roll(own, middle, 1), pltpu.roll(high, edge, 1)),
        )
        for edge, middle in ((80, 16), (16, 80))
    ]
    weights = (
        1.0 - jnp.abs(cx) - jnp.abs(cy) - 4.0 * MIXING,
        MIXING + jnp.maximum(cx, 0.0),
        MIXING + jnp.maximum(-cx, 0.0),
        MIXING + jnp.maximum(cy, 0.0),
        MIXING + jnp.maximum(-cy, 0.0),
    )
    for i, value in enumerate(weights):
        for row in range(1, 11):
            weight[i, row] = jnp.broadcast_to(value[row : row + 1], (8, 128))


def place_kernel(place, got, own, forwarded, out, summed, window):
    total = got[:, 0] + got[:, 1] + got[:, 2] + got[:, 3]
    summed[...] = total.reshape(256, 128)
    target = lax.broadcasted_iota(jnp.int32, (64, 128), 0)
    one_hot = jnp.where(target == place[...], 1.0, 0.0).astype(jnp.bfloat16)
    one_hot = jnp.concatenate([one_hot] * 3, axis=1)
    fields = []
    for h in range(2):
        rest = summed[pl.ds(h, 128, stride=2), :]
        parts = []
        for _ in range(3):
            part = rest.astype(jnp.bfloat16)
            parts.append(part)
            rest = rest - part.astype(jnp.float32)
        fields.append(
            jnp.dot(
                one_hot, jnp.concatenate(parts, axis=0), preferred_element_type=jnp.float32
            ).reshape(4, 16, 128)
        )
    shape = (8, 8, 128)
    sub = lax.broadcasted_iota(jnp.int32, shape, 1)
    group = lax.broadcasted_iota(jnp.int32, shape, 2) // 16
    sides = []
    for h in range(2):
        x = jnp.concatenate([f[:, 8 * h : 8 * h + 8] for f in fields], axis=1).reshape(shape)
        for bit in (1, 2, 4):
            in_sub, in_group = (sub & bit) != 0, (group & bit) != 0
            later = pltpu.roll(pltpu.roll(x, 8 - bit, 1), 16 * bit, 2)
            earlier = pltpu.roll(pltpu.roll(x, bit, 1), 128 - 16 * bit, 2)
            x = jnp.where(in_sub == in_group, x, jnp.where(in_group, later, earlier))
        sides.append(x.reshape(64, 128))
    lane = lax.broadcasted_iota(jnp.int32, (64, 128), 1)
    for nd in range(4):
        shift = 80 if nd % 2 else 16
        first, second = (sides[1], sides[0]) if nd in (0, 3) else (sides[0], sides[1])
        window[nd] = jnp.where(
            lane < shift, pltpu.roll(first, shift, 1), pltpu.roll(second, shift, 1)
        )
    first = lax.axis_index("wide") % 8 == 0
    edge = jnp.where(first, forwarded[0:3], forwarded[1:4])
    edge = jnp.concatenate([pltpu.roll(edge, 96 - 32 * q, 1) for q in range(4)], axis=0)
    free = lax.broadcasted_iota(jnp.int32, (12, 128), 1) >= 96
    for txl in range(2):
        for k in range(4):
            start = 12 + 16 * txl + 4 * k
            for nd in range(4):
                d = txl * 16 + k * 4 + nd
                out[d, 0:12] = jnp.where(free, edge, window[nd, start : start + 12, :])
                out[d, 12:16] = own[...]


def block_kernel(slots, got, out, weight):
    members = out.shape[0]
    r = lax.axis_index("wide") % 8
    n = lax.axis_index("narrow")
    lane = lax.broadcasted_iota(jnp.int32, (3, 128), 1)

    def across(slot):
        edge = jnp.zeros((3, 128), jnp.float32)
        for q in range(4):
            moved = pltpu.roll(slots[slot, 3 * q : 3 * q + 3, :], (32 * q + 32) % 128, 1)
            edge = jnp.where(lane // 32 == q, moved, edge)
        return edge

    zero = jnp.zeros((1, 128), jnp.float32)
    around = []
    for step in (3, 0, 1):
        column = (n + step) % 4
        below = slots[jnp.maximum(r - 1, 0) * 4 + column, 13:16, :]
        above = slots[jnp.minimum(r + 1, 7) * 4 + column, 12:15, :]
        below = jnp.where(r == 0, across(28 + column), below)
        above = jnp.where(r == 7, across(column), above)
        around.append(
            jnp.concatenate([zero, below, slots[r * 4 + column, 12:16, :], above, zero], axis=0)
        )
    set_weights(*around, weight)
    for start in range(0, members, 8):
        field = {r: got[pl.ds(16 * start + r, 8, stride=16), :] for r in range(12)}
        for step in range(ITERS):
            field = {
                r: weight[0, r] * field[r]
                + weight[1, r] * field[r - 1]
                + weight[2, r] * field[r + 1]
                + weight[3, r] * pltpu.roll(field[r], 1, 1)
                + weight[4, r] * pltpu.roll(field[r], 127, 1)
                for r in range(1 + step, 11 - step)
            }
        for i in range(4):
            out[start : start + 8, i, :] = pltpu.roll(field[4 + i], 112, 1)[:, :64]


def per_device(
    noise,
    diagonal_tile_blocks,
    left_factors,
    right_factors,
    ranks,
    owner,
    courant_x,
    courant_number_second,
    upwind_x,
    upwind_y,
):
    wide, narrow = lax.axis_size("wide"), lax.axis_size("narrow")
    group = wide // narrow
    devices = wide * narrow
    plane = lax.axis_index("wide") // group
    rows, cols = ranks.shape
    rank_max = left_factors.shape[2]
    members = noise.shape[1]
    cells = noise.shape[2]
    f32 = jnp.float32

    slabs = [[z * group * narrow + i for i in range(group * narrow)] for z in range(narrow)]

    def server(plane_to, source):
        return source ^ (3, 1, 0, 2)[(plane_to - source) % 4]

    swaps = [
        [
            ((s * group + r) * narrow + server(z, s), (z * group + (r ^ flip)) * narrow + s)
            for s in range(narrow)
            for r in range(group)
            for z in range(narrow)
        ]
        for flip in (0, 1)
    ]
    lines = [[z * group + 2 * y + x for y in range(group // 2)] for z in range(narrow) for x in (0, 1)]

    with jax.named_scope("diagonal_gather"):
        own_diag = diagonal_tile_blocks[0]
        beside, across = [[(i, i ^ j) for i in range(narrow)] for j in (1, 2)]
        opposite = lax.ppermute(own_diag, "narrow", across)
        diags = [
            own_diag,
            lax.ppermute(own_diag, "narrow", beside),
            opposite,
            lax.ppermute(opposite, "narrow", beside),
        ]

    with jax.named_scope("noise_gather"):
        swapped, partner = [lax.ppermute(noise, BOTH, swap) for swap in swaps]

    with jax.named_scope("coefficient_halo"):
        own = jnp.concatenate(
            [
                jnp.where(flag == 1, value, -value)
                for value, flag in ((courant_x, upwind_x), (courant_number_second, upwind_y))
            ],
            axis=1,
        )
        swapped, partner, own = lax.optimization_barrier((swapped, partner, own))
        last = group - 1
        forwarded = lax.ppermute(
            own,
            BOTH,
            [
                ((z * group + r) * narrow + b, ((z + step) % narrow * group + r) * narrow + b)
                for z in range(narrow)
                for r, step in ((0, -1), (last, 1))
                for b in range(narrow)
            ],
        )

    with jax.named_scope("noise_gather"):
        odd = lax.axis_index("wide") % 2 == 1
        both = jnp.stack(
            [jnp.where(odd, partner, swapped), jnp.where(odd, swapped, partner)]
        )
        sending = jnp.broadcast_to(both[None], (group // 2, *both.shape))
        sending, right_factors, own_diag = lax.optimization_barrier(
            (sending, right_factors, own_diag)
        )
        early, first_diag = pl.pallas_call(
            fetch_kernel,
            out_shape=[
                pltpu.VMEM((rows, EARLY, rank_max, cells), right_factors.dtype),
                pltpu.VMEM(own_diag.shape, own_diag.dtype),
            ],
            in_specs=specs(pltpu.HBM, pltpu.HBM),
            out_specs=specs(VMEM, VMEM),
            scratch_shapes=[pltpu.SemaphoreType.DMA((rows + 1,))],
            compiler_params=limit(1),
            cost_estimate=pl.CostEstimate(
                flops=0, transcendentals=0, bytes_accessed=rows * EARLY * rank_max * cells * 4
            ),
        )(far(right_factors), far(own_diag))
        columns = lax.all_to_all(
            sending, "wide", 0, 0, axis_index_groups=lines, tiled=True
        ).reshape(cols, members, cells)
        columns, forwarded = lax.optimization_barrier((columns, forwarded))

    with jax.named_scope("factors"):
        keep = (
            jnp.arange(rank_max, dtype=jnp.int32)[None, None, :] < ranks[:, :, None]
        ).astype(f32).reshape(rows, cols * rank_max)
        partial_sums = pl.pallas_call(
            factor_kernel,
            out_shape=pltpu.VMEM((devices, 8, 128), f32),
            in_specs=specs(SMEM, *[VMEM] * 4, *[pltpu.HBM] * 2, *[VMEM] * (narrow - 1)),
            out_specs=pl.BlockSpec(memory_space=VMEM),
            scratch_shapes=[
                pltpu.VMEM((rows, members, cols * rank_max), jnp.bfloat16),
                pltpu.VMEM((members * 8, 128), f32),
                pltpu.VMEM((rows, members, cells), f32),
                pltpu.VMEM((rows, cols - EARLY, rank_max, cells), right_factors.dtype),
                pltpu.VMEM(left_factors.shape, left_factors.dtype),
                pltpu.VMEM(own_diag.shape, own_diag.dtype),
                pltpu.SemaphoreType.DMA((CHUNKS + 2 * rows,)),
            ],
            compiler_params=limit(24),
        )(
            far(owner),
            near(keep),
            near(columns),
            early,
            first_diag,
            far(right_factors),
            far(left_factors),
            *[near(d) for d in diags[1:]],
        )

    with jax.named_scope("member_exchange"):
        got = lax.all_to_all(partial_sums, BOTH, 0, 0, tiled=True)

    with jax.named_scope("place"):
        bits = [(owner >> b) & 1 for b in range(7)]
        tile_y = bits[0] | bits[2] << 1 | bits[4] << 2 | bits[6] << 3
        tile_x = bits[1] | bits[3] << 1 | bits[5] << 2
        place = (tile_x * 16 + tile_y - 32 * plane.astype(jnp.int32) + 16) & 127
        blocks = pl.pallas_call(
            place_kernel,
            out_shape=pltpu.VMEM((members, 16, 128), f32),
            in_specs=specs(*[VMEM] * 4),
            out_specs=pl.BlockSpec(memory_space=VMEM),
            scratch_shapes=[pltpu.VMEM((256, 128), f32), pltpu.VMEM((4, 64, 128), f32)],
            compiler_params=limit(4),
        )(near(place[None]), near(got.reshape(wide, narrow, 8, 128)), near(own), near(forwarded))

    with jax.named_scope("block_exchange"):
        mine = lax.all_to_all(blocks, BOTH, 0, 0, axis_index_groups=slabs, tiled=True)

    with jax.named_scope("stencil"):
        return pl.pallas_call(
            block_kernel,
            out_shape=jax.ShapeDtypeStruct((members, 4, 64), f32),
            in_specs=specs(VMEM, VMEM),
            out_specs=pl.BlockSpec(memory_space=VMEM),
            scratch_shapes=[pltpu.VMEM((5, 12, 8, 128), f32)],
            compiler_params=limit(4),
        )(near(mine), near(mine.reshape(members * 16, 128)))


def solution(mesh):
    placed = (
        P("wide", None, None),
        P(("wide", "narrow"), None, None),
        P("wide", "narrow", None, None),
        P("wide", "narrow", None, None),
        P("wide", "narrow"),
        P(),
        P("wide", "narrow"),
        P("wide", "narrow"),
        P("wide", "narrow"),
        P("wide", "narrow"),
    )
    return jax.shard_map(
        per_device, mesh=mesh, in_specs=placed, out_specs=P(None, "wide", "narrow"), check_vma=False
    )
```
